32 devices in a mesh: dp: 16 (over z, y, x), heads: 2 (over core).
Axes of the slice: x: 2, y: 2, z: 4, core: 2. Of those that a mesh axis runs over, the one named last changes fastest.
Arguments:
- tokens: bfloat16 [12288, 768], P('dp'), may hold values from -6 to 6
- memory: bfloat16 [12288, 768], P('dp'), may hold values from -6 to 6
- cotangent: bfloat16 [12288, 768], P(('dp', 'heads')), may hold values from -6 to 6
- seq_modes: int32 [32], replicated, may hold values from 0 to 2, as said below
- dec_lengths: int32 [32], replicated, may hold values from 192 to 384, as said below
- enc_lengths: int32 [32], replicated, may hold values from 96 to 384
- slot_plan: int32 [32], replicated, may hold values from 0 to 31, as said below
- buckets: int32 [384], replicated, may hold values from 0 to 31, as said below
- mode_table: bfloat16 [3, 768], P(None, 'dp'), may hold values from -6 to 6
- gain_self: bfloat16 [768], P('dp'), may hold values from 0.5 to 1.5
- gain_cross: bfloat16 [768], P('dp'), may hold values from 0.5 to 1.5
- gain_ffn: bfloat16 [768], P('dp'), may hold values from 0.5 to 1.5
- bucket_table: bfloat16 [32, 12], P(None, 'heads'), may hold values from -6 to 6
- self_query: bfloat16 [768, 768], P('dp', 'heads'), may hold values from -0.109375 to 0.109375
- self_key: bfloat16 [768, 768], P('dp', 'heads'), may hold values from -0.109375 to 0.109375
- self_value: bfloat16 [768, 768], P('dp', 'heads'), may hold values from -0.21875 to 0.21875
- self_output: bfloat16 [768, 768], P('heads', 'dp'), may hold values from -1.75 to 1.75
- cross_query: bfloat16 [768, 768], P('dp', 'heads'), may hold values from -0.109375 to 0.109375
- cross_key: bfloat16 [768, 768], P('dp', 'heads'), may hold values from -0.109375 to 0.109375
- cross_value: bfloat16 [768, 768], P('dp', 'heads'), may hold values from -0.21875 to 0.21875
- cross_output: bfloat16 [768, 768], P('heads', 'dp'), may hold values from -1.75 to 1.75
- ffn_gate: bfloat16 [768, 2048], P('dp', 'heads'), may hold values from -0.21875 to 0.21875
- ffn_up: bfloat16 [768, 2048], P('dp', 'heads'), may hold values from -0.21875 to 0.21875
- ffn_down: bfloat16 [2048, 768], P('heads', 'dp'), may hold values from -0.125 to 0.125
Outputs:
- layer_output: bfloat16 [12288, 768], P(('dp', 'heads'))
- tokens_grad: float32 [12288, 768], P('dp')
- memory_grad: float32 [12288, 768], P('dp')
- mode_table_grad: float32 [3, 768], P(None, 'dp')
- gain_self_grad: float32 [768], P('dp')
- gain_cross_grad: float32 [768], P('dp')
- gain_ffn_grad: float32 [768], P('dp')
- bucket_table_grad: float32 [32, 12], P(None, 'heads')
- self_query_grad: float32 [768, 768], P('dp', 'heads')
- self_key_grad: float32 [768, 768], P('dp', 'heads')
- self_value_grad: float32 [768, 768], P('dp', 'heads')
- self_output_grad: float32 [768, 768], P('heads', 'dp')
- cross_query_grad: float32 [768, 768], P('dp', 'heads')
- cross_key_grad: float32 [768, 768], P('dp', 'heads')
- cross_value_grad: float32 [768, 768], P('dp', 'heads')
- cross_output_grad: float32 [768, 768], P('heads', 'dp')
- ffn_gate_grad: float32 [768, 2048], P('dp', 'heads')
- ffn_up_grad: float32 [768, 2048], P('dp', 'heads')
- ffn_down_grad: float32 [2048, 768], P('heads', 'dp')
The draws below stay inside these ranges and needn't reach their ends.
Inputs may be any that keep to these rules, and one draw needn't show every extreme that they name: `seq_modes`: all 2 sequences assigned to slots of one index of dp have the same mode. A permutation of the slots; sequence s is processed by index slot_plan[s] // 2 of dp. `dec_lengths`: the lengths of the 2 sequences assigned to one index of dp sum to 576. `buckets`: never falls as the distance grows; distance 0 is bucket 0.
All inputs are finite; a program needn't handle non-finite values.
Results may differ from the reference program's by a relative error of at most 0.024.
Values may be sent and summed in bfloat16 or wider, within the bound.
No kernel may reach another device: no remote copies, remote signals or barrier semaphores. Data moves between devices by JAX's collectives and lax.ppermute only.
A program may use at most 192 MiB of HBM per device.

```python
import jax
import jax.numpy as jnp
from jax import lax

D = 768
H = 12
DH = 64
FF = 2048
BUCKETS = 32
MODES = 3
SLOT = 384
SEQ_DEV = 2
NSEQ = 32
TOKENS = 12288


def plan_parts(key):
    group_total = NSEQ // SEQ_DEV
    group_modes = jax.random.randint(jax.random.fold_in(key, 101), (group_total,), 0, MODES)
    group_modes = group_modes.at[0].set(MODES - 1).at[group_total - 1].set(0)
    slot_plan = jax.random.permutation(jax.random.fold_in(key, 102), NSEQ).astype(jnp.int32)
    firsts = jax.random.randint(jax.random.fold_in(key, 103), (NSEQ // 2,), SLOT // 2, SLOT + 1)
    firsts = firsts.at[0].set(SLOT)
    slot_lengths = jnp.stack([firsts, 3 * SLOT // 2 - firsts], axis=1).reshape(NSEQ)
    slot_modes = jnp.repeat(group_modes, SEQ_DEV)
    return (slot_plan, jnp.take(slot_modes, slot_plan), jnp.take(slot_lengths, slot_plan))


def draw_slot_plan(key, part):
    return plan_parts(key)[0]


def draw_seq_modes(key, part):
    return plan_parts(key)[1].astype(jnp.int32)


def draw_dec_lengths(key, part):
    return plan_parts(key)[2].astype(jnp.int32)


def draw_enc_lengths(key, part):
    drawn = jax.random.randint(jax.random.fold_in(key, 104), (NSEQ,), SLOT // 4, SLOT + 1)
    return drawn.at[0].set(SLOT).astype(jnp.int32)


def draw_buckets(key, part):
    points = jax.random.permutation(jax.random.fold_in(key, 105), SLOT - 1)[:BUCKETS - 1] + 1
    distance = jnp.arange(SLOT)
    return jnp.sum((points[None, :] <= distance[:, None]).astype(jnp.int32), axis=1).astype(jnp.int32)


def raised(values, key, source, target, parts, factor):
    owner, partner = [(jnp.arange(values.shape[axis_at]) // (values.shape[axis_at] // parts)).reshape([-1 if axis == axis_at else 1 for axis in range(values.ndim)]) for axis_at in (source, target)]
    chosen = jax.random.permutation(key, parts)[partner]
    strong = (owner == chosen) | (owner == (partner + parts // 2) % parts)
    return jnp.where(strong, factor * values, values)


def block_levels(stream_key, shape, split, low, top_value):
    gain = 1.0
    for axis_at, blocks in split:
        draws = jax.random.uniform(jax.random.fold_in(jax.random.fold_in(stream_key, 6), axis_at), (blocks,), jnp.float32, low / len(split), top_value / len(split))
        gain = gain * jnp.repeat(jnp.exp(draws), shape[axis_at] // blocks).reshape((-1,) + (1,) * (len(shape) - 1 - axis_at))
    return gain


def centred(stream_key, extent, spread, reach, cuts=(), held_as=jnp.bfloat16):
    factor_of = block_levels(stream_key, extent, cuts, -0.22, 0.18) if cuts else 1.0
    values = jax.random.normal(stream_key, extent, jnp.float32) * spread * factor_of
    return jnp.minimum(jnp.maximum(values, -reach), reach).astype(held_as)


def heavy_noise(own_key, shape, deviation, most, pieces, heavy, kind=jnp.bfloat16):
    values = deviation * jax.random.normal(own_key, shape, jnp.float32)
    if pieces:
        values = values * block_levels(own_key, shape, pieces, -0.22, 0.18)
    return jnp.clip(raised(values, jax.random.fold_in(own_key, 3), *heavy), -most, most).astype(kind)


def setup_inputs(seed: int = 0) -> dict:
    arg_keys = jax.random.split(jax.random.key(seed), 25)
    tokens = centred(arg_keys[0], (TOKENS, D), 1.0, 6.0, ((0, 16),))
    memory = centred(arg_keys[1], (TOKENS, D), 1.0, 6.0, ((0, 16),))
    cotangent = heavy_noise(arg_keys[2], (TOKENS, D), 1.0, 6.0, ((0, 32),), (0, 1, 32, 2.75))
    seq_modes = draw_seq_modes(jax.random.fold_in(arg_keys[24], 71), 0)
    dec_lengths = draw_dec_lengths(jax.random.fold_in(arg_keys[24], 71), 0)
    enc_lengths = draw_enc_lengths(jax.random.fold_in(arg_keys[24], 71), 0)
    slot_plan = draw_slot_plan(jax.random.fold_in(arg_keys[24], 71), 0)
    buckets = draw_buckets(jax.random.fold_in(arg_keys[24], 71), 0)
    mode_table = centred(arg_keys[8], (MODES, D), 1.0, 6.0, ((1, 16),))
    gain_self = jnp.clip(1.0 + 0.1 * jax.random.normal(arg_keys[9], (D,), jnp.float32), 0.5, 1.5).astype(jnp.bfloat16)
    gain_cross = jnp.clip(1.0 + 0.1 * jax.random.normal(arg_keys[10], (D,), jnp.float32), 0.5, 1.5).astype(jnp.bfloat16)
    gain_ffn = jnp.clip(1.0 + 0.1 * jax.random.normal(arg_keys[11], (D,), jnp.float32), 0.5, 1.5).astype(jnp.bfloat16)
    bucket_table = centred(arg_keys[12], (BUCKETS, H), 1.0, 6.0, ((1, 2),))
    self_query = centred(arg_keys[13], (D, H * DH), (4 * D) ** -0.5, 0.109375, ((0, 16), (1, 2)))
    self_key = centred(arg_keys[14], (D, H * DH), (4 * D) ** -0.5, 0.109375, ((0, 16), (1, 2)))
    self_value = centred(arg_keys[15], (D, H * DH), D ** -0.5, 0.21875, ((0, 16), (1, 2)))
    self_output = centred(arg_keys[16], (H * DH, D), (H * DH // 64) ** -0.5, 1.75, ((0, 2), (1, 16)))
    cross_query = centred(arg_keys[17], (D, H * DH), (4 * D) ** -0.5, 0.109375, ((0, 16), (1, 2)))
    cross_key = centred(arg_keys[18], (D, H * DH), (4 * D) ** -0.5, 0.109375, ((0, 16), (1, 2)))
    cross_value = centred(arg_keys[19], (D, H * DH), D ** -0.5, 0.21875, ((0, 16), (1, 2)))
    cross_output = centred(arg_keys[20], (H * DH, D), (H * DH // 64) ** -0.5, 1.75, ((0, 2), (1, 16)))
    ffn_gate = centred(arg_keys[21], (D, FF), D ** -0.5, 0.21875, ((0, 16), (1, 2)))
    ffn_up = centred(arg_keys[22], (D, FF), D ** -0.5, 0.21875, ((0, 16), (1, 2)))
    ffn_down = centred(arg_keys[23], (FF, D), FF ** -0.5, 0.125, ((0, 2), (1, 16)))
    return {"tokens": tokens, "memory": memory, "cotangent": cotangent, "seq_modes": seq_modes, "dec_lengths": dec_lengths, "enc_lengths": enc_lengths, "slot_plan": slot_plan, "buckets": buckets, "mode_table": mode_table, "gain_self": gain_self, "gain_cross": gain_cross, "gain_ffn": gain_ffn, "bucket_table": bucket_table, "self_query": self_query, "self_key": self_key, "self_value": self_value, "self_output": self_output, "cross_query": cross_query, "cross_key": cross_key, "cross_value": cross_value, "cross_output": cross_output, "ffn_gate": ffn_gate, "ffn_up": ffn_up, "ffn_down": ffn_down}


norm_epsilon = 1e-06
masked_score = -1000000000.0
highest = lax.Precision.HIGHEST

@jax.custom_vjp
def low(v):
    return lax.optimization_barrier(v.astype(jnp.bfloat16)).astype(jnp.float32)

@jax.custom_vjp
def low_back(v):
    return v

def low_keep(v):
    return (low(v), None)

def low_pass(kept, grad):
    return (grad,)

def back_keep(v):
    return (v, None)

def back_low(kept, grad):
    return (low(grad),)
low.defvjp(low_keep, low_pass)
low_back.defvjp(back_keep, back_low)

def rms_norm(hidden, gain_row):
    return hidden * lax.rsqrt(lax.optimization_barrier(jnp.mean(hidden * hidden, axis=-1, keepdims=True)) + norm_epsilon) * gain_row

def gelu_tanh(values):
    return 0.5 * values * (1.0 + jnp.tanh(0.7978845608028654 * (values + 0.044715 * values * values * values)))

def matmul(left_side, right_side):
    return jnp.dot(left_side, right_side, precision=highest, preferred_element_type=jnp.float32)

def attend(queries, key_rows, value_rows, bias, allowed):
    seq_len = queries.shape[0]
    query_heads = queries.reshape(seq_len, H, DH)
    key_heads = key_rows.reshape(seq_len, H, DH)
    value_heads = value_rows.reshape(seq_len, H, DH)
    scores = jnp.einsum('qhd,khd->hqk', query_heads, key_heads, precision=highest)
    if bias is not None:
        scores = scores + bias
    scores = low_back(scores)
    scores = jnp.where(allowed[None], scores, masked_score)
    largest = lax.optimization_barrier(jnp.max(scores, axis=-1, keepdims=True))
    exponent = jnp.exp(scores - largest)
    weights_soft = exponent / lax.optimization_barrier(jnp.sum(exponent, axis=-1, keepdims=True))
    blended = jnp.einsum('hqk,khd->qhd', low(weights_soft), value_heads, precision=highest)
    return blended.reshape(seq_len, H * DH)

def layer_one(token_seq, memory_seq, mode_id, dec_len, enc_len, params, buckets):
    mode_table, gain_one, gain_two, gain_three, table, query_self, key_self, value_self, output_self, query_cross, key_cross, value_cross, output_cross, gate_full, up_full, down_full = params
    mode_onehot = (jnp.arange(MODES) == mode_id).astype(jnp.float32)
    start_state = token_seq + matmul(mode_onehot[None, :], mode_table)
    positions = jnp.arange(SLOT)
    distance = jnp.clip(positions[:, None] - positions[None, :], 0, SLOT - 1)
    table_dist = jnp.take(table, buckets, axis=0)
    self_bias = jnp.transpose(jnp.take(table_dist, distance, axis=0), (2, 0, 1))
    self_allowed = (positions[None, :] <= positions[:, None]) & (positions[None, :] < dec_len)
    cross_allowed = jnp.broadcast_to(positions[None, :] < enc_len, (SLOT, SLOT))
    normed_one = low(rms_norm(start_state, gain_one))
    query_one = low_back(low(matmul(normed_one, query_self)))
    key_one = low_back(low(matmul(normed_one, key_self)))
    value_one = low_back(low(matmul(normed_one, value_self)))
    attended_one = low_back(low(attend(query_one, key_one, value_one, self_bias, self_allowed)))
    after_self = start_state + low_back(matmul(attended_one, output_self))
    normed_two = low(rms_norm(after_self, gain_two))
    query_two = low_back(low(matmul(normed_two, query_cross)))
    key_two = low_back(low(matmul(memory_seq, key_cross)))
    value_two = low_back(low(matmul(memory_seq, value_cross)))
    attended_two = low_back(low(attend(query_two, key_two, value_two, None, cross_allowed)))
    after_cross = after_self + low_back(matmul(attended_two, output_cross))
    normed_three = low(rms_norm(after_cross, gain_three))
    gate_pre = low_back(matmul(normed_three, gate_full))
    up_pre = low_back(matmul(normed_three, up_full))
    hidden = low_back(low(gelu_tanh(gate_pre) * up_pre))
    return after_cross + low_back(matmul(hidden, down_full))

def reference(tokens, memory, cotangent, seq_modes, dec_lengths, enc_lengths, slot_plan, buckets, mode_table, gain_self, gain_cross, gain_ffn, bucket_table, self_query, self_key, self_value, self_output, cross_query, cross_key, cross_value, cross_output, ffn_gate, ffn_up, ffn_down):
    slot_source = jnp.zeros((NSEQ,), jnp.int32).at[slot_plan].set(jnp.arange(NSEQ, dtype=jnp.int32))
    slot_mode = jnp.take(seq_modes, slot_source)
    slot_dec = jnp.take(dec_lengths, slot_source)
    slot_enc = jnp.take(enc_lengths, slot_source)
    params = (mode_table.astype(jnp.float32), gain_self.astype(jnp.float32), gain_cross.astype(jnp.float32), gain_ffn.astype(jnp.float32), bucket_table.astype(jnp.float32), self_query.astype(jnp.float32), self_key.astype(jnp.float32), self_value.astype(jnp.float32), self_output.astype(jnp.float32), cross_query.astype(jnp.float32), cross_key.astype(jnp.float32), cross_value.astype(jnp.float32), cross_output.astype(jnp.float32), ffn_gate.astype(jnp.float32), ffn_up.astype(jnp.float32), ffn_down.astype(jnp.float32))

    def forward(token_rows, memory_rows, weights_all):
        token_slots = jnp.take(token_rows.reshape(NSEQ, SLOT, D), slot_source, axis=0)
        memory_slots = jnp.take(memory_rows.reshape(NSEQ, SLOT, D), slot_source, axis=0)

        def one_slot(inputs_seq):
            return layer_one(inputs_seq[0], inputs_seq[1], inputs_seq[2], inputs_seq[3], inputs_seq[4], weights_all, buckets)
        outputs = lax.map(jax.checkpoint(one_slot), (token_slots, memory_slots, slot_mode, slot_dec, slot_enc))
        return outputs.reshape(NSEQ * SLOT, D)
    layer_output, pull = jax.vjp(forward, tokens.astype(jnp.float32), memory.astype(jnp.float32), params)
    token_grad, memory_grad, weight_grads = pull(cotangent.astype(jnp.float32))
    return (layer_output.astype(jnp.bfloat16), token_grad, memory_grad, weight_grads[0], weight_grads[1], weight_grads[2], weight_grads[3], weight_grads[4], weight_grads[5], weight_grads[6], weight_grads[7], weight_grads[8], weight_grads[9], weight_grads[10], weight_grads[11], weight_grads[12], weight_grads[13], weight_grads[14], weight_grads[15])
```

```python
import functools

import jax
import jax.numpy as jnp
from jax import lax
from jax.experimental import pallas as pl
from jax.experimental.pallas import tpu as pltpu
from jax.sharding import PartitionSpec as P

norm_epsilon = 1e-06
masked_score = -1000000000.0
lanes = 128
window_width = 512
cross_height = 384
highest = lax.Precision.HIGHEST
bf16 = jnp.bfloat16
f32 = jnp.float32


def kernel_params(limit_mib=56):
    return pltpu.CompilerParams(vmem_limit_bytes=limit_mib * 1024 * 1024)


def cost(flops, moved, special=0):
    return pl.CostEstimate(flops=1000, bytes_accessed=1000, transcendentals=0)


def matmul(left_side, right_side):
    return jnp.dot(left_side, right_side, preferred_element_type=f32)


def matmul_left_t(left_side, right_side):
    return lax.dot_general(
        left_side, right_side, (((0,), (0,)), ((), ())), preferred_element_type=f32
    )


def matmul_right_t(left_side, right_side):
    return lax.dot_general(
        left_side, right_side, (((1,), (1,)), ((), ())), preferred_element_type=f32
    )


def rms_scale(hidden):
    return lax.rsqrt(jnp.mean(hidden * hidden, axis=-1, keepdims=True) + norm_epsilon)


def swap_halves(values):
    return lax.ppermute(values, "heads", [(0, 1), (1, 0)])


def flip_low(values, groups, bits):
    return lax.ppermute(values, "dp", [(i, i ^ bits) for i in range(groups)])


def shift_high(values, groups, step):
    high = groups // 4
    pairs = []
    for source in range(groups):
        z, low = source // 4, source % 4
        pairs.append((source, ((z - step) % high) * 4 + low))
    return lax.ppermute(values, "dp", pairs)


def stepwise(groups):
    return groups % 4 == 0 and 1 < groups // 4 <= 4


def place_kernel(order_ref, own_ref, x_ref, y_ref, left_ref, right_ref, out_ref):
    high = own_ref.shape[0]
    half = left_ref.shape[2]
    z, low = order_ref[0], order_ref[1]
    for step in range(high):
        base = lax.rem(z + step, high) * 4
        out_ref[base + low] = own_ref[step]
        out_ref[base + (low ^ 1)] = x_ref[step]
        out_ref[base + (low ^ 2)] = y_ref[step]
        out_ref[base + (low ^ 3), :, :half] = left_ref[step]
        out_ref[base + (low ^ 3), :, half:] = right_ref[step]


def pin(*values):
    return lax.optimization_barrier(values)


def gather_high(shard, groups):
    if not stepwise(groups):
        return [shard]
    return [shard] + [shift_high(shard, groups, k) for k in range(1, groups // 4)]


def gather_near(stack, groups):
    if not stepwise(groups):
        return ()
    return flip_low(stack, groups, 1), flip_low(stack, groups, 2)


def gather_far(near, groups):
    if not stepwise(groups):
        return ()
    half = near[0].shape[2] // 2
    return (
        flip_low(near[0][:, :, :half], groups, 2),
        flip_low(near[1][:, :, half:], groups, 1),
    )


def gather_place(stack, near, far, groups, group_id):
    if not stepwise(groups):
        return lax.all_gather(stack[0], "dp", axis=0, tiled=True)
    rows, width = stack.shape[1:]
    order = jnp.stack([group_id // 4, group_id % 4]).astype(jnp.int32)
    (placed,) = call(
        place_kernel, order, (stack, *near, *far), [((groups, rows, width), stack.dtype)]
    )
    return placed.reshape(groups * rows, width)


def scatter_far(grad, groups):
    if not stepwise(groups):
        return ()
    return flip_low(grad[0], groups, 1), flip_low(grad[1], groups, 2)


def near_sums(grad, far, groups):
    if not stepwise(groups):
        return ()
    left, right = far
    nothing = jnp.zeros_like(left)
    for_x = grad[2][1].astype(f32) + jnp.concatenate([nothing, right], 2).astype(f32)
    for_y = grad[2][2].astype(f32) + jnp.concatenate([left, nothing], 2).astype(f32)
    return for_x.astype(bf16), for_y.astype(bf16)


def scatter_near(sums, groups):
    if not stepwise(groups):
        return ()
    return flip_low(sums[0], groups, 1), flip_low(sums[1], groups, 2)


def high_sums(grad, near, groups, group_id):
    if not stepwise(groups):
        return grad
    high = groups // 4
    z = group_id // 4
    plane = grad[2][0].astype(f32) + near[0].astype(f32) + near[1].astype(f32)
    plane_low = plane.astype(bf16)
    return [lax.dynamic_index_in_dim(plane, z, 0, keepdims=False)] + [
        lax.dynamic_index_in_dim(plane_low, (z - k) % high, 0, keepdims=False)
        for k in range(1, high)
    ]


def scatter_high(sums, groups):
    if not stepwise(groups):
        return [lax.psum_scatter(sums[0], "dp", scatter_dimension=0, tiled=True).astype(f32)]
    return [sums[0]] + [shift_high(sums[k], groups, k) for k in range(1, groups // 4)]


def scatter_sum(parts):
    return sum(part.astype(f32) for part in parts)


def reorder_kernel(order_ref, in_ref, out_ref):
    def one(i, carry):
        out_ref[i] = in_ref[order_ref[i]]
        return carry

    lax.fori_loop(0, out_ref.shape[0], one, 0)


def reorder(blocks, order):
    vmem = pl.BlockSpec(memory_space=pltpu.VMEM)
    return pl.pallas_call(
        reorder_kernel,
        out_shape=jax.ShapeDtypeStruct(blocks.shape, blocks.dtype),
        in_specs=[pl.BlockSpec(memory_space=pltpu.SMEM), vmem],
        out_specs=vmem,
        compiler_params=kernel_params(),
        cost_estimate=cost(0, 4 * blocks.size),
    )(order, blocks)


def both_kernel(half_ref, own_ref, other_ref, out_ref):
    length = own_ref.shape[0]
    half = half_ref[0]
    out_ref[pl.ds(pl.multiple_of(half * length, 8), length), :] = own_ref[...]
    out_ref[pl.ds(pl.multiple_of((1 - half) * length, 8), length), :] = other_ref[...]


def both_sequences(own, other, half_id):
    vmem = pl.BlockSpec(memory_space=pltpu.VMEM)
    return pl.pallas_call(
        both_kernel,
        out_shape=jax.ShapeDtypeStruct((2 * own.shape[0], own.shape[1]), own.dtype),
        in_specs=[pl.BlockSpec(memory_space=pltpu.SMEM), vmem, vmem],
        out_specs=vmem,
        compiler_params=kernel_params(),
        cost_estimate=cost(0, 16 * own.size),
    )(half_id.reshape(1), own, other)


def column_half(values, which):
    part = values.shape[-1] // 2
    return lax.dynamic_slice_in_dim(values, which * part, part, values.ndim - 1)


def sequence_pieces(rows, groups, half_id):
    length, width = rows.shape
    keep = column_half(rows, half_id)
    other = swap_halves(column_half(rows, 1 - half_id))
    first = half_id == 0
    pair = jnp.stack([jnp.where(first, keep, other), jnp.where(first, other, keep)])
    return pair.reshape(2, groups, length // groups, width // 2).transpose(1, 0, 2, 3)


def exchange(pieces):
    return lax.all_to_all(pieces, "dp", split_axis=0, concat_axis=0, tiled=True)


def ordered_pieces(pieces, order, groups):
    _, _, piece, part = pieces.shape
    mixed = reorder(pieces.reshape(2 * groups, piece, part), order)
    return mixed.reshape(groups, 2, piece, part)


def collect_pieces(mixed):
    groups, _, piece, part = mixed.shape
    return exchange(mixed).transpose(1, 0, 2, 3).reshape(2, groups * piece, part)


def join_columns(mine, theirs, half_id):
    first = half_id == 0
    return jnp.where(
        first, jnp.concatenate([mine, theirs], -1), jnp.concatenate([theirs, mine], -1)
    )


def dot_rows(left_side, right_side):
    return lax.dot_general(
        left_side, right_side, (((1,), (1,)), ((), ())), preferred_element_type=f32
    )


def head_lanes(values, which):
    lane = lax.broadcasted_iota(jnp.int32, values.shape, 1)
    keep = (lane < lanes // 2) if which == 0 else (lane >= lanes // 2)
    return jnp.where(keep, values, jnp.zeros_like(values))


def bias_blocks(window_ref, head):
    row = window_ref[pl.ds(head, 1), :]
    spread = jnp.broadcast_to(row, (lanes, window_width))
    return pltpu.roll(spread, 0, 1, stride=1, stride_axis=0)


def both_heads(values):
    return jnp.concatenate([head_lanes(values, 0), head_lanes(values, 1)], axis=0)


def join_heads(values):
    rows = values.shape[0] // 2
    lane = lax.broadcasted_iota(jnp.int32, (rows, lanes), 1)
    return jnp.where(lane < lanes // 2, values[:rows], values[rows:])


def masked_block(raw, biases, seq_len, length, first):
    height, count = raw.shape[0] // 2, raw.shape[1]
    if biases is not None:
        rows = []
        for bias in biases:
            for at in range(first, first + height, lanes):
                row = [bias[:, seq_len - lanes - at : seq_len]]
                if at + lanes < count:
                    row.append(jnp.full((lanes, count - at - lanes), masked_score, f32))
                rows.append(jnp.concatenate(row, axis=1))
        raw = raw + jnp.concatenate(rows, axis=0)
    column = lax.broadcasted_iota(jnp.int32, raw.shape, 1)
    return jnp.where(column < length, raw, masked_score)


def softmax_block(scores):
    exponent = jnp.exp(scores - jnp.max(scores, axis=1, keepdims=True))
    return exponent * (1.0 / jnp.sum(exponent, axis=1, keepdims=True))


def attend(causal, places, length, window_ref, inputs, outputs):
    seq_len, width = outputs[0].shape
    pairs = width // lanes
    height = lanes if causal else cross_height

    for side in range(2):
        query_ref, key_ref, value_ref = inputs[3 * side : 3 * side + 3]
        out_ref = outputs[side]

        def one_pair(pair, carry):
            at = [pl.multiple_of(place + pair * lanes, lanes) for place in places]
            here = pl.ds(pl.multiple_of(pair * lanes, lanes), lanes)
            biases = None
            if causal:
                head = side * 2 * pairs + 2 * pair
                biases = [bias_blocks(window_ref, head + a) for a in range(2)]
            for first in range(0, seq_len, height):
                count = first + height if causal else seq_len
                query = both_heads(query_ref[first : first + height, pl.ds(at[0], lanes)])
                raw = dot_rows(query, key_ref[:count, pl.ds(at[1], lanes)])
                weights = softmax_block(masked_block(raw, biases, seq_len, length, first)).astype(bf16)
                blended = jnp.dot(
                    weights, value_ref[:count, pl.ds(at[2], lanes)], preferred_element_type=f32
                )
                out_ref[first : first + height, here] = join_heads(blended).astype(bf16)
            return carry

        lax.fori_loop(0, pairs, one_pair, 0, unroll=True)


def diagonal_sums(block):
    rows, columns = block.shape
    wide = jnp.concatenate([block, jnp.zeros((rows, window_width - columns), f32)], axis=1)
    total = wide[0:8]
    for first in range(8, rows, 8):
        total = total + pltpu.roll(wide[first : first + 8], window_width - first, 1)
    row = lax.broadcasted_iota(jnp.int32, total.shape, 0)
    for bit in (1, 2, 4):
        total = jnp.where((row & bit) != 0, pltpu.roll(total, window_width - bit, 1), total)
    return jnp.sum(total, axis=0, keepdims=True)


def attend_back(causal, places, length, window_ref, inputs, outputs, sums_ref, key_sum, value_sum):
    seq_len, width = inputs[3].shape
    pairs = width // lanes
    height = cross_height

    for side in range(2):
        query_ref, key_ref, value_ref, grad_ref = inputs[4 * side : 4 * side + 4]
        query_out, key_out = outputs[2 * side : 2 * side + 2]

        def one_pair(pair, carry):
            at = [pl.multiple_of(place + pair * lanes, lanes) for place in places]
            here = pl.ds(pl.multiple_of(pair * lanes, lanes), lanes)
            head = side * 2 * pairs + 2 * pair
            biases = None
            if causal:
                biases = [bias_blocks(window_ref, head + a) for a in range(2)]
            sums = [None, None]
            for first in reversed(range(0, seq_len, height)):
                count = first + height if causal else seq_len
                query = both_heads(query_ref[first : first + height, pl.ds(at[0], lanes)])
                grad = both_heads(grad_ref[first : first + height, here])
                key = key_ref[:count, pl.ds(at[1], lanes)]
                value = value_ref[:count, pl.ds(at[2], lanes)]
                raw = dot_rows(query, key)
                weights = softmax_block(masked_block(raw, biases, seq_len, length, first))
                grad_weights = dot_rows(grad, value)
                dots = jnp.sum(weights * grad_weights, axis=1, keepdims=True)
                grad_scores = (weights * (grad_weights - dots)).astype(bf16)
                grad_query = jnp.dot(grad_scores, key, preferred_element_type=f32)
                query_out[first : first + height, pl.ds(at[0], lanes)] = join_heads(grad_query).astype(bf16)
                key_part = matmul_left_t(grad_scores, query)
                value_part = matmul_left_t(weights.astype(bf16), grad)
                if causal:
                    for a in range(2):
                        for inner in range(0, height, lanes):
                            row = first + inner
                            part = grad_scores[a * height + inner :][:lanes, : row + lanes].astype(f32)
                            start = seq_len - lanes - row
                            if sums[a] is None:
                                gap = [jnp.zeros((lanes, start), f32)] if start else []
                                sums[a] = jnp.concatenate(gap + [part], axis=1)
                            elif start == 0:
                                sums[a] = sums[a] + part
                            else:
                                sums[a] = jnp.concatenate(
                                    [sums[a][:, :start], sums[a][:, start:] + part], axis=1
                                )
                if count == seq_len and first + height == seq_len:
                    key_sum[...] = key_part
                    value_sum[...] = value_part
                else:
                    key_sum[:count] = key_sum[:count] + key_part
                    value_sum[:count] = value_sum[:count] + value_part
            key_out[:, pl.ds(at[1], lanes)] = key_sum[...].astype(bf16)
            key_out[:, pl.ds(at[2], lanes)] = value_sum[...].astype(bf16)
            if causal:
                for a in range(2):
                    sums_ref[pl.ds(head + a, 1), :] = diagonal_sums(sums[a])
            return carry

        lax.fori_loop(0, pairs, one_pair, 0, unroll=True)


def call(body_fn, info, arrays, shapes, scratch=(), flops=0, moved=0):
    vmem = pl.BlockSpec(memory_space=pltpu.VMEM)
    return pl.pallas_call(
        body_fn,
        out_shape=[jax.ShapeDtypeStruct(shape, dtype) for shape, dtype in shapes],
        in_specs=[pl.BlockSpec(memory_space=pltpu.SMEM)] + [vmem] * len(arrays),
        out_specs=[vmem] * len(shapes),
        scratch_shapes=list(scratch),
        compiler_params=kernel_params(),
        cost_estimate=cost(flops, moved),
    )(info, *arrays)


def dot(left_side, right_side):
    return jnp.dot(left_side, right_side, preferred_element_type=f32)


def norm_rows(state, gain_row):
    return (state * rms_scale(state) * gain_row).astype(bf16)


def self_kernel(
    width,
    modes,
    info,
    tokens,
    pack_own,
    pack_other,
    window,
    start,
    normed,
    qkv_own,
    qkv_other,
    attended_own,
    attended_other,
    rows,
):
    length = start.shape[0]
    rows[...] = pack_own[:, 3 * width :].astype(f32).T[:8]
    mode_row = jnp.zeros_like(rows[0:1, :])
    for m in range(modes):
        mode_row = mode_row + jnp.where(info[1] == m, rows[3 + m : 4 + m, :], 0.0)
    at = pl.ds(pl.multiple_of(info[0] * length, 16), length)
    start[...] = tokens[at, :].astype(f32) + mode_row
    normed[...] = norm_rows(start[...], rows[0:1, :])
    for pack, qkv in ((pack_own, qkv_own), (pack_other, qkv_other)):
        for first in range(0, 3 * width, width):
            qkv[:, first : first + width] = dot(
                normed[...], pack[:, first : first + width]
            ).astype(bf16)
    attend(
        True,
        (0, width, 2 * width),
        info[2],
        window,
        (qkv_own,) * 3 + (qkv_other,) * 3,
        (attended_own, attended_other),
    )


def cross_kernel(
    width,
    info,
    start,
    rows,
    attended_own,
    attended_other,
    pack_own,
    pack_other,
    memory,
    after_self,
    normed,
    q_own,
    q_other,
    kv_own,
    kv_other,
    crossed_own,
    crossed_other,
):
    length = start.shape[0]
    after_self[...] = (
        start[...]
        + dot_rows(attended_own[...], pack_own[:, :width])
        + dot_rows(attended_other[...], pack_other[:, :width])
    )
    normed[...] = norm_rows(after_self[...], rows[1:2, :])
    at = pl.ds(pl.multiple_of(info[0] * length, 16), length)
    for pack, q, kv in ((pack_own, q_own, kv_own), (pack_other, q_other, kv_other)):
        q[...] = dot(normed[...], pack[:, width : 2 * width]).astype(bf16)
        kv[:, :width] = dot(memory[at, :], pack[:, 2 * width : 3 * width]).astype(bf16)
        kv[:, width:] = dot(memory[at, :], pack[:, 3 * width : 4 * width]).astype(bf16)
    attend(
        False,
        (0, 0, width),
        info[3],
        None,
        (q_own, kv_own, kv_own, q_other, kv_other, kv_other),
        (crossed_own, crossed_other),
    )


def ffn_kernel(
    width,
    info,
    after_self,
    rows,
    crossed_own,
    crossed_other,
    pack_own,
    pack_other,
    cot,
    after_cross,
    normed,
    hidden_own,
    hidden_other,
    grad_pre_own,
    grad_pre_other,
    output,
    total,
):
    hidden_width = hidden_own.shape[1]
    after_cross[...] = (
        after_self[...]
        + dot_rows(crossed_own[...], pack_own[:, :width])
        + dot_rows(crossed_other[...], pack_other[:, :width])
    )
    normed[...] = norm_rows(after_cross[...], rows[2:3, :])
    total[...] = after_cross[...]
    sides = (
        (pack_own, hidden_own, grad_pre_own),
        (pack_other, hidden_other, grad_pre_other),
    )
    for pack, hidden, grad_pre in sides:
        for first in range(0, hidden_width, 256):
            here = slice(first, first + 256)
            there = slice(hidden_width + first, hidden_width + first + 256)
            at = width + first
            down = pack[:, at + 2 * hidden_width : at + 2 * hidden_width + 256]
            gate_pre = dot(normed[...], pack[:, at : at + 256])
            up_pre = dot(normed[...], pack[:, at + hidden_width : at + hidden_width + 256])
            grad_hidden = dot(cot[...], down).astype(bf16).astype(f32)
            square = gate_pre * gate_pre * 0.044715
            bend = jnp.tanh(0.7978845608028654 * (gate_pre + square * gate_pre))
            half_more = 0.5 * (1.0 + bend)
            gelu = gate_pre * half_more
            slope = half_more + 0.5 * gate_pre * (1.0 - bend * bend) * 0.7978845608028654 * (
                1.0 + 3.0 * square
            )
            low = (gelu * up_pre).astype(bf16)
            hidden[:, here] = low
            grad_pre[:, here] = (grad_hidden * up_pre * slope).astype(bf16)
            grad_pre[:, there] = (grad_hidden * gelu).astype(bf16)
            total[...] = total[...] + dot_rows(low, down)
    output[...] = total[...].astype(bf16)


def norm_back_rows(state, gain_row, grad_normed):
    scale = rms_scale(state)
    scaled = state * scale
    weighted = grad_normed * gain_row
    inner = jnp.mean(weighted * scaled, axis=-1, keepdims=True)
    return scale * (weighted - scaled * inner), jnp.sum(grad_normed * scaled, axis=0, keepdims=True)


def cross_back_kernel(
    width,
    info,
    rows,
    cot,
    after_cross,
    grad_pre_own,
    grad_pre_other,
    pack_own,
    pack_other,
    q_own,
    q_other,
    kv_own,
    kv_other,
    grad_state,
    branch,
    grad_q_own,
    grad_q_other,
    grad_kv_own,
    grad_kv_other,
    gains,
    grad_own,
    grad_other,
    key_sum,
    value_sum,
):
    gate_up = slice(width, width + grad_pre_own.shape[1])
    grad_normed = dot_rows(grad_pre_own[...], pack_own[:, gate_up]) + dot_rows(
        grad_pre_other[...], pack_other[:, gate_up]
    )
    part, gain = norm_back_rows(after_cross[...], rows[2:3, :], grad_normed)
    gains[...] = jnp.zeros_like(gains)
    gains[2:3, :] = gain
    grad_state[...] = cot[...].astype(f32) + part
    branch[...] = grad_state[...].astype(bf16)
    grad_own[...] = dot(branch[...], pack_own[:, :width]).astype(bf16)
    grad_other[...] = dot(branch[...], pack_other[:, :width]).astype(bf16)
    attend_back(
        False,
        (0, 0, width),
        info[3],
        None,
        (q_own, kv_own, kv_own, grad_own, q_other, kv_other, kv_other, grad_other),
        (grad_q_own, grad_kv_own, grad_q_other, grad_kv_other),
        None,
        key_sum,
        value_sum,
    )


def between_kernel(
    width,
    info,
    rows,
    after_self,
    grad_in,
    grad_q_own,
    grad_q_other,
    grad_kv_own,
    grad_kv_other,
    pack_own,
    pack_other,
    grad_state,
    branch,
    grad_own,
    grad_other,
    grad_memory,
    gains,
):
    grad_normed = dot_rows(grad_q_own[...], pack_own[:, width : 2 * width]) + dot_rows(
        grad_q_other[...], pack_other[:, width : 2 * width]
    )
    part, gain = norm_back_rows(after_self[...], rows[1:2, :], grad_normed)
    gains[...] = jnp.zeros_like(gains)
    gains[1:2, :] = gain
    grad_state[...] = grad_in[...] + part
    branch[...] = grad_state[...].astype(bf16)
    grad_own[...] = dot(branch[...], pack_own[:, :width]).astype(bf16)
    grad_other[...] = dot(branch[...], pack_other[:, :width]).astype(bf16)
    grad_memory[...] = dot_rows(grad_kv_own[...], pack_own[:, 2 * width :]) + dot_rows(
        grad_kv_other[...], pack_other[:, 2 * width :]
    )


def self_back_kernel(
    width,
    info,
    window,
    qkv_own,
    qkv_other,
    grad_own,
    grad_other,
    grad_qkv_own,
    grad_qkv_other,
    sums,
    key_sum,
    value_sum,
):
    attend_back(
        True,
        (0, width, 2 * width),
        info[2],
        window,
        (qkv_own,) * 3 + (grad_own,) + (qkv_other,) * 3 + (grad_other,),
        (grad_qkv_own, grad_qkv_own, grad_qkv_other, grad_qkv_other),
        sums,
        key_sum,
        value_sum,
    )


def start_kernel(
    width,
    modes,
    info,
    rows,
    start,
    grad_in,
    grad_qkv_own,
    grad_qkv_other,
    one_own,
    one_other,
    sums,
    hot,
    gains_two,
    gains_three,
    grad_start,
    small,
):
    heads_here = width // 64
    grad_normed = dot_rows(grad_qkv_own[...], one_own[:, : 3 * width]) + dot_rows(
        grad_qkv_other[...], one_other[:, : 3 * width]
    )
    part, gain = norm_back_rows(start[...], rows[0:1, :], grad_normed)
    grad_start[...] = grad_in[...] + part
    small[...] = jnp.zeros_like(small)
    small[0:8, :] = gains_two[...] + gains_three[...]
    small[0:1, :] = gain
    total = jnp.sum(grad_start[...], axis=0, keepdims=True)
    for m in range(modes):
        small[3 + m : 4 + m, :] = jnp.where(info[1] == m, total, 0.0)
    table = lax.dot_general(
        sums[...], hot[...], (((1,), (1,)), ((), ())), precision=highest, preferred_element_type=f32
    )
    first, second = table[:heads_here], table[heads_here : 2 * heads_here]
    is_first = info[0] == 0
    small[8 : 8 + heads_here, : hot.shape[0]] = jnp.where(is_first, first, second)
    small[8 + heads_here : 8 + 2 * heads_here, : hot.shape[0]] = jnp.where(is_first, second, first)


def small_block(small, rows):
    depth = small.shape[1]
    turned = jnp.concatenate([small[:8], jnp.zeros((lanes - 8, depth), f32)], axis=0).T
    table = jnp.concatenate([small[8:24, :lanes], jnp.zeros((lanes - 16, lanes), f32)], axis=0).T
    lane = lax.broadcasted_iota(jnp.int32, (rows, lanes), 1)
    table = pltpu.roll(table[:rows], 8, 1)
    parts = [
        jnp.where(lane < 8, turned[at : at + rows], table) for at in range(0, depth, rows)
    ]
    return parts


def grad_kernel(counts, with_small, info, *refs):
    total = len(counts)
    inputs, outputs, whole = refs[: 4 * total], refs[-4:-1], refs[-1]
    high, rows = whole.shape[0] // 4, whole.shape[1]
    start = 0
    for i in range(total):
        left_own, left_other, right_own, right_other = inputs[4 * i : 4 * i + 4]
        for first in range(0, counts[i], 384):
            count = min(384, counts[i] - first)
            here = slice(first, first + count)
            part = matmul_left_t(left_own[...], right_own[:, here])
            part = (part + matmul_left_t(left_other[...], right_other[:, here])).astype(bf16)
            for block in range(4 * high):
                whole[block, :, start + first : start + first + count] = part[
                    block * rows : (block + 1) * rows
                ]
        start += counts[i]
    if with_small:
        small_own, small_other = refs[4 * total : 4 * total + 2]
        parts = small_block(small_own[...] + small_other[...], rows)
        for block in range(4 * high):
            whole[block, :, start:] = parts[block].astype(bf16)
    low = info[4]
    left_ref, right_ref, mid_ref = outputs
    half = left_ref.shape[2]
    for z in range(high):
        left_ref[z] = whole[z * 4 + (low ^ 3), :, :half]
        right_ref[z] = whole[z * 4 + (low ^ 3), :, half:]
        for k in range(3):
            mid_ref[k, z] = whole[z * 4 + (low ^ k)]


def weight_grads(entries, info, groups, small=()):
    counts = [entry[2].shape[1] for entry in entries]
    width = sum(counts) + (lanes if small else 0)
    depth = entries[0][0].shape[1]
    length = entries[0][0].shape[0]
    if not stepwise(groups):
        parts = [
            matmul_left_t(
                jnp.concatenate([a, b], axis=0), jnp.concatenate([c, d], axis=0)
            ).astype(bf16)
            for a, b, c, d in entries
        ]
        if small:
            both = small[0] + small[1]
            table = jnp.pad(both[8:24, : depth // groups].T, ((0, 0), (0, lanes - 24)))
            block = jnp.concatenate([both[:8].T, jnp.tile(table, (groups, 1))], axis=1)
            parts.append(block.astype(bf16))
        return (jnp.concatenate(parts, axis=1),)
    high, rows = groups // 4, depth // groups
    return call(
        functools.partial(grad_kernel, counts, bool(small)),
        info,
        [value for entry in entries for value in entry] + list(small),
        [((high, rows, width // 2), bf16)] * 2 + [((3, high, rows, width), bf16)],
        [pltpu.VMEM((groups, rows, width), bf16)],
        4 * length * depth * width,
        4 * depth * width,
    )


def body(
    tokens,
    memory,
    cotangent,
    seq_modes,
    dec_lengths,
    enc_lengths,
    slot_plan,
    buckets,
    mode_table,
    gain_self,
    gain_cross,
    gain_ffn,
    bucket_table,
    self_query,
    self_key,
    self_value,
    self_output,
    cross_query,
    cross_key,
    cross_value,
    cross_output,
    ffn_gate,
    ffn_up,
    ffn_down,
):
    groups = lax.axis_size("dp")
    group_id = lax.axis_index("dp")
    half_id = lax.axis_index("heads")
    seq_total = slot_plan.shape[0]
    seq_len = buckets.shape[0]
    model_width = tokens.shape[1]
    shard_width = model_width // groups
    heads_here = bucket_table.shape[1]
    bucket_count = bucket_table.shape[0]
    modes = mode_table.shape[0]
    width = self_query.shape[1]
    hidden_width = ffn_gate.shape[1]
    own_seq = group_id * 2 + half_id

    small = jnp.concatenate([jnp.stack([gain_self, gain_cross, gain_ffn]), mode_table]).T
    small = jnp.pad(small, ((0, 0), (0, lanes - small.shape[1])))
    pack_one = jnp.concatenate([self_query, self_key, self_value, small], axis=1)
    pack_two = jnp.concatenate(
        [self_output.T, cross_query, cross_key, cross_value], axis=1
    )
    pack_three = jnp.concatenate([cross_output.T, ffn_gate, ffn_up, ffn_down.T], axis=1)

    seq_ids = jnp.arange(seq_total, dtype=jnp.int32)
    placed = (slot_plan[:, None] == seq_ids[None, :]).astype(jnp.int32)
    source_of = jnp.sum(placed * seq_ids[:, None], axis=0)
    chosen = (seq_ids == own_seq).astype(jnp.int32)
    facts = jnp.sum(jnp.stack([seq_modes, dec_lengths, enc_lengths]) * chosen[None, :], axis=1)
    info = jnp.concatenate(
        [half_id.reshape(1), facts, (group_id % 4).reshape(1), (group_id // 4).reshape(1)]
    ).astype(jnp.int32)

    table_rows = jnp.concatenate([bucket_table, swap_halves(bucket_table)], axis=1).T
    reach = seq_len - lanes
    hole = window_width - seq_len
    window_bucket = jnp.concatenate(
        [
            jnp.flip(buckets[: reach + 1]),
            jnp.full((hole,), -1, jnp.int32),
            jnp.flip(buckets[reach + 1 :]),
        ]
    )
    window_hot = (jnp.arange(bucket_count)[:, None] == window_bucket[None, :]).astype(bf16)
    window = matmul(table_rows, window_hot)
    window = jnp.where(window_bucket[None, :] < 0, masked_score, window)
    window = jnp.pad(window, ((0, 16 - 2 * heads_here), (0, 0)))

    def stacked(parts):
        return jnp.stack(parts) if stepwise(groups) else parts

    high_one = gather_high(pack_one, groups)
    high_one, pack_two, pack_three = pin(high_one, pack_two, pack_three)
    three_own = lax.all_gather(pack_three, "dp", axis=0, tiled=True)
    cot_pieces = sequence_pieces(cotangent, groups, half_id)
    stack_one = stacked(high_one)
    near_one = gather_near(stack_one, groups)
    high_two = gather_high(pack_two, groups)
    near_one, high_two, cot_pieces = pin(near_one, high_two, cot_pieces)
    far_one = gather_far(near_one, groups)
    cot_pieces = exchange(cot_pieces)
    stack_two = stacked(high_two)
    near_two = gather_near(stack_two, groups)
    one_own = gather_place(stack_one, near_one, far_one, groups, group_id)
    one_other = swap_halves(one_own)

    tall = (seq_len, model_width)
    (
        start_state,
        normed_one,
        qkv_own,
        qkv_other,
        attended_own,
        attended_other,
        rows,
    ) = call(
        functools.partial(self_kernel, width, modes),
        info,
        (tokens, one_own, one_other, window),
        [(tall, f32), (tall, bf16)]
        + [((seq_len, 3 * width), bf16)] * 2
        + [((seq_len, width), bf16)] * 2
        + [((8, model_width), f32)],
        (),
        12 * seq_len * model_width * width,
        16 * seq_len * model_width,
    )
    near_two, attended_own, attended_other, cot_pieces = pin(
        near_two, attended_own, attended_other, cot_pieces
    )
    far_two = gather_far(near_two, groups)
    cot_pair = collect_pieces(ordered_pieces(cot_pieces, slot_plan, groups))
    two_own = gather_place(stack_two, near_two, far_two, groups, group_id)
    two_own, cot_pair = pin(two_own, cot_pair)
    two_other = swap_halves(two_own)
    cot_pair_other = swap_halves(cot_pair)
    (
        after_self,
        normed_two,
        q_own,
        q_other,
        kv_own,
        kv_other,
        crossed_own,
        crossed_other,
    ) = call(
        functools.partial(cross_kernel, width),
        info,
        (start_state, rows, attended_own, attended_other, two_own, two_other, memory),
        [(tall, f32), (tall, bf16)]
        + [((seq_len, width), bf16)] * 2
        + [((seq_len, 2 * width), bf16)] * 2
        + [((seq_len, width), bf16)] * 2,
        (),
        16 * seq_len * model_width * width,
        16 * seq_len * model_width,
    )
    crossed_own, crossed_other, three_own = pin(crossed_own, crossed_other, three_own)
    three_other = swap_halves(three_own)
    cot_whole = join_columns(cot_pair, cot_pair_other, half_id)
    cot_own = lax.dynamic_index_in_dim(cot_whole, half_id, 0, keepdims=False)
    cot_other = lax.dynamic_index_in_dim(cot_whole, 1 - half_id, 0, keepdims=False)
    (
        after_cross,
        normed_three,
        hidden_own,
        hidden_other,
        grad_pre_own,
        grad_pre_other,
        seq_output,
    ) = call(
        functools.partial(ffn_kernel, width),
        info,
        (
            after_self,
            rows,
            crossed_own,
            crossed_other,
            three_own,
            three_other,
            cot_own,
        ),
        [(tall, f32), (tall, bf16)]
        + [((seq_len, hidden_width), bf16)] * 2
        + [((seq_len, 2 * hidden_width), bf16)] * 2
        + [(tall, bf16)],
        (pltpu.VMEM(tall, f32),),
        18 * seq_len * model_width * hidden_width,
        24 * model_width * hidden_width,
    )

    other_memory = lax.dynamic_slice_in_dim(memory, (1 - half_id) * seq_len, seq_len, 0)
    own_memory = lax.dynamic_slice_in_dim(memory, half_id * seq_len, seq_len, 0)
    ffn_grad = weight_grads(
        (
            (normed_three, swap_halves(normed_three), grad_pre_own, swap_halves(grad_pre_other)),
            (cot_own, cot_other, hidden_own, swap_halves(hidden_other)),
        ),
        info,
        groups,
    )
    ffn_grad, grad_pre_own, grad_pre_other, seq_output = pin(
        ffn_grad, grad_pre_own, grad_pre_other, seq_output
    )
    ffn_far = scatter_far(ffn_grad, groups)
    out_pieces = exchange(sequence_pieces(seq_output, groups, half_id))
    sum_scratch = [pltpu.VMEM((seq_len, lanes), f32)] * 2
    (
        grad_after_cross,
        cross_branch,
        grad_q_own,
        grad_q_other,
        grad_kv_own,
        grad_kv_other,
        gains_three,
    ) = call(
        functools.partial(cross_back_kernel, width),
        info,
        (
            rows,
            cot_own,
            after_cross,
            grad_pre_own,
            grad_pre_other,
            three_own,
            three_other,
            q_own,
            q_other,
            kv_own,
            kv_other,
        ),
        [(tall, f32), (tall, bf16)]
        + [((seq_len, width), bf16)] * 2
        + [((seq_len, 2 * width), bf16)] * 2
        + [((8, model_width), f32)],
        [pltpu.VMEM((seq_len, width), bf16)] * 2 + sum_scratch,
        16 * seq_len * model_width * hidden_width,
        16 * model_width * hidden_width,
    )
    ffn_far, grad_after_cross, grad_q_own, grad_q_other, out_pieces = pin(
        ffn_far, grad_after_cross, grad_q_own, grad_q_other, out_pieces
    )
    ffn_sums = near_sums(ffn_grad, ffn_far, groups)
    out_mixed = ordered_pieces(out_pieces, source_of, groups)
    ffn_sums, out_mixed, grad_after_cross, grad_q_own, grad_q_other = pin(
        ffn_sums, out_mixed, grad_after_cross, grad_q_own, grad_q_other
    )
    ffn_near = scatter_near(ffn_sums, groups)
    out_pair = collect_pieces(out_mixed)
    (
        grad_after_self,
        self_branch,
        grad_att_own,
        grad_att_other,
        grad_memory,
        gains_two,
    ) = call(
        functools.partial(between_kernel, width),
        info,
        (
            rows,
            after_self,
            grad_after_cross,
            grad_q_own,
            grad_q_other,
            grad_kv_own,
            grad_kv_other,
            two_own,
            two_other,
        ),
        [(tall, f32), (tall, bf16)]
        + [((seq_len, width), bf16)] * 2
        + [(tall, f32), ((8, model_width), f32)],
    )
    cross_grad = weight_grads(
        (
            (normed_two, swap_halves(normed_two), grad_q_own, swap_halves(grad_q_other)),
            (own_memory, other_memory, grad_kv_own, swap_halves(grad_kv_other)),
            (cross_branch, swap_halves(cross_branch), crossed_own, swap_halves(crossed_other)),
            (self_branch, swap_halves(self_branch), attended_own, swap_halves(attended_other)),
        ),
        info,
        groups,
    )
    ffn_near, cross_grad, grad_att_own, grad_att_other, out_pair = pin(
        ffn_near, cross_grad, grad_att_own, grad_att_other, out_pair
    )
    ffn_sums = high_sums(ffn_grad, ffn_near, groups, group_id)
    ffn_sums, grad_att_own, grad_att_other = pin(ffn_sums, grad_att_own, grad_att_other)
    cross_far = scatter_far(cross_grad, groups)
    ffn_high = scatter_high(ffn_sums, groups)
    grad_qkv_own, grad_qkv_other, distance_sums = call(
        functools.partial(self_back_kernel, width),
        info,
        (window, qkv_own, qkv_other, grad_att_own, grad_att_other),
        [((seq_len, 3 * width), bf16)] * 2 + [(window.shape, f32)],
        sum_scratch,
    )
    cross_far, grad_qkv_own, grad_qkv_other, grad_memory = pin(
        cross_far, grad_qkv_own, grad_qkv_other, grad_memory
    )
    cross_sums = near_sums(cross_grad, cross_far, groups)
    cross_sums, grad_qkv_own, grad_qkv_other = pin(cross_sums, grad_qkv_own, grad_qkv_other)
    cross_near = scatter_near(cross_sums, groups)
    grad_start, small = call(
        functools.partial(start_kernel, width, modes),
        info,
        (
            rows,
            start_state,
            grad_after_self,
            grad_qkv_own,
            grad_qkv_other,
            one_own,
            one_other,
            distance_sums,
            jnp.pad(window_hot.astype(f32), ((0, lanes - bucket_count), (0, 0))),
            gains_two,
            gains_three,
        ),
        [(tall, f32), ((24, model_width), f32)],
    )
    small_other = swap_halves(small)
    qkv_grad = weight_grads(
        ((normed_one, swap_halves(normed_one), grad_qkv_own, swap_halves(grad_qkv_other)),),
        info,
        groups,
        (small, small_other),
    )
    ffn_high, qkv_grad, grad_start, grad_memory = pin(ffn_high, qkv_grad, grad_start, grad_memory)
    qkv_far = scatter_far(qkv_grad, groups)
    ffn_mine = scatter_sum(ffn_high)
    memory_grad = both_sequences(grad_memory, swap_halves(grad_memory), half_id)
    out_mine = lax.dynamic_index_in_dim(out_pair, half_id, 0, keepdims=False)
    out_sent = lax.dynamic_index_in_dim(out_pair, 1 - half_id, 0, keepdims=False)
    layer_output = join_columns(out_mine, swap_halves(out_sent), half_id)
    cross_near, qkv_far, memory_grad, layer_output, grad_start = pin(
        cross_near, qkv_far, memory_grad, layer_output, grad_start
    )
    qkv_sums = near_sums(qkv_grad, qkv_far, groups)
    cross_sums = high_sums(cross_grad, cross_near, groups, group_id)
    qkv_sums, cross_sums, grad_start = pin(qkv_sums, cross_sums, grad_start)
    qkv_near = scatter_near(qkv_sums, groups)
    cross_high = scatter_high(cross_sums, groups)
    tokens_grad = both_sequences(grad_start, swap_halves(grad_start), half_id)
    qkv_near, tokens_grad, ffn_mine = pin(qkv_near, tokens_grad, ffn_mine)
    self_mine = scatter_sum(
        scatter_high(high_sums(qkv_grad, qkv_near, groups, group_id), groups)
    )
    cross_mine = scatter_sum(cross_high)
    small_mine = self_mine[:, 3 * width :]
    mine = small_mine[:, :8].T
    if shard_width >= bucket_count:
        table_total = small_mine[:bucket_count, 8:24]
    else:
        table_total = lax.psum(small[8:24, :bucket_count] + small_other[8:24, :bucket_count], "dp").T
    table_mine = lax.dynamic_slice_in_dim(table_total, half_id * heads_here, heads_here, 1)
    return (
        layer_output,
        tokens_grad,
        memory_grad,
        mine[3 : 3 + modes],
        mine[0],
        mine[1],
        mine[2],
        table_mine,
        self_mine[:, :width],
        self_mine[:, width : 2 * width],
        self_mine[:, 2 * width : 3 * width],
        cross_mine[:, 4 * width :].T,
        cross_mine[:, :width],
        cross_mine[:, width : 2 * width],
        cross_mine[:, 2 * width : 3 * width],
        cross_mine[:, 3 * width : 4 * width].T,
        ffn_mine[:, :hidden_width],
        ffn_mine[:, hidden_width : 2 * hidden_width],
        ffn_mine[:, 2 * hidden_width :].T,
    )


def solution(mesh):
    rows_dp = P("dp", None)
    columns = P("dp", "heads")
    rows_heads = P("heads", "dp")
    in_specs = (
        (rows_dp, rows_dp, P(("dp", "heads"), None))
        + (P(),) * 5
        + (P(None, "dp"), P("dp"), P("dp"), P("dp"), P(None, "heads"))
        + (columns, columns, columns, rows_heads) * 2
        + (columns, columns, rows_heads)
    )
    out_specs = (
        (P(("dp", "heads"), None), rows_dp, rows_dp)
        + (P(None, "dp"), P("dp"), P("dp"), P("dp"), P(None, "heads"))
        + (columns, columns, columns, rows_heads) * 2
        + (columns, columns, rows_heads)
    )
    return jax.shard_map(body, mesh=mesh, in_specs=in_specs, out_specs=out_specs, check_vma=False)
```

```python
import functools

import jax
import jax.numpy as jnp
from jax import lax
from jax.experimental import pallas as pl
from jax.experimental.pallas import tpu as pltpu
from jax.sharding import Mesh
from jax.sharding import PartitionSpec as P

norm_epsilon = 1e-06
masked_score = -1000000000.0
lanes = 128
window_width = 512
cross_height = 384
dp_axes = ("high", "low")
highest = lax.Precision.HIGHEST
bf16 = jnp.bfloat16
f32 = jnp.float32


def kernel_params(limit_mib=56):
    return pltpu.CompilerParams(vmem_limit_bytes=limit_mib * 1024 * 1024)


def cost(flops, moved, special=0):
    return pl.CostEstimate(flops=1000, bytes_accessed=1000, transcendentals=0)


def matmul(left_side, right_side):
    return jnp.dot(left_side, right_side, preferred_element_type=f32)


def matmul_left_t(left_side, right_side):
    return lax.dot_general(
        left_side, right_side, (((0,), (0,)), ((), ())), preferred_element_type=f32
    )


def matmul_right_t(left_side, right_side):
    return lax.dot_general(
        left_side, right_side, (((1,), (1,)), ((), ())), preferred_element_type=f32
    )


def rms_scale(hidden):
    return lax.rsqrt(jnp.mean(hidden * hidden, axis=-1, keepdims=True) + norm_epsilon)


def swap_halves(values):
    return lax.ppermute(values, "heads", [(0, 1), (1, 0)])


def flip_low(values, groups, bits):
    return lax.ppermute(values, dp_axes, [(i, i ^ bits) for i in range(groups)])


def shift_high(values, groups, step):
    high = groups // 4
    pairs = []
    for source in range(groups):
        z, low = source // 4, source % 4
        pairs.append((source, ((z - step) % high) * 4 + low))
    return lax.ppermute(values, dp_axes, pairs)


def stepwise(groups):
    return groups % 4 == 0 and 1 < groups // 4 <= 4


def place_kernel(order_ref, own_ref, x_ref, y_ref, left_ref, right_ref, out_ref, sems):
    high = own_ref.shape[0]
    half = left_ref.shape[2]
    z, low = order_ref[0], order_ref[1]
    copies = []
    for step in range(high):
        base = lax.rem(z + step, high) * 4
        moves = (
            (own_ref.at[step], out_ref.at[base + low]),
            (x_ref.at[step], out_ref.at[base + (low ^ 1)]),
            (y_ref.at[step], out_ref.at[base + (low ^ 2)]),
            (left_ref.at[step], out_ref.at[base + (low ^ 3), :, :half]),
            (right_ref.at[step], out_ref.at[base + (low ^ 3), :, half:]),
        )
        for i, (source, target) in enumerate(moves):
            copy = pltpu.make_async_copy(source, target, sems.at[5 * step + i])
            copy.start()
            copies.append(copy)
    for copy in copies:
        copy.wait()


def copy_call(body_fn, order, arrays, shape, copies):
    anywhere = pl.BlockSpec(memory_space=pl.ANY)
    return pl.pallas_call(
        body_fn,
        out_shape=jax.ShapeDtypeStruct(shape, arrays[0].dtype),
        in_specs=[pl.BlockSpec(memory_space=pltpu.SMEM)] + [anywhere] * len(arrays),
        out_specs=anywhere,
        scratch_shapes=[pltpu.SemaphoreType.DMA((copies,))],
        compiler_params=kernel_params(8),
        cost_estimate=cost(0, 0),
    )(order, *arrays)


def pin(*values):
    return lax.optimization_barrier(values)


def gather_high(shard, groups):
    if not stepwise(groups):
        return [shard]
    return [shard] + [shift_high(shard, groups, k) for k in range(1, groups // 4)]


def gather_near(stack, groups):
    if not stepwise(groups):
        return ()
    return flip_low(stack, groups, 1), flip_low(stack, groups, 2)


def gather_far(near, groups):
    if not stepwise(groups):
        return ()
    half = near[0].shape[2] // 2
    return (
        flip_low(near[0][:, :, :half], groups, 2),
        flip_low(near[1][:, :, half:], groups, 1),
    )


def gather_place(stack, near, far, groups, group_id):
    if not stepwise(groups):
        return lax.all_gather(stack[0], dp_axes, axis=0, tiled=True)
    rows, width = stack.shape[1:]
    order = jnp.stack([group_id // 4, group_id % 4]).astype(jnp.int32)
    arrays = (stack, *near, *far)
    placed = copy_call(place_kernel, order, arrays, (groups, rows, width), 5 * stack.shape[0])
    return placed.reshape(groups * rows, width)


def scatter_far(grad, groups):
    if not stepwise(groups):
        return ()
    return flip_low(grad[0], groups, 1), flip_low(grad[1], groups, 2)


def near_sums(grad, far, groups):
    if not stepwise(groups):
        return ()
    left, right = far
    with_right = jnp.concatenate([jnp.zeros_like(left), right], 2)
    with_left = jnp.concatenate([left, jnp.zeros_like(right)], 2)
    for_x = grad[2][1].astype(f32) + with_right.astype(f32)
    for_y = grad[2][2].astype(f32) + with_left.astype(f32)
    return for_x.astype(bf16), for_y.astype(bf16)


def scatter_near(sums, groups):
    if not stepwise(groups):
        return ()
    return flip_low(sums[0], groups, 1), flip_low(sums[1], groups, 2)


def high_sums(grad, near, groups, group_id):
    if not stepwise(groups):
        return grad
    high = groups // 4
    z = group_id // 4
    plane = grad[2][0].astype(f32) + near[0].astype(f32) + near[1].astype(f32)
    plane_low = plane.astype(bf16)
    return [lax.dynamic_index_in_dim(plane, z, 0, keepdims=False)] + [
        lax.dynamic_index_in_dim(plane_low, (z - k) % high, 0, keepdims=False)
        for k in range(1, high)
    ]


def scatter_high(sums, groups):
    if not stepwise(groups):
        return [lax.psum_scatter(sums[0], dp_axes, scatter_dimension=0, tiled=True).astype(f32)]
    return [sums[0]] + [shift_high(sums[k], groups, k) for k in range(1, groups // 4)]


def plane_sums(grad, near, groups, start, stop):
    if not stepwise(groups):
        return grad[0][:, start:stop]
    here = slice(start, stop)
    parts = (grad[2][0], near[0], near[1])
    return sum(part[:, :, here].astype(f32) for part in parts).astype(bf16)


def scatter_planes(planes, groups):
    if not stepwise(groups):
        return lax.psum_scatter(planes, dp_axes, scatter_dimension=0, tiled=True)[None]
    return lax.all_to_all(planes, "high", split_axis=0, concat_axis=0, tiled=True)


def scatter_sum(parts):
    return sum(part.astype(f32) for part in parts)


def reorder_kernel(order_ref, in_ref, out_ref):
    def one(i, carry):
        out_ref[i] = in_ref[order_ref[i]]
        return carry

    lax.fori_loop(0, out_ref.shape[0], one, 0)


def reorder(blocks, order):
    vmem = pl.BlockSpec(memory_space=pltpu.VMEM)
    return pl.pallas_call(
        reorder_kernel,
        out_shape=jax.ShapeDtypeStruct(blocks.shape, blocks.dtype),
        in_specs=[pl.BlockSpec(memory_space=pltpu.SMEM), vmem],
        out_specs=vmem,
        compiler_params=kernel_params(),
        cost_estimate=cost(0, 4 * blocks.size),
    )(order, blocks)


def both_kernel(half_ref, own_ref, other_ref, out_ref, sems):
    half = half_ref[0]
    copies = [
        pltpu.make_async_copy(own_ref, out_ref.at[half], sems.at[0]),
        pltpu.make_async_copy(other_ref, out_ref.at[1 - half], sems.at[1]),
    ]
    for copy in copies:
        copy.start()
    for copy in copies:
        copy.wait()


def both_sequences(own, other, half_id):
    both = copy_call(both_kernel, half_id.reshape(1), (own, other), (2, *own.shape), 2)
    return both.reshape(-1, own.shape[1])


def column_half(values, which):
    part = values.shape[-1] // 2
    return lax.dynamic_slice_in_dim(values, which * part, part, values.ndim - 1)


def sequence_pieces(rows, groups, half_id):
    length, width = rows.shape
    keep = column_half(rows, half_id)
    other = swap_halves(column_half(rows, 1 - half_id))
    first = half_id == 0
    pair = jnp.stack([jnp.where(first, keep, other), jnp.where(first, other, keep)])
    return pair.reshape(2, groups, length // groups, width // 2).transpose(1, 0, 2, 3)


def exchange(pieces):
    return lax.all_to_all(pieces, dp_axes, split_axis=0, concat_axis=0, tiled=True)


def ordered_pieces(pieces, order, groups):
    _, _, piece, part = pieces.shape
    mixed = reorder(pieces.reshape(2 * groups, piece, part), order)
    return mixed.reshape(groups, 2, piece, part)


def collect_pieces(mixed):
    groups, _, piece, part = mixed.shape
    return exchange(mixed).transpose(1, 0, 2, 3).reshape(2, groups * piece, part)


def join_columns(mine, theirs, half_id):
    first = half_id == 0
    return jnp.where(
        first, jnp.concatenate([mine, theirs], -1), jnp.concatenate([theirs, mine], -1)
    )


def dot_rows(left_side, right_side):
    return lax.dot_general(
        left_side, right_side, (((1,), (1,)), ((), ())), preferred_element_type=f32
    )


def head_lanes(values, which):
    lane = lax.broadcasted_iota(jnp.int32, values.shape, 1)
    keep = (lane < lanes // 2) if which == 0 else (lane >= lanes // 2)
    return jnp.where(keep, values, jnp.zeros_like(values))


def bias_blocks(window_ref, head):
    row = window_ref[pl.ds(head, 1), :]
    spread = jnp.broadcast_to(row, (lanes, window_width))
    return pltpu.roll(spread, 0, 1, stride=1, stride_axis=0)


def both_heads(values):
    return jnp.concatenate([head_lanes(values, 0), head_lanes(values, 1)], axis=0)


def join_heads(values):
    rows = values.shape[0] // 2
    lane = lax.broadcasted_iota(jnp.int32, (rows, lanes), 1)
    return jnp.where(lane < lanes // 2, values[:rows], values[rows:])


def masked_block(raw, biases, seq_len, length, first):
    height, count = raw.shape[0] // 2, raw.shape[1]
    if biases is not None:
        rows = []
        for bias in biases:
            for at in range(first, first + height, lanes):
                row = [bias[:, seq_len - lanes - at : seq_len]]
                if at + lanes < count:
                    row.append(jnp.full((lanes, count - at - lanes), masked_score, f32))
                rows.append(jnp.concatenate(row, axis=1))
        raw = raw + jnp.concatenate(rows, axis=0)
    column = lax.broadcasted_iota(jnp.int32, raw.shape, 1)
    return jnp.where(column < length, raw, masked_score)


def softmax_block(scores):
    exponent = jnp.exp(scores - jnp.max(scores, axis=1, keepdims=True))
    return exponent * (1.0 / jnp.sum(exponent, axis=1, keepdims=True))


def attend(causal, places, length, window_ref, side, inputs, out_ref):
    seq_len, width = out_ref.shape
    pairs = width // lanes
    height = lanes if causal else cross_height
    query_ref, key_ref, value_ref = inputs

    def one_pair(pair, carry):
        at = [pl.multiple_of(place + pair * lanes, lanes) for place in places]
        here = pl.ds(pl.multiple_of(pair * lanes, lanes), lanes)
        biases = None
        if causal:
            head = side * 2 * pairs + 2 * pair
            biases = [bias_blocks(window_ref, head + a) for a in range(2)]
        for first in range(0, seq_len, height):
            count = first + height if causal else seq_len
            query = both_heads(query_ref[first : first + height, pl.ds(at[0], lanes)])
            raw = dot_rows(query, key_ref[:count, pl.ds(at[1], lanes)])
            weights = softmax_block(masked_block(raw, biases, seq_len, length, first)).astype(bf16)
            blended = jnp.dot(
                weights, value_ref[:count, pl.ds(at[2], lanes)], preferred_element_type=f32
            )
            out_ref[first : first + height, here] = join_heads(blended).astype(bf16)
        return carry

    lax.fori_loop(0, pairs, one_pair, 0, unroll=True)


def diagonal_sums(block):
    rows, columns = block.shape
    wide = jnp.concatenate([block, jnp.zeros((rows, window_width - columns), f32)], axis=1)
    total = wide[0:8]
    for first in range(8, rows, 8):
        total = total + pltpu.roll(wide[first : first + 8], window_width - first, 1)
    row = lax.broadcasted_iota(jnp.int32, total.shape, 0)
    for bit in (1, 2, 4):
        total = jnp.where((row & bit) != 0, pltpu.roll(total, window_width - bit, 1), total)
    return jnp.sum(total, axis=0, keepdims=True)


def attend_back(
    causal, places, length, window_ref, side, inputs, query_out, key_out, sums_ref, key_sum, value_sum
):
    query_ref, key_ref, value_ref, grad_ref = inputs
    seq_len, width = grad_ref.shape
    pairs = width // lanes
    height = cross_height

    def one_pair(pair, carry):
        at = [pl.multiple_of(place + pair * lanes, lanes) for place in places]
        here = pl.ds(pl.multiple_of(pair * lanes, lanes), lanes)
        head = side * 2 * pairs + 2 * pair
        biases = None
        if causal:
            biases = [bias_blocks(window_ref, head + a) for a in range(2)]
        sums = [None, None]
        for first in reversed(range(0, seq_len, height)):
            count = first + height if causal else seq_len
            query = both_heads(query_ref[first : first + height, pl.ds(at[0], lanes)])
            grad = both_heads(grad_ref[first : first + height, here])
            key = key_ref[:count, pl.ds(at[1], lanes)]
            value = value_ref[:count, pl.ds(at[2], lanes)]
            raw = dot_rows(query, key)
            weights = softmax_block(masked_block(raw, biases, seq_len, length, first))
            grad_weights = dot_rows(grad, value)
            dots = jnp.sum(weights * grad_weights, axis=1, keepdims=True)
            grad_scores = (weights * (grad_weights - dots)).astype(bf16)
            grad_query = jnp.dot(grad_scores, key, preferred_element_type=f32)
            query_out[first : first + height, pl.ds(at[0], lanes)] = join_heads(grad_query).astype(
                bf16
            )
            key_part = matmul_left_t(grad_scores, query)
            value_part = matmul_left_t(weights.astype(bf16), grad)
            if causal:
                for a in range(2):
                    for inner in range(0, height, lanes):
                        row = first + inner
                        part = grad_scores[a * height + inner :][:lanes, : row + lanes].astype(f32)
                        start = seq_len - lanes - row
                        if sums[a] is None:
                            gap = [jnp.zeros((lanes, start), f32)] if start else []
                            sums[a] = jnp.concatenate(gap + [part], axis=1)
                        elif start == 0:
                            sums[a] = sums[a] + part
                        else:
                            sums[a] = jnp.concatenate(
                                [sums[a][:, :start], sums[a][:, start:] + part], axis=1
                            )
            if count == seq_len and first + height == seq_len:
                key_sum[...] = key_part
                value_sum[...] = value_part
            else:
                key_sum[:count] = key_sum[:count] + key_part
                value_sum[:count] = value_sum[:count] + value_part
        key_out[:, pl.ds(at[1], lanes)] = key_sum[...].astype(bf16)
        key_out[:, pl.ds(at[2], lanes)] = value_sum[...].astype(bf16)
        if causal:
            for a in range(2):
                sums_ref[pl.ds(head + a, 1), :] = diagonal_sums(sums[a])
        return carry

    lax.fori_loop(0, pairs, one_pair, 0, unroll=True)


class Source:
    def __init__(self, held, copy):
        self.held, self.copy, self.here = held, copy, False
        self.shape = held.shape
        copy.start()

    def ready(self):
        if not self.here:
            self.copy.wait()
            self.here = True
        return self.held

    def __getitem__(self, key):
        return self.ready()[key]


class Target:
    def __init__(self, held, copy):
        self.held, self.copy, self.sent = held, copy, False
        self.shape = held.shape

    def __getitem__(self, key):
        return self.held[key]

    def __setitem__(self, key, value):
        self.held[key] = value

    def send(self):
        if not self.sent:
            self.copy.start()
            self.sent = True


class Whole:
    def __init__(self, held):
        self.held, self.shape = held, held.shape

    def ready(self):
        return self.held

    def send(self):
        pass

    def __getitem__(self, key):
        return self.held[key]

    def __setitem__(self, key, value):
        self.held[key] = value


def all_columns(entries):
    return [entry if isinstance(entry, tuple) else (entry, 0, entry.shape[1]) for entry in entries]


def call(body_fn, info, entries, shapes, scratch=()):
    entries = all_columns(entries)
    arrays = []
    for array, _, _ in entries:
        if all(array is not known for known in arrays):
            arrays.append(array)

    def kernel(info_ref, *refs):
        ins = []
        for array, first, last in entries:
            ref = next(r for r, known in zip(refs, arrays) if known is array)
            ins.append(Whole(ref.at[:, first:last] if last - first < array.shape[1] else ref))
        outs = refs[len(arrays) : len(arrays) + len(shapes)]
        body_fn(info_ref, *ins, *map(Whole, outs), *refs[len(arrays) + len(shapes) :])

    vmem = pl.BlockSpec(memory_space=pltpu.VMEM)
    return pl.pallas_call(
        kernel,
        out_shape=[jax.ShapeDtypeStruct(shape, dtype) for shape, dtype in shapes],
        in_specs=[pl.BlockSpec(memory_space=pltpu.SMEM)] + [vmem] * len(arrays),
        out_specs=[vmem] * len(shapes),
        scratch_shapes=list(scratch),
        compiler_params=kernel_params(),
        cost_estimate=cost(0, 0),
    )(info, *arrays)


def stream(body_fn, info, entries, shapes, scratch=()):
    entries = all_columns(entries)
    count, outs = len(entries), len(shapes)

    def kernel(info_ref, *refs):
        sources, targets = refs[:count], refs[count : count + outs]
        held = refs[count + outs : 2 * (count + outs)]
        sems = refs[2 * (count + outs)]
        rest = refs[2 * (count + outs) + 1 :]
        ins = []
        for i, (array, first, last) in enumerate(entries):
            source = sources[i]
            if last - first < array.shape[1]:
                source = source.at[:, first:last]
            ins.append(Source(held[i], pltpu.make_async_copy(source, held[i], sems.at[i])))
        gone = []
        for i in range(outs):
            copy = pltpu.make_async_copy(held[count + i], targets[i], sems.at[count + i])
            gone.append(Target(held[count + i], copy))
        body_fn(info_ref, *ins, *gone, *rest)
        for target in gone:
            target.send()
        for source in ins:
            source.ready()
        for target in gone:
            target.copy.wait()

    anywhere = pl.BlockSpec(memory_space=pl.ANY)
    return pl.pallas_call(
        kernel,
        out_shape=[jax.ShapeDtypeStruct(shape, dtype) for shape, dtype in shapes],
        in_specs=[pl.BlockSpec(memory_space=pltpu.SMEM)] + [anywhere] * count,
        out_specs=[anywhere] * outs,
        scratch_shapes=[
            pltpu.VMEM((array.shape[0], last - first), array.dtype)
            for array, first, last in entries
        ]
        + [pltpu.VMEM(shape, dtype) for shape, dtype in shapes]
        + [pltpu.SemaphoreType.DMA((count + outs,))]
        + list(scratch),
        compiler_params=kernel_params(),
        cost_estimate=cost(0, 0),
    )(info, *[array for array, _, _ in entries])


def dot(left_side, right_side):
    return jnp.dot(left_side, right_side, preferred_element_type=f32)


def norm_rows(state, gain_row):
    return (state * rms_scale(state) * gain_row).astype(bf16)


def self_kernel(
    width,
    modes,
    info,
    small,
    tokens,
    weight_own,
    weight_other,
    window,
    start,
    normed,
    qkv_own,
    qkv_other,
    attended_own,
    attended_other,
    rows,
):
    length = start.shape[0]
    rows[...] = small[...].astype(f32).T[:8]
    mode_row = jnp.zeros_like(rows[0:1, :])
    for m in range(modes):
        mode_row = mode_row + jnp.where(info[1] == m, rows[3 + m : 4 + m, :], 0.0)
    at = pl.ds(pl.multiple_of(info[0] * length, 16), length)
    start[...] = tokens[at, :].astype(f32) + mode_row
    normed[...] = norm_rows(start[...], rows[0:1, :])
    for target in (rows, start, normed):
        target.send()
    sides = ((weight_own, qkv_own, attended_own), (weight_other, qkv_other, attended_other))
    for side, (weight, qkv, attended) in enumerate(sides):
        for first in range(0, 3 * width, width):
            qkv[:, first : first + width] = dot(
                normed[...], weight[:, first : first + width]
            ).astype(bf16)
        qkv.send()
        attend(
            True,
            (0, width, 2 * width),
            info[2],
            window.ready(),
            side,
            (qkv.held,) * 3,
            attended.held,
        )
        attended.send()


def cross_kernel(
    width,
    info,
    attended_own,
    out_own,
    attended_other,
    out_other,
    start,
    rows,
    memory,
    kv_weight_own,
    q_weight_own,
    kv_weight_other,
    q_weight_other,
    after_self,
    normed,
    q_own,
    q_other,
    kv_own,
    kv_other,
    crossed_own,
    crossed_other,
):
    length = start.shape[0]
    part = dot_rows(attended_own[...], out_own[...])
    part = part + dot_rows(attended_other[...], out_other[...])
    after_self[...] = start[...] + part
    normed[...] = norm_rows(after_self[...], rows[1:2, :])
    after_self.send()
    normed.send()
    at = pl.ds(pl.multiple_of(info[0] * length, 16), length)
    sides = (
        (kv_weight_own, q_weight_own, q_own, kv_own, crossed_own),
        (kv_weight_other, q_weight_other, q_other, kv_other, crossed_other),
    )
    for side, (kv_weight, q_weight, q, kv, crossed) in enumerate(sides):
        kv[:, :width] = dot(memory[at, :], kv_weight[:, :width]).astype(bf16)
        kv[:, width:] = dot(memory[at, :], kv_weight[:, width:]).astype(bf16)
        q[...] = dot(normed[...], q_weight[...]).astype(bf16)
        q.send()
        kv.send()
        attend(
            False,
            (0, 0, width),
            info[3],
            None,
            side,
            (q.held, kv.held, kv.held),
            crossed.held,
        )
        crossed.send()


def ffn_kernel(
    info,
    crossed_own,
    out_own,
    crossed_other,
    out_other,
    after_self,
    rows,
    cot,
    gate_own,
    up_own,
    down_own,
    gate_other,
    up_other,
    down_other,
    after_cross,
    normed,
    hidden_own,
    hidden_other,
    grad_pre_own,
    grad_pre_other,
    output,
    total,
):
    hidden_width = hidden_own.shape[1]
    part = dot_rows(crossed_own[...], out_own[...])
    part = part + dot_rows(crossed_other[...], out_other[...])
    after_cross[...] = after_self[...] + part
    normed[...] = norm_rows(after_cross[...], rows[2:3, :])
    total[...] = after_cross[...]
    after_cross.send()
    normed.send()
    sides = (
        (gate_own, up_own, down_own, hidden_own, grad_pre_own),
        (gate_other, up_other, down_other, hidden_other, grad_pre_other),
    )
    for gate, up, down, hidden, grad_pre in sides:
        for first in range(0, hidden_width, 256):
            here = slice(first, first + 256)
            there = slice(hidden_width + first, hidden_width + first + 256)
            gate_pre = dot(normed[...], gate[:, here])
            up_pre = dot(normed[...], up[:, here])
            grad_hidden = dot(cot[...], down[:, here]).astype(bf16).astype(f32)
            square = gate_pre * gate_pre * 0.044715
            bend = jnp.tanh(0.7978845608028654 * (gate_pre + square * gate_pre))
            half_more = 0.5 * (1.0 + bend)
            gelu = gate_pre * half_more
            slope = half_more + 0.5 * gate_pre * (1.0 - bend * bend) * 0.7978845608028654 * (
                1.0 + 3.0 * square
            )
            low = (gelu * up_pre).astype(bf16)
            hidden[:, here] = low
            grad_pre[:, here] = (grad_hidden * up_pre * slope).astype(bf16)
            grad_pre[:, there] = (grad_hidden * gelu).astype(bf16)
            total[...] = total[...] + dot_rows(low, down[:, here])
        hidden.send()
        grad_pre.send()
    output[...] = total[...].astype(bf16)


def norm_back_rows(state, gain_row, grad_normed):
    scale = rms_scale(state)
    scaled = state * scale
    weighted = grad_normed * gain_row
    inner = jnp.mean(weighted * scaled, axis=-1, keepdims=True)
    return scale * (weighted - scaled * inner), jnp.sum(grad_normed * scaled, axis=0, keepdims=True)


def cross_back_kernel(
    width,
    info,
    grad_pre_own,
    gate_up_own,
    grad_pre_other,
    gate_up_other,
    after_cross,
    rows,
    cot,
    out_own,
    out_other,
    q_own,
    kv_own,
    q_other,
    kv_other,
    grad_state,
    branch,
    grad_q_own,
    grad_q_other,
    grad_kv_own,
    grad_kv_other,
    gains,
    grad_own,
    grad_other,
    key_sum,
    value_sum,
):
    grad_normed = dot_rows(grad_pre_own[...], gate_up_own[...])
    grad_normed = grad_normed + dot_rows(grad_pre_other[...], gate_up_other[...])
    part, gain = norm_back_rows(after_cross[...], rows[2:3, :], grad_normed)
    gains[...] = jnp.zeros_like(gains[...])
    gains[2:3, :] = gain
    grad_state[...] = cot[...].astype(f32) + part
    branch[...] = grad_state[...].astype(bf16)
    for target in (gains, grad_state, branch):
        target.send()
    sides = (
        (out_own, q_own, kv_own, grad_own, grad_q_own, grad_kv_own),
        (out_other, q_other, kv_other, grad_other, grad_q_other, grad_kv_other),
    )
    for side, (out, q, kv, grad, grad_q, grad_kv) in enumerate(sides):
        grad[...] = dot(branch[...], out[...]).astype(bf16)
        attend_back(
            False,
            (0, 0, width),
            info[3],
            None,
            side,
            (q.ready(), kv.ready(), kv.ready(), grad),
            grad_q.held,
            grad_kv.held,
            None,
            key_sum,
            value_sum,
        )
        grad_q.send()
        grad_kv.send()


def between_kernel(
    info,
    grad_q_own,
    q_weight_own,
    grad_q_other,
    q_weight_other,
    after_self,
    rows,
    grad_in,
    out_own,
    out_other,
    grad_kv_own,
    kv_weight_own,
    grad_kv_other,
    kv_weight_other,
    grad_state,
    branch,
    grad_own,
    grad_other,
    grad_memory,
    gains,
):
    grad_normed = dot_rows(grad_q_own[...], q_weight_own[...])
    grad_normed = grad_normed + dot_rows(grad_q_other[...], q_weight_other[...])
    part, gain = norm_back_rows(after_self[...], rows[1:2, :], grad_normed)
    gains[...] = jnp.zeros_like(gains[...])
    gains[1:2, :] = gain
    grad_state[...] = grad_in[...] + part
    branch[...] = grad_state[...].astype(bf16)
    for target in (gains, grad_state, branch):
        target.send()
    grad_own[...] = dot(branch[...], out_own[...]).astype(bf16)
    grad_own.send()
    grad_other[...] = dot(branch[...], out_other[...]).astype(bf16)
    grad_other.send()
    memory_part = dot_rows(grad_kv_own[...], kv_weight_own[...])
    grad_memory[...] = memory_part + dot_rows(grad_kv_other[...], kv_weight_other[...])


def self_back_kernel(
    width,
    info,
    window,
    qkv_own,
    grad_own,
    qkv_other,
    grad_other,
    grad_qkv_own,
    grad_qkv_other,
    sums,
    key_sum,
    value_sum,
):
    sides = ((qkv_own, grad_own, grad_qkv_own), (qkv_other, grad_other, grad_qkv_other))
    for side, (qkv, grad, grad_qkv) in enumerate(sides):
        attend_back(
            True,
            (0, width, 2 * width),
            info[2],
            window.ready(),
            side,
            (qkv.ready(),) * 3 + (grad.ready(),),
            grad_qkv.held,
            grad_qkv.held,
            sums.held,
            key_sum,
            value_sum,
        )
        grad_qkv.send()


def start_kernel(
    width,
    modes,
    info,
    grad_qkv_own,
    weight_own,
    grad_qkv_other,
    weight_other,
    start,
    rows,
    grad_in,
    sums,
    hot,
    gains_two,
    gains_three,
    grad_start,
    small,
):
    heads_here = width // 64
    grad_normed = dot_rows(grad_qkv_own[...], weight_own[...])
    grad_normed = grad_normed + dot_rows(grad_qkv_other[...], weight_other[...])
    part, gain = norm_back_rows(start[...], rows[0:1, :], grad_normed)
    grad_start[...] = grad_in[...] + part
    grad_start.send()
    small[...] = jnp.zeros_like(small[...])
    small[0:8, :] = gains_two[...] + gains_three[...]
    small[0:1, :] = gain
    total = jnp.sum(grad_start[...], axis=0, keepdims=True)
    for m in range(modes):
        small[3 + m : 4 + m, :] = jnp.where(info[1] == m, total, 0.0)
    table = lax.dot_general(
        sums[...], hot[...], (((1,), (1,)), ((), ())), precision=highest, preferred_element_type=f32
    )
    first, second = table[:heads_here], table[heads_here : 2 * heads_here]
    is_first = info[0] == 0
    small[8 : 8 + heads_here, : hot.shape[0]] = jnp.where(is_first, first, second)
    small[8 + heads_here : 8 + 2 * heads_here, : hot.shape[0]] = jnp.where(is_first, second, first)


def small_block(small, rows):
    depth = small.shape[1]
    turned = jnp.concatenate([small[:8], jnp.zeros((lanes - 8, depth), f32)], axis=0).T
    table = jnp.concatenate([small[8:24, :lanes], jnp.zeros((lanes - 16, lanes), f32)], axis=0).T
    lane = lax.broadcasted_iota(jnp.int32, (rows, lanes), 1)
    table = pltpu.roll(table[:rows], 8, 1)
    parts = [
        jnp.where(lane < 8, turned[at : at + rows], table) for at in range(0, depth, rows)
    ]
    return parts


def grad_tiles(counts, with_small, half):
    tiles, start = [], 0
    for i, count in enumerate(counts):
        for first in range(0, count, 512):
            stop = min(count, first + 512)
            cuts = [start + first, start + stop]
            if cuts[0] < half < cuts[1]:
                cuts.insert(1, half)
            for a, b in zip(cuts[:-1], cuts[1:]):
                tiles.append((i, a - start, b - start, a))
        start += count
    if with_small:
        tiles.append((len(counts), 0, lanes, start))
    return tiles


def grad_kernel(counts, with_small, info, *refs):
    total = 4 * len(counts) + (2 if with_small else 0)
    given, (left_ref, right_ref, mid_ref) = refs[:total], refs[total : total + 3]
    held, (quad, in_sems, out_sems) = refs[total + 3 : -3], refs[-3:]
    inputs = [
        Source(held[i], pltpu.make_async_copy(given[i], held[i], in_sems.at[i]))
        for i in range(total)
    ]
    high, rows = quad.shape[1], quad.shape[2]
    half = left_ref.shape[2]
    low = info[4]
    copies = []
    for n, (i, first, stop, at) in enumerate(grad_tiles(counts, with_small, half)):
        width = stop - first
        here = slice(at, at + width)
        if i < len(counts):
            left_own, left_other, right_own, right_other = inputs[4 * i : 4 * i + 4]
            part = matmul_left_t(left_own[...], right_own[:, first:stop])
            part = part + matmul_left_t(left_other[...], right_other[:, first:stop])
            part = part.astype(bf16)
            blocks = [part[k * rows : (k + 1) * rows] for k in range(4 * high)]
        else:
            small = inputs[-2][...] + inputs[-1][...]
            blocks = [block.astype(bf16) for block in small_block(small, rows)]
        for z in range(high):
            for l in range(4):
                quad[low ^ l, z, :, here] = blocks[4 * z + l]
        far_ref, far_at = (left_ref, at) if at < half else (right_ref, at - half)
        moves = (
            (quad.at[3, :, :, here], far_ref.at[:, :, far_at : far_at + width]),
            (quad.at[0:3, :, :, here], mid_ref.at[:, :, :, here]),
        )
        for j, (source, target) in enumerate(moves):
            copy = pltpu.make_async_copy(source, target, out_sems.at[2 * n + j])
            copy.start()
            copies.append(copy)
    for copy in copies:
        copy.wait()


def weight_grads(entries, info, groups, small=()):
    counts = [entry[2].shape[1] for entry in entries]
    width = sum(counts) + (lanes if small else 0)
    depth = entries[0][0].shape[1]
    length = entries[0][0].shape[0]
    if not stepwise(groups):
        parts = [
            matmul_left_t(
                jnp.concatenate([a, b], axis=0), jnp.concatenate([c, d], axis=0)
            ).astype(bf16)
            for a, b, c, d in entries
        ]
        if small:
            both = small[0] + small[1]
            table = jnp.pad(both[8:24, : depth // groups].T, ((0, 0), (0, lanes - 24)))
            block = jnp.concatenate([both[:8].T, jnp.tile(table, (groups, 1))], axis=1)
            parts.append(block.astype(bf16))
        return (jnp.concatenate(parts, axis=1),)
    high, rows = groups // 4, depth // groups
    arrays = [value for entry in entries for value in entry] + list(small)
    anywhere = pl.BlockSpec(memory_space=pl.ANY)
    half = width // 2 // lanes * lanes
    shapes = [(high, rows, half), (high, rows, width - half), (3, high, rows, width)]
    tiles = len(grad_tiles(counts, bool(small), half))
    return pl.pallas_call(
        functools.partial(grad_kernel, counts, bool(small)),
        out_shape=[jax.ShapeDtypeStruct(shape, bf16) for shape in shapes],
        in_specs=[pl.BlockSpec(memory_space=pltpu.SMEM)] + [anywhere] * len(arrays),
        out_specs=[anywhere] * 3,
        scratch_shapes=[pltpu.VMEM(array.shape, array.dtype) for array in arrays]
        + [
            pltpu.VMEM((4, high, rows, width), bf16),
            pltpu.SemaphoreType.DMA((len(arrays),)),
            pltpu.SemaphoreType.DMA((2 * tiles,)),
        ],
        compiler_params=kernel_params(),
        cost_estimate=cost(0, 0),
    )(info, *arrays)


def body(
    tokens,
    memory,
    cotangent,
    seq_modes,
    dec_lengths,
    enc_lengths,
    slot_plan,
    buckets,
    mode_table,
    gain_self,
    gain_cross,
    gain_ffn,
    bucket_table,
    self_query,
    self_key,
    self_value,
    self_output,
    cross_query,
    cross_key,
    cross_value,
    cross_output,
    ffn_gate,
    ffn_up,
    ffn_down,
):
    groups = lax.axis_size(dp_axes)
    group_id = lax.axis_index(dp_axes)
    half_id = lax.axis_index("heads")
    seq_total = slot_plan.shape[0]
    seq_len = buckets.shape[0]
    model_width = tokens.shape[1]
    shard_width = model_width // groups
    heads_here = bucket_table.shape[1]
    bucket_count = bucket_table.shape[0]
    modes = mode_table.shape[0]
    width = self_query.shape[1]
    hidden_width = ffn_gate.shape[1]
    own_seq = group_id * 2 + half_id

    small = jnp.concatenate([jnp.stack([gain_self, gain_cross, gain_ffn]), mode_table]).T
    small = jnp.pad(small, ((0, 0), (0, lanes - small.shape[1])))
    pack_one = jnp.concatenate([self_query, self_key, self_value, small], axis=1)
    pack_two = jnp.concatenate(
        [self_output.T, cross_query, cross_key, cross_value], axis=1
    )
    pack_three = jnp.concatenate([cross_output.T, ffn_gate, ffn_up, ffn_down.T], axis=1)

    seq_ids = jnp.arange(seq_total, dtype=jnp.int32)
    placed = (slot_plan[:, None] == seq_ids[None, :]).astype(jnp.int32)
    source_of = jnp.sum(placed * seq_ids[:, None], axis=0)
    chosen = (seq_ids == own_seq).astype(jnp.int32)
    facts = jnp.sum(jnp.stack([seq_modes, dec_lengths, enc_lengths]) * chosen[None, :], axis=1)
    info = jnp.concatenate(
        [half_id.reshape(1), facts, (group_id % 4).reshape(1), (group_id // 4).reshape(1)]
    ).astype(jnp.int32)

    table_rows = jnp.concatenate([bucket_table, swap_halves(bucket_table)], axis=1).T
    reach = seq_len - lanes
    hole = window_width - seq_len
    window_bucket = jnp.concatenate(
        [
            jnp.flip(buckets[: reach + 1]),
            jnp.full((hole,), -1, jnp.int32),
            jnp.flip(buckets[reach + 1 :]),
        ]
    )
    window_hot = (jnp.arange(bucket_count)[:, None] == window_bucket[None, :]).astype(bf16)
    window = matmul(table_rows, window_hot)
    window = jnp.where(window_bucket[None, :] < 0, masked_score, window)
    window = jnp.pad(window, ((0, 16 - 2 * heads_here), (0, 0)))

    def stacked(parts):
        return jnp.stack(parts) if stepwise(groups) else parts

    high_one = gather_high(pack_one, groups)
    high_one, pack_two, pack_three = pin(high_one, pack_two, pack_three)
    three_own = lax.all_gather(pack_three, dp_axes, axis=0, tiled=True)
    cot_pieces = sequence_pieces(cotangent, groups, half_id)
    stack_one = stacked(high_one)
    near_one = gather_near(stack_one, groups)
    high_two = gather_high(pack_two, groups)
    near_one, high_two, cot_pieces = pin(near_one, high_two, cot_pieces)
    far_one = gather_far(near_one, groups)
    cot_pieces = exchange(cot_pieces)
    stack_two = stacked(high_two)
    near_two = gather_near(stack_two, groups)
    one_own = gather_place(stack_one, near_one, far_one, groups, group_id)
    one_other = swap_halves(one_own)

    tall = (seq_len, model_width)
    gate_at, up_at, down_at = width, width + hidden_width, width + 2 * hidden_width
    (
        start_state,
        normed_one,
        qkv_own,
        qkv_other,
        attended_own,
        attended_other,
        rows,
    ) = call(
        functools.partial(self_kernel, width, modes),
        info,
        (
            (one_own, 3 * width, 3 * width + lanes),
            tokens,
            (one_own, 0, 3 * width),
            (one_other, 0, 3 * width),
            window,
        ),
        [(tall, f32), (tall, bf16)]
        + [((seq_len, 3 * width), bf16)] * 2
        + [((seq_len, width), bf16)] * 2
        + [((8, model_width), f32)],
    )
    near_two, attended_own, attended_other, cot_pieces = pin(
        near_two, attended_own, attended_other, cot_pieces
    )
    far_two = gather_far(near_two, groups)
    cot_pair = collect_pieces(ordered_pieces(cot_pieces, slot_plan, groups))
    two_own = gather_place(stack_two, near_two, far_two, groups, group_id)
    two_own, cot_pair = pin(two_own, cot_pair)
    two_other = swap_halves(two_own)
    cot_pair_other = swap_halves(cot_pair)
    (
        after_self,
        normed_two,
        q_own,
        q_other,
        kv_own,
        kv_other,
        crossed_own,
        crossed_other,
    ) = call(
        functools.partial(cross_kernel, width),
        info,
        (
            attended_own,
            (two_own, 0, width),
            attended_other,
            (two_other, 0, width),
            start_state,
            rows,
            memory,
            (two_own, 2 * width, 4 * width),
            (two_own, width, 2 * width),
            (two_other, 2 * width, 4 * width),
            (two_other, width, 2 * width),
        ),
        [(tall, f32), (tall, bf16)]
        + [((seq_len, width), bf16)] * 2
        + [((seq_len, 2 * width), bf16)] * 2
        + [((seq_len, width), bf16)] * 2,
    )
    crossed_own, crossed_other, three_own = pin(crossed_own, crossed_other, three_own)
    three_other = swap_halves(three_own)
    cot_whole = join_columns(cot_pair, cot_pair_other, half_id)
    cot_own = lax.dynamic_index_in_dim(cot_whole, half_id, 0, keepdims=False)
    cot_other = lax.dynamic_index_in_dim(cot_whole, 1 - half_id, 0, keepdims=False)
    (
        after_cross,
        normed_three,
        hidden_own,
        hidden_other,
        grad_pre_own,
        grad_pre_other,
        seq_output,
    ) = stream(
        ffn_kernel,
        info,
        (
            crossed_own,
            (three_own, 0, width),
            crossed_other,
            (three_other, 0, width),
            after_self,
            rows,
            cot_own,
            (three_own, gate_at, up_at),
            (three_own, up_at, down_at),
            (three_own, down_at, down_at + hidden_width),
            (three_other, gate_at, up_at),
            (three_other, up_at, down_at),
            (three_other, down_at, down_at + hidden_width),
        ),
        [(tall, f32), (tall, bf16)]
        + [((seq_len, hidden_width), bf16)] * 2
        + [((seq_len, 2 * hidden_width), bf16)] * 2
        + [(tall, bf16)],
        (pltpu.VMEM(tall, f32),),
    )

    other_memory = lax.dynamic_slice_in_dim(memory, (1 - half_id) * seq_len, seq_len, 0)
    own_memory = lax.dynamic_slice_in_dim(memory, half_id * seq_len, seq_len, 0)
    ffn_grad = weight_grads(
        (
            (normed_three, swap_halves(normed_three), grad_pre_own, swap_halves(grad_pre_other)),
            (cot_own, cot_other, hidden_own, swap_halves(hidden_other)),
        ),
        info,
        groups,
    )
    out_pieces = sequence_pieces(seq_output, groups, half_id)
    ffn_grad, grad_pre_own, grad_pre_other, out_pieces = pin(
        ffn_grad, grad_pre_own, grad_pre_other, out_pieces
    )
    ffn_far = scatter_far(ffn_grad, groups)
    out_pieces = exchange(out_pieces)
    sum_scratch = [pltpu.VMEM((seq_len, lanes), f32)] * 2
    (
        grad_after_cross,
        cross_branch,
        grad_q_own,
        grad_q_other,
        grad_kv_own,
        grad_kv_other,
        gains_three,
    ) = stream(
        functools.partial(cross_back_kernel, width),
        info,
        (
            grad_pre_own,
            (three_own, gate_at, down_at),
            grad_pre_other,
            (three_other, gate_at, down_at),
            after_cross,
            rows,
            cot_own,
            (three_own, 0, width),
            (three_other, 0, width),
            q_own,
            kv_own,
            q_other,
            kv_other,
        ),
        [(tall, f32), (tall, bf16)]
        + [((seq_len, width), bf16)] * 2
        + [((seq_len, 2 * width), bf16)] * 2
        + [((8, model_width), f32)],
        [pltpu.VMEM((seq_len, width), bf16)] * 2 + sum_scratch,
    )
    ffn_far, grad_after_cross, grad_q_own, grad_q_other, out_pieces = pin(
        ffn_far, grad_after_cross, grad_q_own, grad_q_other, out_pieces
    )
    ffn_sums = near_sums(ffn_grad, ffn_far, groups)
    out_mixed = ordered_pieces(out_pieces, source_of, groups)
    ffn_sums, out_mixed, grad_after_cross, grad_q_own, grad_q_other = pin(
        ffn_sums, out_mixed, grad_after_cross, grad_q_own, grad_q_other
    )
    ffn_near = scatter_near(ffn_sums, groups)
    out_pair = collect_pieces(out_mixed)
    (
        grad_after_self,
        self_branch,
        grad_att_own,
        grad_att_other,
        grad_memory,
        gains_two,
    ) = call(
        between_kernel,
        info,
        (
            grad_q_own,
            (two_own, width, 2 * width),
            grad_q_other,
            (two_other, width, 2 * width),
            after_self,
            rows,
            grad_after_cross,
            (two_own, 0, width),
            (two_other, 0, width),
            grad_kv_own,
            (two_own, 2 * width, 4 * width),
            grad_kv_other,
            (two_other, 2 * width, 4 * width),
        ),
        [(tall, f32), (tall, bf16)]
        + [((seq_len, width), bf16)] * 2
        + [(tall, f32), ((8, model_width), f32)],
    )
    cross_grad = weight_grads(
        (
            (normed_two, swap_halves(normed_two), grad_q_own, swap_halves(grad_q_other)),
            (own_memory, other_memory, grad_kv_own, swap_halves(grad_kv_other)),
            (cross_branch, swap_halves(cross_branch), crossed_own, swap_halves(crossed_other)),
            (self_branch, swap_halves(self_branch), attended_own, swap_halves(attended_other)),
        ),
        info,
        groups,
    )
    ffn_near, cross_grad, grad_att_own, grad_att_other, out_pair = pin(
        ffn_near, cross_grad, grad_att_own, grad_att_other, out_pair
    )
    cut = 3 * hidden_width // 2
    ffn_planes = plane_sums(ffn_grad, ffn_near, groups, 0, cut)
    more_planes = plane_sums(ffn_grad, ffn_near, groups, cut, 2 * cut)
    ffn_planes, more_planes, grad_att_own, grad_att_other = pin(
        ffn_planes, more_planes, grad_att_own, grad_att_other
    )
    cross_far = scatter_far(cross_grad, groups)
    ffn_high = scatter_planes(ffn_planes, groups)
    grad_qkv_own, grad_qkv_other, distance_sums = call(
        functools.partial(self_back_kernel, width),
        info,
        (
            window,
            qkv_own,
            grad_att_own,
            qkv_other,
            grad_att_other,
        ),
        [((seq_len, 3 * width), bf16)] * 2 + [(window.shape, f32)],
        sum_scratch,
    )
    cross_far, ffn_high, more_planes, grad_qkv_own, grad_qkv_other, grad_memory = pin(
        cross_far, ffn_high, more_planes, grad_qkv_own, grad_qkv_other, grad_memory
    )
    more_high = scatter_planes(more_planes, groups)
    cross_sums = near_sums(cross_grad, cross_far, groups)
    cross_sums, grad_qkv_own, grad_qkv_other = pin(cross_sums, grad_qkv_own, grad_qkv_other)
    cross_near = scatter_near(cross_sums, groups)
    grad_start, small = call(
        functools.partial(start_kernel, width, modes),
        info,
        (
            grad_qkv_own,
            (one_own, 0, 3 * width),
            grad_qkv_other,
            (one_other, 0, 3 * width),
            start_state,
            rows,
            grad_after_self,
            distance_sums,
            jnp.pad(window_hot.astype(f32), ((0, lanes - bucket_count), (0, 0))),
            gains_two,
            gains_three,
        ),
        [(tall, f32), ((24, model_width), f32)],
    )
    small_other = swap_halves(small)
    qkv_grad = weight_grads(
        ((normed_one, swap_halves(normed_one), grad_qkv_own, swap_halves(grad_qkv_other)),),
        info,
        groups,
        (small, small_other),
    )
    qkv_grad, more_high, cross_near, grad_start, grad_memory = pin(
        qkv_grad, more_high, cross_near, grad_start, grad_memory
    )
    qkv_far = scatter_far(qkv_grad, groups)
    cross_planes = plane_sums(cross_grad, cross_near, groups, 0, 5 * width)
    cross_high = scatter_planes(cross_planes, groups)
    memory_grad = both_sequences(grad_memory, swap_halves(grad_memory), half_id)
    out_mine = lax.dynamic_index_in_dim(out_pair, half_id, 0, keepdims=False)
    out_sent = lax.dynamic_index_in_dim(out_pair, 1 - half_id, 0, keepdims=False)
    layer_output = join_columns(out_mine, swap_halves(out_sent), half_id)
    qkv_far, memory_grad, grad_start = pin(qkv_far, memory_grad, grad_start)
    qkv_sums = near_sums(qkv_grad, qkv_far, groups)
    qkv_sums, grad_start = pin(qkv_sums, grad_start)
    qkv_near = scatter_near(qkv_sums, groups)
    tokens_grad = both_sequences(grad_start, swap_halves(grad_start), half_id)
    ffn_mine = jnp.concatenate(
        [jnp.sum(part.astype(f32), axis=0) for part in (ffn_high, more_high)], axis=1
    )
    qkv_near, tokens_grad, ffn_mine, layer_output = pin(
        qkv_near, tokens_grad, ffn_mine, layer_output
    )
    self_mine = scatter_sum(
        scatter_high(high_sums(qkv_grad, qkv_near, groups, group_id), groups)
    )
    cross_mine = jnp.sum(cross_high.astype(f32), axis=0)
    small_mine = self_mine[:, 3 * width :]
    mine = small_mine[:, :8].T
    if shard_width >= bucket_count:
        table_total = small_mine[:bucket_count, 8:24]
    else:
        table_total = lax.psum(small[8:24, :bucket_count] + small_other[8:24, :bucket_count], dp_axes).T
    table_mine = lax.dynamic_slice_in_dim(table_total, half_id * heads_here, heads_here, 1)
    return (
        layer_output,
        tokens_grad,
        memory_grad,
        mine[3 : 3 + modes],
        mine[0],
        mine[1],
        mine[2],
        table_mine,
        self_mine[:, :width],
        self_mine[:, width : 2 * width],
        self_mine[:, 2 * width : 3 * width],
        cross_mine[:, 4 * width :].T,
        cross_mine[:, :width],
        cross_mine[:, width : 2 * width],
        cross_mine[:, 2 * width : 3 * width],
        cross_mine[:, 3 * width : 4 * width].T,
        ffn_mine[:, :hidden_width],
        ffn_mine[:, hidden_width : 2 * hidden_width],
        ffn_mine[:, 2 * hidden_width :].T,
    )


def solution(mesh):
    groups, halves = mesh.shape["dp"], mesh.shape["heads"]
    low = 4 if groups % 4 == 0 else 1
    mesh = Mesh(mesh.devices.reshape(groups // low, low, halves), dp_axes + ("heads",))
    rows_dp = P(dp_axes, None)
    columns = P(dp_axes, "heads")
    rows_heads = P("heads", dp_axes)
    in_specs = (
        (rows_dp, rows_dp, P(dp_axes + ("heads",), None))
        + (P(),) * 5
        + (P(None, dp_axes), P(dp_axes), P(dp_axes), P(dp_axes), P(None, "heads"))
        + (columns, columns, columns, rows_heads) * 2
        + (columns, columns, rows_heads)
    )
    out_specs = (
        (P(dp_axes + ("heads",), None), rows_dp, rows_dp)
        + (P(None, dp_axes), P(dp_axes), P(dp_axes), P(dp_axes), P(None, "heads"))
        + (columns, columns, columns, rows_heads) * 2
        + (columns, columns, rows_heads)
    )
    return jax.shard_map(body, mesh=mesh, in_specs=in_specs, out_specs=out_specs, check_vma=False)
```

```python
import functools

import jax
import jax.numpy as jnp
from jax import lax
from jax.experimental import pallas as pl
from jax.experimental.pallas import tpu as pltpu
from jax.sharding import Mesh
from jax.sharding import PartitionSpec as P

norm_epsilon = 1e-06
masked_score = -1000000000.0
lanes = 128
window_width = 512
cross_height = 384
dp_axes = ("high", "low")
highest = lax.Precision.HIGHEST
bf16 = jnp.bfloat16
f32 = jnp.float32


def kernel_params(limit_mib=56):
    return pltpu.CompilerParams(vmem_limit_bytes=limit_mib * 1024 * 1024)


def cost(flops, moved, special=0):
    return pl.CostEstimate(flops=1000, bytes_accessed=1000, transcendentals=0)


def matmul(left_side, right_side):
    return jnp.dot(left_side, right_side, preferred_element_type=f32)


def matmul_left_t(left_side, right_side):
    return lax.dot_general(
        left_side, right_side, (((0,), (0,)), ((), ())), preferred_element_type=f32
    )


def matmul_right_t(left_side, right_side):
    return lax.dot_general(
        left_side, right_side, (((1,), (1,)), ((), ())), preferred_element_type=f32
    )


def rms_scale(hidden):
    return lax.rsqrt(jnp.mean(hidden * hidden, axis=-1, keepdims=True) + norm_epsilon)


def swap_halves(values):
    return lax.ppermute(values, "heads", [(0, 1), (1, 0)])


def flip_low(values, groups, bits):
    return lax.ppermute(values, dp_axes, [(i, i ^ bits) for i in range(groups)])


def shift_high(values, groups, step):
    high = groups // 4
    pairs = []
    for source in range(groups):
        z, low = source // 4, source % 4
        pairs.append((source, ((z - step) % high) * 4 + low))
    return lax.ppermute(values, dp_axes, pairs)


def stepwise(groups):
    return groups % 4 == 0 and 1 < groups // 4 <= 4


def place_kernel(order_ref, own_ref, x_ref, y_ref, left_ref, right_ref, out_ref, sems):
    high = own_ref.shape[0]
    half = left_ref.shape[2]
    z, low = order_ref[0], order_ref[1]
    copies = []
    for step in range(high):
        base = lax.rem(z + step, high) * 4
        moves = (
            (own_ref.at[step], out_ref.at[base + low]),
            (x_ref.at[step], out_ref.at[base + (low ^ 1)]),
            (y_ref.at[step], out_ref.at[base + (low ^ 2)]),
            (left_ref.at[step], out_ref.at[base + (low ^ 3), :, :half]),
            (right_ref.at[step], out_ref.at[base + (low ^ 3), :, half:]),
        )
        for i, (source, target) in enumerate(moves):
            copy = pltpu.make_async_copy(source, target, sems.at[5 * step + i])
            copy.start()
            copies.append(copy)
    for copy in copies:
        copy.wait()


def copy_call(body_fn, order, arrays, shape, copies):
    anywhere = pl.BlockSpec(memory_space=pl.ANY)
    return pl.pallas_call(
        body_fn,
        out_shape=jax.ShapeDtypeStruct(shape, arrays[0].dtype),
        in_specs=[pl.BlockSpec(memory_space=pltpu.SMEM)] + [anywhere] * len(arrays),
        out_specs=anywhere,
        scratch_shapes=[pltpu.SemaphoreType.DMA((copies,))],
        compiler_params=kernel_params(8),
        cost_estimate=cost(0, 0),
    )(order, *arrays)


def pin(*values):
    return lax.optimization_barrier(values)


def gather_high(shard, groups):
    if not stepwise(groups):
        return [shard]
    return [shard] + [shift_high(shard, groups, k) for k in range(1, groups // 4)]


def gather_near(stack, groups):
    if not stepwise(groups):
        return ()
    return flip_low(stack, groups, 1), flip_low(stack, groups, 2)


def gather_far(near, groups):
    if not stepwise(groups):
        return ()
    half = near[0].shape[2] // 2
    return (
        flip_low(near[0][:, :, :half], groups, 2),
        flip_low(near[1][:, :, half:], groups, 1),
    )


def gather_place(stack, near, far, groups, group_id):
    if not stepwise(groups):
        return lax.all_gather(stack[0], dp_axes, axis=0, tiled=True)
    rows, width = stack.shape[1:]
    order = jnp.stack([group_id // 4, group_id % 4]).astype(jnp.int32)
    arrays = (stack, *near, *far)
    placed = copy_call(place_kernel, order, arrays, (groups, rows, width), 5 * stack.shape[0])
    return placed.reshape(groups * rows, width)


def scatter_far(grad, groups):
    if not stepwise(groups):
        return ()
    return flip_low(grad[0], groups, 1), flip_low(grad[1], groups, 2)


def near_sums(grad, far, groups):
    if not stepwise(groups):
        return ()
    left, right = far
    with_right = jnp.concatenate([jnp.zeros_like(left), right], 2)
    with_left = jnp.concatenate([left, jnp.zeros_like(right)], 2)
    for_x = grad[2][1].astype(f32) + with_right.astype(f32)
    for_y = grad[2][2].astype(f32) + with_left.astype(f32)
    return for_x.astype(bf16), for_y.astype(bf16)


def scatter_near(sums, groups):
    if not stepwise(groups):
        return ()
    return flip_low(sums[0], groups, 1), flip_low(sums[1], groups, 2)


def high_sums(grad, near, groups, group_id):
    if not stepwise(groups):
        return grad
    high = groups // 4
    z = group_id // 4
    plane = grad[2][0].astype(f32) + near[0].astype(f32) + near[1].astype(f32)
    plane_low = plane.astype(bf16)
    return [lax.dynamic_index_in_dim(plane, z, 0, keepdims=False)] + [
        lax.dynamic_index_in_dim(plane_low, (z - k) % high, 0, keepdims=False)
        for k in range(1, high)
    ]


def scatter_high(sums, groups):
    if not stepwise(groups):
        return [lax.psum_scatter(sums[0], dp_axes, scatter_dimension=0, tiled=True).astype(f32)]
    return [sums[0]] + [shift_high(sums[k], groups, k) for k in range(1, groups // 4)]


def plane_sums(grad, near, groups, start, stop):
    if not stepwise(groups):
        return grad[0][:, start:stop]
    here = slice(start, stop)
    parts = (grad[2][0], near[0], near[1])
    return sum(part[:, :, here].astype(f32) for part in parts).astype(bf16)


def scatter_planes(planes, groups):
    if not stepwise(groups):
        return lax.psum_scatter(planes, dp_axes, scatter_dimension=0, tiled=True)[None]
    return lax.all_to_all(planes, "high", split_axis=0, concat_axis=0, tiled=True)


def scatter_sum(parts):
    return sum(part.astype(f32) for part in parts)


def reorder_kernel(order_ref, in_ref, out_ref):
    def one(i, carry):
        out_ref[i] = in_ref[order_ref[i]]
        return carry

    lax.fori_loop(0, out_ref.shape[0], one, 0)


def reorder(blocks, order):
    vmem = pl.BlockSpec(memory_space=pltpu.VMEM)
    return pl.pallas_call(
        reorder_kernel,
        out_shape=jax.ShapeDtypeStruct(blocks.shape, blocks.dtype),
        in_specs=[pl.BlockSpec(memory_space=pltpu.SMEM), vmem],
        out_specs=vmem,
        compiler_params=kernel_params(),
        cost_estimate=cost(0, 4 * blocks.size),
    )(order, blocks)


def both_kernel(half_ref, own_ref, other_ref, out_ref):
    half = half_ref[0]
    out_ref[half] = own_ref[...]
    out_ref[1 - half] = other_ref[...]


def both_sequences(own, other, half_id):
    vmem = pl.BlockSpec(memory_space=pltpu.VMEM)
    both = pl.pallas_call(
        both_kernel,
        out_shape=jax.ShapeDtypeStruct((2, *own.shape), own.dtype),
        in_specs=[pl.BlockSpec(memory_space=pltpu.SMEM), vmem, vmem],
        out_specs=vmem,
        compiler_params=kernel_params(),
        cost_estimate=cost(0, 0),
    )(half_id.reshape(1), own, other)
    return both.reshape(-1, own.shape[1])


def column_half(values, which):
    part = values.shape[-1] // 2
    return lax.dynamic_slice_in_dim(values, which * part, part, values.ndim - 1)


def sequence_pieces(rows, groups, half_id):
    length, width = rows.shape
    keep = column_half(rows, half_id)
    other = swap_halves(column_half(rows, 1 - half_id))
    first = half_id == 0
    pair = jnp.stack([jnp.where(first, keep, other), jnp.where(first, other, keep)])
    return pair.reshape(2, groups, length // groups, width // 2).transpose(1, 0, 2, 3)


def exchange(pieces):
    return lax.all_to_all(pieces, dp_axes, split_axis=0, concat_axis=0, tiled=True)


def ordered_pieces(pieces, order, groups):
    _, _, piece, part = pieces.shape
    mixed = reorder(pieces.reshape(2 * groups, piece, part), order)
    return mixed.reshape(groups, 2, piece, part)


def collect_pieces(mixed):
    groups, _, piece, part = mixed.shape
    return exchange(mixed).transpose(1, 0, 2, 3).reshape(2, groups * piece, part)


def join_columns(mine, theirs, half_id):
    first = half_id == 0
    return jnp.where(
        first, jnp.concatenate([mine, theirs], -1), jnp.concatenate([theirs, mine], -1)
    )


def dot_rows(left_side, right_side):
    return lax.dot_general(
        left_side, right_side, (((1,), (1,)), ((), ())), preferred_element_type=f32
    )


def head_lanes(values, which):
    lane = lax.broadcasted_iota(jnp.int32, values.shape, 1)
    keep = (lane < lanes // 2) if which == 0 else (lane >= lanes // 2)
    return jnp.where(keep, values, jnp.zeros_like(values))


def bias_blocks(window_ref, head):
    row = window_ref[pl.ds(head, 1), :]
    spread = jnp.broadcast_to(row, (lanes, window_width))
    return pltpu.roll(spread, 0, 1, stride=1, stride_axis=0)


def both_heads(values):
    return jnp.concatenate([head_lanes(values, 0), head_lanes(values, 1)], axis=0)


def join_heads(values):
    rows = values.shape[0] // 2
    lane = lax.broadcasted_iota(jnp.int32, (rows, lanes), 1)
    return jnp.where(lane < lanes // 2, values[:rows], values[rows:])


def masked_block(raw, biases, seq_len, length, first):
    height, count = raw.shape[0] // 2, raw.shape[1]
    if biases is not None:
        rows = []
        for bias in biases:
            for at in range(first, first + height, lanes):
                row = [bias[:, seq_len - lanes - at : seq_len]]
                if at + lanes < count:
                    row.append(jnp.full((lanes, count - at - lanes), masked_score, f32))
                rows.append(jnp.concatenate(row, axis=1))
        raw = raw + jnp.concatenate(rows, axis=0)
    column = lax.broadcasted_iota(jnp.int32, raw.shape, 1)
    return jnp.where(column < length, raw, masked_score)


def softmax_block(scores):
    exponent = jnp.exp(scores - jnp.max(scores, axis=1, keepdims=True))
    return exponent * (1.0 / jnp.sum(exponent, axis=1, keepdims=True))


def attend(causal, places, length, window_ref, side, inputs, out_ref):
    seq_len, width = out_ref.shape
    pairs = width // lanes
    height = lanes if causal else cross_height
    query_ref, key_ref, value_ref = inputs

    def one_pair(pair, carry):
        at = [pl.multiple_of(place + pair * lanes, lanes) for place in places]
        here = pl.ds(pl.multiple_of(pair * lanes, lanes), lanes)
        biases = None
        if causal:
            head = side * 2 * pairs + 2 * pair
            biases = [bias_blocks(window_ref, head + a) for a in range(2)]
        for first in range(0, seq_len, height):
            count = first + height if causal else seq_len
            query = both_heads(query_ref[first : first + height, pl.ds(at[0], lanes)])
            raw = dot_rows(query, key_ref[:count, pl.ds(at[1], lanes)])
            weights = softmax_block(masked_block(raw, biases, seq_len, length, first)).astype(bf16)
            blended = jnp.dot(
                weights, value_ref[:count, pl.ds(at[2], lanes)], preferred_element_type=f32
            )
            out_ref[first : first + height, here] = join_heads(blended).astype(bf16)
        return carry

    lax.fori_loop(0, pairs, one_pair, 0, unroll=True)


def diagonal_sums(block):
    rows, columns = block.shape
    wide = jnp.concatenate([block, jnp.zeros((rows, window_width - columns), f32)], axis=1)
    total = wide[0:8]
    for first in range(8, rows, 8):
        total = total + pltpu.roll(wide[first : first + 8], window_width - first, 1)
    row = lax.broadcasted_iota(jnp.int32, total.shape, 0)
    for bit in (1, 2, 4):
        total = jnp.where((row & bit) != 0, pltpu.roll(total, window_width - bit, 1), total)
    return jnp.sum(total, axis=0, keepdims=True)


def attend_back(
    causal, places, length, window_ref, side, inputs, query_out, key_out, sums_ref, key_sum, value_sum
):
    query_ref, key_ref, value_ref, grad_ref = inputs
    seq_len, width = grad_ref.shape
    pairs = width // lanes
    height = cross_height

    def one_pair(pair, carry):
        at = [pl.multiple_of(place + pair * lanes, lanes) for place in places]
        here = pl.ds(pl.multiple_of(pair * lanes, lanes), lanes)
        head = side * 2 * pairs + 2 * pair
        biases = None
        if causal:
            biases = [bias_blocks(window_ref, head + a) for a in range(2)]
        sums = [None, None]
        for first in reversed(range(0, seq_len, height)):
            count = first + height if causal else seq_len
            query = both_heads(query_ref[first : first + height, pl.ds(at[0], lanes)])
            grad = both_heads(grad_ref[first : first + height, here])
            key = key_ref[:count, pl.ds(at[1], lanes)]
            value = value_ref[:count, pl.ds(at[2], lanes)]
            raw = dot_rows(query, key)
            weights = softmax_block(masked_block(raw, biases, seq_len, length, first))
            grad_weights = dot_rows(grad, value)
            dots = jnp.sum(weights * grad_weights, axis=1, keepdims=True)
            grad_scores = (weights * (grad_weights - dots)).astype(bf16)
            grad_query = jnp.dot(grad_scores, key, preferred_element_type=f32)
            query_out[first : first + height, pl.ds(at[0], lanes)] = join_heads(grad_query).astype(
                bf16
            )
            key_part = matmul_left_t(grad_scores, query)
            value_part = matmul_left_t(weights.astype(bf16), grad)
            if causal:
                for a in range(2):
                    for inner in range(0, height, lanes):
                        row = first + inner
                        part = grad_scores[a * height + inner :][:lanes, : row + lanes].astype(f32)
                        start = seq_len - lanes - row
                        if sums[a] is None:
                            gap = [jnp.zeros((lanes, start), f32)] if start else []
                            sums[a] = jnp.concatenate(gap + [part], axis=1)
                        elif start == 0:
                            sums[a] = sums[a] + part
                        else:
                            sums[a] = jnp.concatenate(
                                [sums[a][:, :start], sums[a][:, start:] + part], axis=1
                            )
            if count == seq_len and first + height == seq_len:
                key_sum[...] = key_part
                value_sum[...] = value_part
            else:
                key_sum[:count] = key_sum[:count] + key_part
                value_sum[:count] = value_sum[:count] + value_part
        key_out[:, pl.ds(at[1], lanes)] = key_sum[...].astype(bf16)
        key_out[:, pl.ds(at[2], lanes)] = value_sum[...].astype(bf16)
        if causal:
            for a in range(2):
                sums_ref[pl.ds(head + a, 1), :] = diagonal_sums(sums[a])
        return carry

    lax.fori_loop(0, pairs, one_pair, 0, unroll=True)


class Source:
    def __init__(self, held, copy):
        self.held, self.copy, self.here = held, copy, False
        self.shape = held.shape
        copy.start()

    def ready(self):
        if not self.here:
            self.copy.wait()
            self.here = True
        return self.held

    def __getitem__(self, key):
        return self.ready()[key]


class Target:
    def __init__(self, held, copy):
        self.held, self.copy, self.sent = held, copy, False
        self.shape = held.shape

    def __getitem__(self, key):
        return self.held[key]

    def __setitem__(self, key, value):
        self.held[key] = value

    def send(self):
        if not self.sent:
            self.copy.start()
            self.sent = True


class Whole:
    def __init__(self, held):
        self.held, self.shape = held, held.shape

    def ready(self):
        return self.held

    def send(self):
        pass

    def __getitem__(self, key):
        return self.held[key]

    def __setitem__(self, key, value):
        self.held[key] = value


def all_columns(entries):
    return [entry if isinstance(entry, tuple) else (entry, 0, entry.shape[1]) for entry in entries]


def call(body_fn, info, entries, shapes, scratch=()):
    entries = all_columns(entries)
    arrays = []
    for array, _, _ in entries:
        if all(array is not known for known in arrays):
            arrays.append(array)

    def kernel(info_ref, *refs):
        ins = []
        for array, first, last in entries:
            ref = next(r for r, known in zip(refs, arrays) if known is array)
            ins.append(Whole(ref.at[:, first:last] if last - first < array.shape[1] else ref))
        outs = refs[len(arrays) : len(arrays) + len(shapes)]
        body_fn(info_ref, *ins, *map(Whole, outs), *refs[len(arrays) + len(shapes) :])

    vmem = pl.BlockSpec(memory_space=pltpu.VMEM)
    return pl.pallas_call(
        kernel,
        out_shape=[jax.ShapeDtypeStruct(shape, dtype) for shape, dtype in shapes],
        in_specs=[pl.BlockSpec(memory_space=pltpu.SMEM)] + [vmem] * len(arrays),
        out_specs=[vmem] * len(shapes),
        scratch_shapes=list(scratch),
        compiler_params=kernel_params(),
        cost_estimate=cost(0, 0),
    )(info, *arrays)


def stream(body_fn, info, entries, shapes, scratch=()):
    entries = all_columns(entries)
    count, outs = len(entries), len(shapes)
    plain = [a.size * a.dtype.itemsize < 1 << 20 and last - first == a.shape[1] for a, first, last in entries]

    def kernel(info_ref, *refs):
        sources, targets = refs[:count], refs[count : count + outs]
        held = refs[count + outs : 2 * (count + outs)]
        sems = refs[2 * (count + outs)]
        rest = refs[2 * (count + outs) + 1 :]
        ins = []
        for i, (array, first, last) in enumerate(entries):
            source = sources[i]
            if plain[i]:
                ins.append(Whole(source))
                continue
            if last - first < array.shape[1]:
                source = source.at[:, first:last]
            ins.append(Source(held[i], pltpu.make_async_copy(source, held[i], sems.at[i])))
        gone = []
        for i in range(outs):
            copy = pltpu.make_async_copy(held[count + i], targets[i], sems.at[count + i])
            gone.append(Target(held[count + i], copy))
        body_fn(info_ref, *ins, *gone, *rest)
        for target in gone:
            target.send()
        for source in ins:
            source.ready()
        for target in gone:
            target.copy.wait()

    anywhere = pl.BlockSpec(memory_space=pl.ANY)
    vmem = pl.BlockSpec(memory_space=pltpu.VMEM)
    return pl.pallas_call(
        kernel,
        out_shape=[jax.ShapeDtypeStruct(shape, dtype) for shape, dtype in shapes],
        in_specs=[pl.BlockSpec(memory_space=pltpu.SMEM)] + [vmem if p else anywhere for p in plain],
        out_specs=[anywhere] * outs,
        scratch_shapes=[
            pltpu.VMEM((8, lanes) if p else (array.shape[0], last - first), array.dtype)
            for p, (array, first, last) in zip(plain, entries)
        ]
        + [pltpu.VMEM(shape, dtype) for shape, dtype in shapes]
        + [pltpu.SemaphoreType.DMA((count + outs,))]
        + list(scratch),
        compiler_params=kernel_params(),
        cost_estimate=cost(0, 0),
    )(info, *[array for array, _, _ in entries])


def dot(left_side, right_side):
    return jnp.dot(left_side, right_side, preferred_element_type=f32)


def norm_rows(state, gain_row):
    return (state * rms_scale(state) * gain_row).astype(bf16)


def self_kernel(
    width,
    modes,
    info,
    small,
    tokens,
    weight_own,
    weight_other,
    window,
    start,
    normed,
    qkv_own,
    qkv_other,
    attended_own,
    attended_other,
    rows,
):
    length = start.shape[0]
    rows[...] = small[...].astype(f32).T[:8]
    mode_row = jnp.zeros_like(rows[0:1, :])
    for m in range(modes):
        mode_row = mode_row + jnp.where(info[1] == m, rows[3 + m : 4 + m, :], 0.0)
    at = pl.ds(pl.multiple_of(info[0] * length, 16), length)
    start[...] = tokens[at, :].astype(f32) + mode_row
    normed[...] = norm_rows(start[...], rows[0:1, :])
    for target in (rows, start, normed):
        target.send()
    sides = ((weight_own, qkv_own, attended_own), (weight_other, qkv_other, attended_other))
    for side, (weight, qkv, attended) in enumerate(sides):
        for first in range(0, 3 * width, width):
            qkv[:, first : first + width] = dot(
                normed[...], weight[:, first : first + width]
            ).astype(bf16)
        qkv.send()
        attend(
            True,
            (0, width, 2 * width),
            info[2],
            window.ready(),
            side,
            (qkv.held,) * 3,
            attended.held,
        )
        attended.send()


def cross_kernel(
    width,
    info,
    attended_own,
    out_own,
    attended_other,
    out_other,
    start,
    rows,
    memory,
    kv_weight_own,
    q_weight_own,
    kv_weight_other,
    q_weight_other,
    after_self,
    normed,
    q_own,
    q_other,
    kv_own,
    kv_other,
    crossed_own,
    crossed_other,
):
    length = start.shape[0]
    part = dot_rows(attended_own[...], out_own[...])
    part = part + dot_rows(attended_other[...], out_other[...])
    after_self[...] = start[...] + part
    normed[...] = norm_rows(after_self[...], rows[1:2, :])
    after_self.send()
    normed.send()
    at = pl.ds(pl.multiple_of(info[0] * length, 16), length)
    sides = (
        (kv_weight_own, q_weight_own, q_own, kv_own, crossed_own),
        (kv_weight_other, q_weight_other, q_other, kv_other, crossed_other),
    )
    for side, (kv_weight, q_weight, q, kv, crossed) in enumerate(sides):
        kv[:, :width] = dot(memory[at, :], kv_weight[:, :width]).astype(bf16)
        kv[:, width:] = dot(memory[at, :], kv_weight[:, width:]).astype(bf16)
        q[...] = dot(normed[...], q_weight[...]).astype(bf16)
        q.send()
        kv.send()
        attend(
            False,
            (0, 0, width),
            info[3],
            None,
            side,
            (q.held, kv.held, kv.held),
            crossed.held,
        )
        crossed.send()


def ffn_kernel(
    info,
    crossed_own,
    out_own,
    crossed_other,
    out_other,
    after_self,
    rows,
    cot,
    gate_own,
    up_own,
    down_own,
    gate_other,
    up_other,
    down_other,
    after_cross,
    normed,
    hidden_own,
    hidden_other,
    grad_pre_own,
    grad_pre_other,
    output,
    total,
):
    hidden_width = hidden_own.shape[1]
    part = dot_rows(crossed_own[...], out_own[...])
    part = part + dot_rows(crossed_other[...], out_other[...])
    after_cross[...] = after_self[...] + part
    normed[...] = norm_rows(after_cross[...], rows[2:3, :])
    total[...] = after_cross[...]
    after_cross.send()
    normed.send()
    sides = (
        (gate_own, up_own, down_own, hidden_own, grad_pre_own),
        (gate_other, up_other, down_other, hidden_other, grad_pre_other),
    )
    for gate, up, down, hidden, grad_pre in sides:
        for first in range(0, hidden_width, 256):
            here = slice(first, first + 256)
            there = slice(hidden_width + first, hidden_width + first + 256)
            gate_pre = dot(normed[...], gate[:, here])
            up_pre = dot(normed[...], up[:, here])
            grad_hidden = dot(cot[...], down[:, here]).astype(bf16).astype(f32)
            square = gate_pre * gate_pre * 0.044715
            bend = jnp.tanh(0.7978845608028654 * (gate_pre + square * gate_pre))
            half_more = 0.5 * (1.0 + bend)
            gelu = gate_pre * half_more
            slope = half_more + 0.5 * gate_pre * (1.0 - bend * bend) * 0.7978845608028654 * (
                1.0 + 3.0 * square
            )
            low = (gelu * up_pre).astype(bf16)
            hidden[:, here] = low
            grad_pre[:, here] = (grad_hidden * up_pre * slope).astype(bf16)
            grad_pre[:, there] = (grad_hidden * gelu).astype(bf16)
            total[...] = total[...] + dot_rows(low, down[:, here])
        hidden.send()
        grad_pre.send()
    output[...] = total[...].astype(bf16)


def norm_back_rows(state, gain_row, grad_normed):
    scale = rms_scale(state)
    scaled = state * scale
    weighted = grad_normed * gain_row
    inner = jnp.mean(weighted * scaled, axis=-1, keepdims=True)
    return scale * (weighted - scaled * inner), jnp.sum(grad_normed * scaled, axis=0, keepdims=True)


def ffn_back_kernel(
    info,
    grad_pre_own,
    gate_up_own,
    grad_pre_other,
    gate_up_other,
    after_cross,
    rows,
    cot,
    out_own,
    out_other,
    grad_state,
    branch,
    grad_own,
    grad_other,
    gains,
):
    grad_normed = dot_rows(grad_pre_own[...], gate_up_own[...])
    grad_normed = grad_normed + dot_rows(grad_pre_other[...], gate_up_other[...])
    part, gain = norm_back_rows(after_cross[...], rows[2:3, :], grad_normed)
    gains[...] = jnp.zeros_like(gains[...])
    gains[2:3, :] = gain
    grad_state[...] = cot[...].astype(f32) + part
    branch[...] = grad_state[...].astype(bf16)
    for target in (gains, grad_state, branch):
        target.send()
    grad_own[...] = dot(branch[...], out_own[...]).astype(bf16)
    grad_other[...] = dot(branch[...], out_other[...]).astype(bf16)


def cross_back_kernel(
    width,
    info,
    q_own,
    kv_own,
    grad_own,
    q_other,
    kv_other,
    grad_other,
    grad_q_own,
    grad_q_other,
    grad_kv_own,
    grad_kv_other,
    key_sum,
    value_sum,
):
    sides = (
        (q_own, kv_own, grad_own, grad_q_own, grad_kv_own),
        (q_other, kv_other, grad_other, grad_q_other, grad_kv_other),
    )
    for side, (q, kv, grad, grad_q, grad_kv) in enumerate(sides):
        attend_back(
            False,
            (0, 0, width),
            info[3],
            None,
            side,
            (q.ready(), kv.ready(), kv.ready(), grad.ready()),
            grad_q.held,
            grad_kv.held,
            None,
            key_sum,
            value_sum,
        )


def between_kernel(
    info,
    grad_q_own,
    q_weight_own,
    grad_q_other,
    q_weight_other,
    after_self,
    rows,
    grad_in,
    out_own,
    out_other,
    grad_kv_own,
    kv_weight_own,
    grad_kv_other,
    kv_weight_other,
    grad_state,
    branch,
    grad_own,
    grad_other,
    grad_memory,
    gains,
):
    grad_normed = dot_rows(grad_q_own[...], q_weight_own[...])
    grad_normed = grad_normed + dot_rows(grad_q_other[...], q_weight_other[...])
    part, gain = norm_back_rows(after_self[...], rows[1:2, :], grad_normed)
    gains[...] = jnp.zeros_like(gains[...])
    gains[1:2, :] = gain
    grad_state[...] = grad_in[...] + part
    branch[...] = grad_state[...].astype(bf16)
    for target in (gains, grad_state, branch):
        target.send()
    grad_own[...] = dot(branch[...], out_own[...]).astype(bf16)
    grad_own.send()
    grad_other[...] = dot(branch[...], out_other[...]).astype(bf16)
    grad_other.send()
    memory_part = dot_rows(grad_kv_own[...], kv_weight_own[...])
    grad_memory[...] = memory_part + dot_rows(grad_kv_other[...], kv_weight_other[...])


def self_back_kernel(
    width,
    info,
    window,
    qkv_own,
    grad_own,
    qkv_other,
    grad_other,
    grad_qkv_own,
    grad_qkv_other,
    sums,
    key_sum,
    value_sum,
):
    sides = ((qkv_own, grad_own, grad_qkv_own), (qkv_other, grad_other, grad_qkv_other))
    for side, (qkv, grad, grad_qkv) in enumerate(sides):
        attend_back(
            True,
            (0, width, 2 * width),
            info[2],
            window.ready(),
            side,
            (qkv.ready(),) * 3 + (grad.ready(),),
            grad_qkv.held,
            grad_qkv.held,
            sums.held,
            key_sum,
            value_sum,
        )
        grad_qkv.send()


def start_kernel(
    width,
    modes,
    info,
    grad_qkv_own,
    weight_own,
    grad_qkv_other,
    weight_other,
    start,
    rows,
    grad_in,
    sums,
    hot,
    gains_two,
    gains_three,
    grad_start,
    small,
):
    heads_here = width // 64
    grad_normed = dot_rows(grad_qkv_own[...], weight_own[...])
    grad_normed = grad_normed + dot_rows(grad_qkv_other[...], weight_other[...])
    part, gain = norm_back_rows(start[...], rows[0:1, :], grad_normed)
    grad_start[...] = grad_in[...] + part
    grad_start.send()
    small[...] = jnp.zeros_like(small[...])
    small[0:8, :] = gains_two[...] + gains_three[...]
    small[0:1, :] = gain
    total = jnp.sum(grad_start[...], axis=0, keepdims=True)
    for m in range(modes):
        small[3 + m : 4 + m, :] = jnp.where(info[1] == m, total, 0.0)
    table = lax.dot_general(
        sums[...], hot[...], (((1,), (1,)), ((), ())), precision=highest, preferred_element_type=f32
    )
    first, second = table[:heads_here], table[heads_here : 2 * heads_here]
    is_first = info[0] == 0
    small[8 : 8 + heads_here, : hot.shape[0]] = jnp.where(is_first, first, second)
    small[8 + heads_here : 8 + 2 * heads_here, : hot.shape[0]] = jnp.where(is_first, second, first)


def small_block(small, rows):
    depth = small.shape[1]
    turned = jnp.concatenate([small[:8], jnp.zeros((lanes - 8, depth), f32)], axis=0).T
    table = jnp.concatenate([small[8:24, :lanes], jnp.zeros((lanes - 16, lanes), f32)], axis=0).T
    lane = lax.broadcasted_iota(jnp.int32, (rows, lanes), 1)
    table = pltpu.roll(table[:rows], 8, 1)
    parts = [
        jnp.where(lane < 8, turned[at : at + rows], table) for at in range(0, depth, rows)
    ]
    return parts


def grad_tiles(counts, with_small, half):
    tiles, start = [], 0
    for i, count in enumerate(counts):
        for first in range(0, count, 512):
            stop = min(count, first + 512)
            cuts = [start + first, start + stop]
            if cuts[0] < half < cuts[1]:
                cuts.insert(1, half)
            for a, b in zip(cuts[:-1], cuts[1:]):
                tiles.append((i, a - start, b - start, a))
        start += count
    if with_small:
        tiles.append((len(counts), 0, lanes, start))
    return tiles


def grad_kernel(counts, with_small, info, *refs):
    total = 4 * len(counts) + (2 if with_small else 0)
    given, (left_ref, right_ref, mid_ref) = refs[:total], refs[total : total + 3]
    held, (quad, in_sems, out_sems) = refs[total + 3 : -3], refs[-3:]
    inputs = [
        Source(held[i], pltpu.make_async_copy(given[i], held[i], in_sems.at[i]))
        for i in range(total)
    ]
    high, rows = quad.shape[1], quad.shape[2]
    half = left_ref.shape[2]
    low = info[4]
    copies = []
    for n, (i, first, stop, at) in enumerate(grad_tiles(counts, with_small, half)):
        width = stop - first
        here = slice(at, at + width)
        if i < len(counts):
            left_own, left_other, right_own, right_other = inputs[4 * i : 4 * i + 4]
            part = matmul_left_t(left_own[...], right_own[:, first:stop])
            part = part + matmul_left_t(left_other[...], right_other[:, first:stop])
            part = part.astype(bf16)
            blocks = [part[k * rows : (k + 1) * rows] for k in range(4 * high)]
        else:
            small = inputs[-2][...] + inputs[-1][...]
            blocks = [block.astype(bf16) for block in small_block(small, rows)]
        for z in range(high):
            for l in range(4):
                quad[low ^ l, z, :, here] = blocks[4 * z + l]
        far_ref, far_at = (left_ref, at) if at < half else (right_ref, at - half)
        moves = (
            (quad.at[3, :, :, here], far_ref.at[:, :, far_at : far_at + width]),
            (quad.at[0:3, :, :, here], mid_ref.at[:, :, :, here]),
        )
        for j, (source, target) in enumerate(moves):
            copy = pltpu.make_async_copy(source, target, out_sems.at[2 * n + j])
            copy.start()
            copies.append(copy)
    for copy in copies:
        copy.wait()


def weight_grads(entries, info, groups, small=()):
    counts = [entry[2].shape[1] for entry in entries]
    width = sum(counts) + (lanes if small else 0)
    depth = entries[0][0].shape[1]
    length = entries[0][0].shape[0]
    if not stepwise(groups):
        parts = [
            matmul_left_t(
                jnp.concatenate([a, b], axis=0), jnp.concatenate([c, d], axis=0)
            ).astype(bf16)
            for a, b, c, d in entries
        ]
        if small:
            both = small[0] + small[1]
            table = jnp.pad(both[8:24, : depth // groups].T, ((0, 0), (0, lanes - 24)))
            block = jnp.concatenate([both[:8].T, jnp.tile(table, (groups, 1))], axis=1)
            parts.append(block.astype(bf16))
        return (jnp.concatenate(parts, axis=1),)
    high, rows = groups // 4, depth // groups
    arrays = [value for entry in entries for value in entry] + list(small)
    anywhere = pl.BlockSpec(memory_space=pl.ANY)
    half = width // 2 // lanes * lanes
    shapes = [(high, rows, half), (high, rows, width - half), (3, high, rows, width)]
    tiles = len(grad_tiles(counts, bool(small), half))
    return pl.pallas_call(
        functools.partial(grad_kernel, counts, bool(small)),
        out_shape=[jax.ShapeDtypeStruct(shape, bf16) for shape in shapes],
        in_specs=[pl.BlockSpec(memory_space=pltpu.SMEM)] + [anywhere] * len(arrays),
        out_specs=[anywhere] * 3,
        scratch_shapes=[pltpu.VMEM(array.shape, array.dtype) for array in arrays]
        + [
            pltpu.VMEM((4, high, rows, width), bf16),
            pltpu.SemaphoreType.DMA((len(arrays),)),
            pltpu.SemaphoreType.DMA((2 * tiles,)),
        ],
        compiler_params=kernel_params(),
        cost_estimate=cost(0, 0),
    )(info, *arrays)


def body(
    tokens,
    memory,
    cotangent,
    seq_modes,
    dec_lengths,
    enc_lengths,
    slot_plan,
    buckets,
    mode_table,
    gain_self,
    gain_cross,
    gain_ffn,
    bucket_table,
    self_query,
    self_key,
    self_value,
    self_output,
    cross_query,
    cross_key,
    cross_value,
    cross_output,
    ffn_gate,
    ffn_up,
    ffn_down,
):
    groups = lax.axis_size(dp_axes)
    group_id = lax.axis_index(dp_axes)
    half_id = lax.axis_index("heads")
    seq_total = slot_plan.shape[0]
    seq_len = buckets.shape[0]
    model_width = tokens.shape[1]
    shard_width = model_width // groups
    heads_here = bucket_table.shape[1]
    bucket_count = bucket_table.shape[0]
    modes = mode_table.shape[0]
    width = self_query.shape[1]
    hidden_width = ffn_gate.shape[1]
    own_seq = group_id * 2 + half_id

    small = jnp.concatenate([jnp.stack([gain_self, gain_cross, gain_ffn]), mode_table]).T
    small = jnp.pad(small, ((0, 0), (0, lanes - small.shape[1])))
    pack_one = jnp.concatenate([self_query, self_key, self_value, small], axis=1)
    pack_two = jnp.concatenate(
        [self_output.T, cross_query, cross_key, cross_value], axis=1
    )
    pack_three = jnp.concatenate([cross_output.T, ffn_gate, ffn_up, ffn_down.T], axis=1)

    seq_ids = jnp.arange(seq_total, dtype=jnp.int32)
    placed = (slot_plan[:, None] == seq_ids[None, :]).astype(jnp.int32)
    source_of = jnp.sum(placed * seq_ids[:, None], axis=0)
    chosen = (seq_ids == own_seq).astype(jnp.int32)
    facts = jnp.sum(jnp.stack([seq_modes, dec_lengths, enc_lengths]) * chosen[None, :], axis=1)
    info = jnp.concatenate(
        [half_id.reshape(1), facts, (group_id % 4).reshape(1), (group_id // 4).reshape(1)]
    ).astype(jnp.int32)

    table_rows = jnp.concatenate([bucket_table, swap_halves(bucket_table)], axis=1).T
    reach = seq_len - lanes
    hole = window_width - seq_len
    window_bucket = jnp.concatenate(
        [
            jnp.flip(buckets[: reach + 1]),
            jnp.full((hole,), -1, jnp.int32),
            jnp.flip(buckets[reach + 1 :]),
        ]
    )
    window_hot = (jnp.arange(bucket_count)[:, None] == window_bucket[None, :]).astype(bf16)
    window = matmul(table_rows, window_hot)
    window = jnp.where(window_bucket[None, :] < 0, masked_score, window)
    window = jnp.pad(window, ((0, 16 - 2 * heads_here), (0, 0)))

    def stacked(parts):
        return jnp.stack(parts) if stepwise(groups) else parts

    high_one = gather_high(pack_one, groups)
    high_one, pack_two, pack_three = pin(high_one, pack_two, pack_three)
    three_own = lax.all_gather(pack_three, dp_axes, axis=0, tiled=True)
    cot_pieces = sequence_pieces(cotangent, groups, half_id)
    stack_one = stacked(high_one)
    near_one = gather_near(stack_one, groups)
    high_two = gather_high(pack_two, groups)
    near_one, high_two, cot_pieces = pin(near_one, high_two, cot_pieces)
    far_one = gather_far(near_one, groups)
    cot_pieces = exchange(cot_pieces)
    stack_two = stacked(high_two)
    near_two = gather_near(stack_two, groups)
    one_own = gather_place(stack_one, near_one, far_one, groups, group_id)
    one_other = swap_halves(one_own)

    tall = (seq_len, model_width)
    gate_at, up_at, down_at = width, width + hidden_width, width + 2 * hidden_width
    (
        start_state,
        normed_one,
        qkv_own,
        qkv_other,
        attended_own,
        attended_other,
        rows,
    ) = call(
        functools.partial(self_kernel, width, modes),
        info,
        (
            (one_own, 3 * width, 3 * width + lanes),
            tokens,
            (one_own, 0, 3 * width),
            (one_other, 0, 3 * width),
            window,
        ),
        [(tall, f32), (tall, bf16)]
        + [((seq_len, 3 * width), bf16)] * 2
        + [((seq_len, width), bf16)] * 2
        + [((8, model_width), f32)],
    )
    near_two, attended_own, attended_other, cot_pieces = pin(
        near_two, attended_own, attended_other, cot_pieces
    )
    far_two = gather_far(near_two, groups)
    cot_pair = collect_pieces(ordered_pieces(cot_pieces, slot_plan, groups))
    two_own = gather_place(stack_two, near_two, far_two, groups, group_id)
    other_memory = lax.dynamic_slice_in_dim(memory, (1 - half_id) * seq_len, seq_len, 0)
    own_memory = lax.dynamic_slice_in_dim(memory, half_id * seq_len, seq_len, 0)
    wide_hot = jnp.pad(window_hot.astype(f32), ((0, lanes - bucket_count), (0, 0)))
    two_own, cot_pair, other_memory, own_memory, wide_hot, source_of = pin(
        two_own, cot_pair, other_memory, own_memory, wide_hot, source_of
    )
    two_other = swap_halves(two_own)
    cot_pair_other = swap_halves(cot_pair)
    (
        after_self,
        normed_two,
        q_own,
        q_other,
        kv_own,
        kv_other,
        crossed_own,
        crossed_other,
    ) = call(
        functools.partial(cross_kernel, width),
        info,
        (
            attended_own,
            (two_own, 0, width),
            attended_other,
            (two_other, 0, width),
            start_state,
            rows,
            memory,
            (two_own, 2 * width, 4 * width),
            (two_own, width, 2 * width),
            (two_other, 2 * width, 4 * width),
            (two_other, width, 2 * width),
        ),
        [(tall, f32), (tall, bf16)]
        + [((seq_len, width), bf16)] * 2
        + [((seq_len, 2 * width), bf16)] * 2
        + [((seq_len, width), bf16)] * 2,
    )
    crossed_own, crossed_other, three_own = pin(crossed_own, crossed_other, three_own)
    three_other = swap_halves(three_own)
    cot_whole = join_columns(cot_pair, cot_pair_other, half_id)
    cot_own = lax.dynamic_index_in_dim(cot_whole, half_id, 0, keepdims=False)
    cot_other = lax.dynamic_index_in_dim(cot_whole, 1 - half_id, 0, keepdims=False)
    (
        after_cross,
        normed_three,
        hidden_own,
        hidden_other,
        grad_pre_own,
        grad_pre_other,
        seq_output,
    ) = call(
        ffn_kernel,
        info,
        (
            crossed_own,
            (three_own, 0, width),
            crossed_other,
            (three_other, 0, width),
            after_self,
            rows,
            cot_own,
            (three_own, gate_at, up_at),
            (three_own, up_at, down_at),
            (three_own, down_at, down_at + hidden_width),
            (three_other, gate_at, up_at),
            (three_other, up_at, down_at),
            (three_other, down_at, down_at + hidden_width),
        ),
        [(tall, f32), (tall, bf16)]
        + [((seq_len, hidden_width), bf16)] * 2
        + [((seq_len, 2 * hidden_width), bf16)] * 2
        + [(tall, bf16)],
        (pltpu.VMEM(tall, f32),),
    )

    ffn_grad = weight_grads(
        (
            (normed_three, swap_halves(normed_three), grad_pre_own, swap_halves(grad_pre_other)),
            (cot_own, cot_other, hidden_own, swap_halves(hidden_other)),
        ),
        info,
        groups,
    )
    out_pieces = sequence_pieces(seq_output, groups, half_id)
    ffn_grad, grad_pre_own, grad_pre_other, out_pieces = pin(
        ffn_grad, grad_pre_own, grad_pre_other, out_pieces
    )
    ffn_far = scatter_far(ffn_grad, groups)
    sum_scratch = [pltpu.VMEM((seq_len, lanes), f32)] * 2
    grad_after_cross, cross_branch, grad_crossed_own, grad_crossed_other, gains_three = stream(
        ffn_back_kernel,
        info,
        (
            grad_pre_own,
            (three_own, gate_at, down_at),
            grad_pre_other,
            (three_other, gate_at, down_at),
            after_cross,
            rows,
            cot_own,
            (three_own, 0, width),
            (three_other, 0, width),
        ),
        [(tall, f32), (tall, bf16)]
        + [((seq_len, width), bf16)] * 2
        + [((8, model_width), f32)],
    )
    ffn_far, grad_crossed_own, grad_crossed_other, out_pieces = pin(
        ffn_far, grad_crossed_own, grad_crossed_other, out_pieces
    )
    ffn_sums = near_sums(ffn_grad, ffn_far, groups)
    out_pieces = exchange(out_pieces)
    ffn_sums, grad_crossed_own, grad_crossed_other = pin(
        ffn_sums, grad_crossed_own, grad_crossed_other
    )
    ffn_near = scatter_near(ffn_sums, groups)
    grad_q_own, grad_q_other, grad_kv_own, grad_kv_other = call(
        functools.partial(cross_back_kernel, width),
        info,
        (q_own, kv_own, grad_crossed_own, q_other, kv_other, grad_crossed_other),
        [((seq_len, width), bf16)] * 2 + [((seq_len, 2 * width), bf16)] * 2,
        sum_scratch,
    )
    out_pieces, grad_q_own, grad_q_other = pin(out_pieces, grad_q_own, grad_q_other)
    out_mixed = ordered_pieces(out_pieces, source_of, groups)
    out_pair = collect_pieces(out_mixed)
    (
        grad_after_self,
        self_branch,
        grad_att_own,
        grad_att_other,
        grad_memory,
        gains_two,
    ) = call(
        between_kernel,
        info,
        (
            grad_q_own,
            (two_own, width, 2 * width),
            grad_q_other,
            (two_other, width, 2 * width),
            after_self,
            rows,
            grad_after_cross,
            (two_own, 0, width),
            (two_other, 0, width),
            grad_kv_own,
            (two_own, 2 * width, 4 * width),
            grad_kv_other,
            (two_other, 2 * width, 4 * width),
        ),
        [(tall, f32), (tall, bf16)]
        + [((seq_len, width), bf16)] * 2
        + [(tall, f32), ((8, model_width), f32)],
    )
    cross_grad = weight_grads(
        (
            (normed_two, swap_halves(normed_two), grad_q_own, swap_halves(grad_q_other)),
            (own_memory, other_memory, grad_kv_own, swap_halves(grad_kv_other)),
            (cross_branch, swap_halves(cross_branch), crossed_own, swap_halves(crossed_other)),
            (self_branch, swap_halves(self_branch), attended_own, swap_halves(attended_other)),
        ),
        info,
        groups,
    )
    ffn_near, cross_grad, grad_att_own, grad_att_other, out_pair = pin(
        ffn_near, cross_grad, grad_att_own, grad_att_other, out_pair
    )
    cut = 3 * hidden_width // 2
    ffn_planes = plane_sums(ffn_grad, ffn_near, groups, 0, cut)
    more_planes = plane_sums(ffn_grad, ffn_near, groups, cut, 2 * cut)
    ffn_planes, more_planes, grad_att_own, grad_att_other = pin(
        ffn_planes, more_planes, grad_att_own, grad_att_other
    )
    cross_far = scatter_far(cross_grad, groups)
    ffn_high = scatter_planes(ffn_planes, groups)
    grad_qkv_own, grad_qkv_other, distance_sums = call(
        functools.partial(self_back_kernel, width),
        info,
        (
            window,
            qkv_own,
            grad_att_own,
            qkv_other,
            grad_att_other,
        ),
        [((seq_len, 3 * width), bf16)] * 2 + [(window.shape, f32)],
        sum_scratch,
    )
    cross_far, ffn_high, more_planes, grad_qkv_own, grad_qkv_other, grad_memory = pin(
        cross_far, ffn_high, more_planes, grad_qkv_own, grad_qkv_other, grad_memory
    )
    more_high = scatter_planes(more_planes, groups)
    cross_sums = near_sums(cross_grad, cross_far, groups)
    cross_sums, grad_qkv_own, grad_qkv_other = pin(cross_sums, grad_qkv_own, grad_qkv_other)
    cross_near = scatter_near(cross_sums, groups)
    grad_start, small = call(
        functools.partial(start_kernel, width, modes),
        info,
        (
            grad_qkv_own,
            (one_own, 0, 3 * width),
            grad_qkv_other,
            (one_other, 0, 3 * width),
            start_state,
            rows,
            grad_after_self,
            distance_sums,
            wide_hot,
            gains_two,
            gains_three,
        ),
        [(tall, f32), ((24, model_width), f32)],
    )
    small_other = swap_halves(small)
    qkv_grad = weight_grads(
        ((normed_one, swap_halves(normed_one), grad_qkv_own, swap_halves(grad_qkv_other)),),
        info,
        groups,
        (small, small_other),
    )
    qkv_grad, more_high, cross_near, grad_start, grad_memory = pin(
        qkv_grad, more_high, cross_near, grad_start, grad_memory
    )
    qkv_far = scatter_far(qkv_grad, groups)
    cross_planes = plane_sums(cross_grad, cross_near, groups, 0, 5 * width)
    cross_high = scatter_planes(cross_planes, groups)
    out_mine = lax.dynamic_index_in_dim(out_pair, half_id, 0, keepdims=False)
    out_sent = lax.dynamic_index_in_dim(out_pair, 1 - half_id, 0, keepdims=False)
    out_other, memory_other = swap_halves(out_sent), swap_halves(grad_memory)
    qkv_far, out_other, memory_other, grad_start = pin(qkv_far, out_other, memory_other, grad_start)
    qkv_sums = near_sums(qkv_grad, qkv_far, groups)
    qkv_sums, grad_start = pin(qkv_sums, grad_start)
    qkv_near = scatter_near(qkv_sums, groups)
    start_other = swap_halves(grad_start)
    qkv_near, start_other, memory_other, out_mine, out_other, ffn_high, more_high = pin(
        qkv_near, start_other, memory_other, out_mine, out_other, ffn_high, more_high
    )
    layer_output = join_columns(out_mine, out_other, half_id)
    tokens_grad = both_sequences(grad_start, start_other, half_id)
    memory_grad = both_sequences(grad_memory, memory_other, half_id)
    ffn_mine = jnp.concatenate(
        [jnp.sum(part.astype(f32), axis=0) for part in (ffn_high, more_high)], axis=1
    )
    self_mine = scatter_sum(
        scatter_high(high_sums(qkv_grad, qkv_near, groups, group_id), groups)
    )
    cross_mine = jnp.sum(cross_high.astype(f32), axis=0)
    small_mine = self_mine[:, 3 * width :]
    mine = small_mine[:, :8].T
    if shard_width >= bucket_count:
        table_total = small_mine[:bucket_count, 8:24]
    else:
        table_total = lax.psum(small[8:24, :bucket_count] + small_other[8:24, :bucket_count], dp_axes).T
    table_mine = lax.dynamic_slice_in_dim(table_total, half_id * heads_here, heads_here, 1)
    return (
        layer_output,
        tokens_grad,
        memory_grad,
        mine[3 : 3 + modes],
        mine[0],
        mine[1],
        mine[2],
        table_mine,
        self_mine[:, :width],
        self_mine[:, width : 2 * width],
        self_mine[:, 2 * width : 3 * width],
        cross_mine[:, 4 * width :].T,
        cross_mine[:, :width],
        cross_mine[:, width : 2 * width],
        cross_mine[:, 2 * width : 3 * width],
        cross_mine[:, 3 * width : 4 * width].T,
        ffn_mine[:, :hidden_width],
        ffn_mine[:, hidden_width : 2 * hidden_width],
        ffn_mine[:, 2 * hidden_width :].T,
    )


def solution(mesh):
    groups, halves = mesh.shape["dp"], mesh.shape["heads"]
    low = 4 if groups % 4 == 0 else 1
    mesh = Mesh(mesh.devices.reshape(groups // low, low, halves), dp_axes + ("heads",))
    rows_dp = P(dp_axes, None)
    columns = P(dp_axes, "heads")
    rows_heads = P("heads", dp_axes)
    in_specs = (
        (rows_dp, rows_dp, P(dp_axes + ("heads",), None))
        + (P(),) * 5
        + (P(None, dp_axes), P(dp_axes), P(dp_axes), P(dp_axes), P(None, "heads"))
        + (columns, columns, columns, rows_heads) * 2
        + (columns, columns, rows_heads)
    )
    out_specs = (
        (P(dp_axes + ("heads",), None), rows_dp, rows_dp)
        + (P(None, dp_axes), P(dp_axes), P(dp_axes), P(dp_axes), P(None, "heads"))
        + (columns, columns, columns, rows_heads) * 2
        + (columns, columns, rows_heads)
    )
    return jax.shard_map(body, mesh=mesh, in_specs=in_specs, out_specs=out_specs, check_vma=False)
```

```python
import functools

import jax
import jax.numpy as jnp
from jax import lax
from jax.experimental import pallas as pl
from jax.experimental.pallas import tpu as pltpu
from jax.sharding import Mesh
from jax.sharding import PartitionSpec as P

norm_epsilon = 1e-06
masked_score = -1000000000.0
lanes = 128
window_width = 512
cross_height = 384
dp_axes = ("high", "low")
highest = lax.Precision.HIGHEST
bf16 = jnp.bfloat16
f32 = jnp.float32


def kernel_params(limit_mib=56):
    return pltpu.CompilerParams(vmem_limit_bytes=limit_mib * 1024 * 1024)


def cost(flops, moved, special=0):
    return pl.CostEstimate(flops=1000, bytes_accessed=1000, transcendentals=0)


def matmul(left_side, right_side):
    return jnp.dot(left_side, right_side, preferred_element_type=f32)


def matmul_left_t(left_side, right_side):
    return lax.dot_general(
        left_side, right_side, (((0,), (0,)), ((), ())), preferred_element_type=f32
    )


def matmul_right_t(left_side, right_side):
    return lax.dot_general(
        left_side, right_side, (((1,), (1,)), ((), ())), preferred_element_type=f32
    )


def rms_scale(hidden):
    return lax.rsqrt(jnp.mean(hidden * hidden, axis=-1, keepdims=True) + norm_epsilon)


def swap_halves(values):
    return lax.ppermute(values, "heads", [(0, 1), (1, 0)])


def flip_low(values, groups, bits):
    return lax.ppermute(values, dp_axes, [(i, i ^ bits) for i in range(groups)])


def shift_high(values, groups, step):
    high = groups // 4
    pairs = []
    for source in range(groups):
        z, low = source // 4, source % 4
        pairs.append((source, ((z - step) % high) * 4 + low))
    return lax.ppermute(values, dp_axes, pairs)


def stepwise(groups):
    return groups % 4 == 0 and 1 < groups // 4 <= 4


def place_kernel(order_ref, own_ref, x_ref, y_ref, left_ref, right_ref, out_ref, sems):
    high = own_ref.shape[0]
    half = left_ref.shape[2]
    z, low = order_ref[0], order_ref[1]
    copies = []
    for step in range(high):
        base = lax.rem(z + step, high) * 4
        moves = (
            (own_ref.at[step], out_ref.at[base + low]),
            (x_ref.at[step], out_ref.at[base + (low ^ 1)]),
            (y_ref.at[step], out_ref.at[base + (low ^ 2)]),
            (left_ref.at[step], out_ref.at[base + (low ^ 3), :, :half]),
            (right_ref.at[step], out_ref.at[base + (low ^ 3), :, half:]),
        )
        for i, (source, target) in enumerate(moves):
            copy = pltpu.make_async_copy(source, target, sems.at[5 * step + i])
            copy.start()
            copies.append(copy)
    for copy in copies:
        copy.wait()


def copy_call(body_fn, order, arrays, shape, copies):
    anywhere = pl.BlockSpec(memory_space=pl.ANY)
    return pl.pallas_call(
        body_fn,
        out_shape=jax.ShapeDtypeStruct(shape, arrays[0].dtype),
        in_specs=[pl.BlockSpec(memory_space=pltpu.SMEM)] + [anywhere] * len(arrays),
        out_specs=anywhere,
        scratch_shapes=[pltpu.SemaphoreType.DMA((copies,))],
        compiler_params=kernel_params(8),
        cost_estimate=cost(0, 0),
    )(order, *arrays)


def pin(*values):
    return lax.optimization_barrier(values)


def gather_high(shard, groups):
    if not stepwise(groups):
        return [shard]
    return [shard] + [shift_high(shard, groups, k) for k in range(1, groups // 4)]


def gather_near(stack, groups):
    if not stepwise(groups):
        return ()
    return flip_low(stack, groups, 1), flip_low(stack, groups, 2)


def gather_far(near, groups):
    if not stepwise(groups):
        return ()
    half = near[0].shape[2] // 2
    return (
        flip_low(near[0][:, :, :half], groups, 2),
        flip_low(near[1][:, :, half:], groups, 1),
    )


def gather_place(stack, near, far, groups, group_id):
    if not stepwise(groups):
        return lax.all_gather(stack[0], dp_axes, axis=0, tiled=True)
    rows, width = stack.shape[1:]
    order = jnp.stack([group_id // 4, group_id % 4]).astype(jnp.int32)
    arrays = (stack, *near, *far)
    placed = copy_call(place_kernel, order, arrays, (groups, rows, width), 5 * stack.shape[0])
    return placed.reshape(groups * rows, width)


def scatter_far(grad, groups):
    if not stepwise(groups):
        return ()
    return flip_low(grad[0], groups, 1), flip_low(grad[1], groups, 2)


def near_sums(grad, far, groups):
    if not stepwise(groups):
        return ()
    left, right = far
    with_right = jnp.concatenate([jnp.zeros_like(left), right], 2)
    with_left = jnp.concatenate([left, jnp.zeros_like(right)], 2)
    for_x = grad[2][1].astype(f32) + with_right.astype(f32)
    for_y = grad[2][2].astype(f32) + with_left.astype(f32)
    return for_x.astype(bf16), for_y.astype(bf16)


def scatter_near(sums, groups):
    if not stepwise(groups):
        return ()
    return flip_low(sums[0], groups, 1), flip_low(sums[1], groups, 2)


def high_sums(grad, near, groups, group_id):
    if not stepwise(groups):
        return grad
    high = groups // 4
    z = group_id // 4
    plane = grad[2][0].astype(f32) + near[0].astype(f32) + near[1].astype(f32)
    plane_low = plane.astype(bf16)
    return [lax.dynamic_index_in_dim(plane, z, 0, keepdims=False)] + [
        lax.dynamic_index_in_dim(plane_low, (z - k) % high, 0, keepdims=False)
        for k in range(1, high)
    ]


def scatter_high(sums, groups):
    if not stepwise(groups):
        return [lax.psum_scatter(sums[0], dp_axes, scatter_dimension=0, tiled=True).astype(f32)]
    return [sums[0]] + [shift_high(sums[k], groups, k) for k in range(1, groups // 4)]


def plane_sums(grad, near, groups, start, stop):
    if not stepwise(groups):
        return grad[0][:, start:stop]
    here = slice(start, stop)
    parts = (grad[2][0], near[0], near[1])
    return sum(part[:, :, here].astype(f32) for part in parts).astype(bf16)


def scatter_planes(planes, groups):
    if not stepwise(groups):
        return lax.psum_scatter(planes, dp_axes, scatter_dimension=0, tiled=True)[None]
    return lax.all_to_all(planes, "high", split_axis=0, concat_axis=0, tiled=True)


def scatter_sum(parts):
    return sum(part.astype(f32) for part in parts)


def reorder_kernel(order_ref, in_ref, out_ref):
    def one(i, carry):
        out_ref[i] = in_ref[order_ref[i]]
        return carry

    lax.fori_loop(0, out_ref.shape[0], one, 0)


def reorder(blocks, order):
    vmem = pl.BlockSpec(memory_space=pltpu.VMEM)
    return pl.pallas_call(
        reorder_kernel,
        out_shape=jax.ShapeDtypeStruct(blocks.shape, blocks.dtype),
        in_specs=[pl.BlockSpec(memory_space=pltpu.SMEM), vmem],
        out_specs=vmem,
        compiler_params=kernel_params(),
        cost_estimate=cost(0, 4 * blocks.size),
    )(order, blocks)


def both_kernel(half_ref, own_ref, other_ref, out_ref):
    half = half_ref[0]
    out_ref[half] = own_ref[...]
    out_ref[1 - half] = other_ref[...]


def both_sequences(own, other, half_id):
    vmem = pl.BlockSpec(memory_space=pltpu.VMEM)
    both = pl.pallas_call(
        both_kernel,
        out_shape=jax.ShapeDtypeStruct((2, *own.shape), own.dtype),
        in_specs=[pl.BlockSpec(memory_space=pltpu.SMEM), vmem, vmem],
        out_specs=vmem,
        compiler_params=kernel_params(),
        cost_estimate=cost(0, 0),
    )(half_id.reshape(1), own, other)
    return both.reshape(-1, own.shape[1])


def column_half(values, which):
    part = values.shape[-1] // 2
    return lax.dynamic_slice_in_dim(values, which * part, part, values.ndim - 1)


def sequence_pieces(rows, groups, half_id):
    length, width = rows.shape
    keep = column_half(rows, half_id)
    other = swap_halves(column_half(rows, 1 - half_id))
    first = half_id == 0
    pair = jnp.stack([jnp.where(first, keep, other), jnp.where(first, other, keep)])
    return pair.reshape(2, groups, length // groups, width // 2).transpose(1, 0, 2, 3)


def exchange(pieces):
    return lax.all_to_all(pieces, dp_axes, split_axis=0, concat_axis=0, tiled=True)


def ordered_pieces(pieces, order, groups):
    _, _, piece, part = pieces.shape
    mixed = reorder(pieces.reshape(2 * groups, piece, part), order)
    return mixed.reshape(groups, 2, piece, part)


def collect_pieces(mixed):
    groups, _, piece, part = mixed.shape
    return exchange(mixed).transpose(1, 0, 2, 3).reshape(2, groups * piece, part)


def join_columns(mine, theirs, half_id):
    first = half_id == 0
    return jnp.where(
        first, jnp.concatenate([mine, theirs], -1), jnp.concatenate([theirs, mine], -1)
    )


def dot_rows(left_side, right_side):
    return lax.dot_general(
        left_side, right_side, (((1,), (1,)), ((), ())), preferred_element_type=f32
    )


def head_lanes(values, which):
    lane = lax.broadcasted_iota(jnp.int32, values.shape, 1)
    keep = (lane < lanes // 2) if which == 0 else (lane >= lanes // 2)
    return jnp.where(keep, values, jnp.zeros_like(values))


def bias_blocks(window_ref, head):
    row = window_ref[pl.ds(head, 1), :]
    spread = jnp.broadcast_to(row, (lanes, window_width))
    return pltpu.roll(spread, 0, 1, stride=1, stride_axis=0)


def both_heads(values):
    return jnp.concatenate([head_lanes(values, 0), head_lanes(values, 1)], axis=0)


def join_heads(values):
    rows = values.shape[0] // 2
    lane = lax.broadcasted_iota(jnp.int32, (rows, lanes), 1)
    return jnp.where(lane < lanes // 2, values[:rows], values[rows:])


def masked_block(raw, biases, seq_len, length, first):
    height, count = raw.shape[0] // 2, raw.shape[1]
    if biases is not None:
        rows = []
        for bias in biases:
            for at in range(first, first + height, lanes):
                row = [bias[:, seq_len - lanes - at : seq_len]]
                if at + lanes < count:
                    row.append(jnp.full((lanes, count - at - lanes), masked_score, f32))
                rows.append(jnp.concatenate(row, axis=1))
        raw = raw + jnp.concatenate(rows, axis=0)
    column = lax.broadcasted_iota(jnp.int32, raw.shape, 1)
    return jnp.where(column < length, raw, masked_score)


def softmax_block(scores):
    exponent = jnp.exp(scores - jnp.max(scores, axis=1, keepdims=True))
    return exponent * (1.0 / jnp.sum(exponent, axis=1, keepdims=True))


def attend(causal, places, length, window_ref, side, inputs, out_ref):
    seq_len, width = out_ref.shape
    pairs = width // lanes
    height = lanes if causal else cross_height
    query_ref, key_ref, value_ref = inputs

    def one_pair(pair, carry):
        at = [pl.multiple_of(place + pair * lanes, lanes) for place in places]
        here = pl.ds(pl.multiple_of(pair * lanes, lanes), lanes)
        biases = None
        if causal:
            head = side * 2 * pairs + 2 * pair
            biases = [bias_blocks(window_ref, head + a) for a in range(2)]
        for first in range(0, seq_len, height):
            count = first + height if causal else seq_len
            query = both_heads(query_ref[first : first + height, pl.ds(at[0], lanes)])
            raw = dot_rows(query, key_ref[:count, pl.ds(at[1], lanes)])
            weights = softmax_block(masked_block(raw, biases, seq_len, length, first)).astype(bf16)
            blended = jnp.dot(
                weights, value_ref[:count, pl.ds(at[2], lanes)], preferred_element_type=f32
            )
            out_ref[first : first + height, here] = join_heads(blended).astype(bf16)
        return carry

    lax.fori_loop(0, pairs, one_pair, 0, unroll=True)


def diagonal_sums(block):
    rows, columns = block.shape
    wide = jnp.concatenate([block, jnp.zeros((rows, window_width - columns), f32)], axis=1)
    total = wide[0:8]
    for first in range(8, rows, 8):
        total = total + pltpu.roll(wide[first : first + 8], window_width - first, 1)
    row = lax.broadcasted_iota(jnp.int32, total.shape, 0)
    for bit in (1, 2, 4):
        total = jnp.where((row & bit) != 0, pltpu.roll(total, window_width - bit, 1), total)
    return jnp.sum(total, axis=0, keepdims=True)


def attend_back(
    causal, places, length, window_ref, side, inputs, query_out, key_out, sums_ref, key_sum, value_sum
):
    query_ref, key_ref, value_ref, grad_ref = inputs
    seq_len, width = grad_ref.shape
    pairs = width // lanes
    height = cross_height

    def one_pair(pair, carry):
        at = [pl.multiple_of(place + pair * lanes, lanes) for place in places]
        here = pl.ds(pl.multiple_of(pair * lanes, lanes), lanes)
        head = side * 2 * pairs + 2 * pair
        biases = None
        if causal:
            biases = [bias_blocks(window_ref, head + a) for a in range(2)]
        sums = [None, None]
        for first in reversed(range(0, seq_len, height)):
            count = first + height if causal else seq_len
            query = both_heads(query_ref[first : first + height, pl.ds(at[0], lanes)])
            grad = both_heads(grad_ref[first : first + height, here])
            key = key_ref[:count, pl.ds(at[1], lanes)]
            value = value_ref[:count, pl.ds(at[2], lanes)]
            raw = dot_rows(query, key)
            weights = softmax_block(masked_block(raw, biases, seq_len, length, first))
            grad_weights = dot_rows(grad, value)
            dots = jnp.sum(weights * grad_weights, axis=1, keepdims=True)
            grad_scores = (weights * (grad_weights - dots)).astype(bf16)
            grad_query = jnp.dot(grad_scores, key, preferred_element_type=f32)
            query_out[first : first + height, pl.ds(at[0], lanes)] = join_heads(grad_query).astype(
                bf16
            )
            key_part = matmul_left_t(grad_scores, query)
            value_part = matmul_left_t(weights.astype(bf16), grad)
            if causal:
                for a in range(2):
                    for inner in range(0, height, lanes):
                        row = first + inner
                        part = grad_scores[a * height + inner :][:lanes, : row + lanes].astype(f32)
                        start = seq_len - lanes - row
                        if sums[a] is None:
                            gap = [jnp.zeros((lanes, start), f32)] if start else []
                            sums[a] = jnp.concatenate(gap + [part], axis=1)
                        elif start == 0:
                            sums[a] = sums[a] + part
                        else:
                            sums[a] = jnp.concatenate(
                                [sums[a][:, :start], sums[a][:, start:] + part], axis=1
                            )
            if count == seq_len and first + height == seq_len:
                key_sum[...] = key_part
                value_sum[...] = value_part
            else:
                key_sum[:count] = key_sum[:count] + key_part
                value_sum[:count] = value_sum[:count] + value_part
        key_out[:, pl.ds(at[1], lanes)] = key_sum[...].astype(bf16)
        key_out[:, pl.ds(at[2], lanes)] = value_sum[...].astype(bf16)
        if causal:
            for a in range(2):
                sums_ref[pl.ds(head + a, 1), :] = diagonal_sums(sums[a])
        return carry

    lax.fori_loop(0, pairs, one_pair, 0, unroll=True)


class Source:
    def __init__(self, held, copy):
        self.held, self.copy, self.here = held, copy, False
        self.shape = held.shape
        copy.start()

    def ready(self):
        if not self.here:
            self.copy.wait()
            self.here = True
        return self.held

    def __getitem__(self, key):
        return self.ready()[key]


class Target:
    def __init__(self, held, copy):
        self.held, self.copy, self.sent = held, copy, False
        self.shape = held.shape

    def __getitem__(self, key):
        return self.held[key]

    def __setitem__(self, key, value):
        self.held[key] = value

    def send(self):
        if not self.sent:
            self.copy.start()
            self.sent = True


class Whole:
    def __init__(self, held):
        self.held, self.shape = held, held.shape

    def ready(self):
        return self.held

    def send(self):
        pass

    def __getitem__(self, key):
        return self.held[key]

    def __setitem__(self, key, value):
        self.held[key] = value


def all_columns(entries):
    return [entry if isinstance(entry, tuple) else (entry, 0, entry.shape[1]) for entry in entries]


def call(body_fn, info, entries, shapes, scratch=()):
    entries = all_columns(entries)
    arrays = []
    for array, _, _ in entries:
        if all(array is not known for known in arrays):
            arrays.append(array)

    def kernel(info_ref, *refs):
        ins = []
        for array, first, last in entries:
            ref = next(r for r, known in zip(refs, arrays) if known is array)
            ins.append(Whole(ref.at[:, first:last] if last - first < array.shape[1] else ref))
        outs = refs[len(arrays) : len(arrays) + len(shapes)]
        body_fn(info_ref, *ins, *map(Whole, outs), *refs[len(arrays) + len(shapes) :])

    vmem = pl.BlockSpec(memory_space=pltpu.VMEM)
    return pl.pallas_call(
        kernel,
        out_shape=[jax.ShapeDtypeStruct(shape, dtype) for shape, dtype in shapes],
        in_specs=[pl.BlockSpec(memory_space=pltpu.SMEM)] + [vmem] * len(arrays),
        out_specs=[vmem] * len(shapes),
        scratch_shapes=list(scratch),
        compiler_params=kernel_params(),
        cost_estimate=cost(0, 0),
    )(info, *arrays)


def stream(body_fn, info, entries, shapes, scratch=()):
    entries = all_columns(entries)
    count, outs = len(entries), len(shapes)
    plain = [a.size * a.dtype.itemsize < 1 << 20 and last - first == a.shape[1] for a, first, last in entries]

    def kernel(info_ref, *refs):
        sources, targets = refs[:count], refs[count : count + outs]
        held = refs[count + outs : 2 * (count + outs)]
        sems = refs[2 * (count + outs)]
        rest = refs[2 * (count + outs) + 1 :]
        ins = []
        for i, (array, first, last) in enumerate(entries):
            source = sources[i]
            if plain[i]:
                ins.append(Whole(source))
                continue
            if last - first < array.shape[1]:
                source = source.at[:, first:last]
            ins.append(Source(held[i], pltpu.make_async_copy(source, held[i], sems.at[i])))
        gone = []
        for i in range(outs):
            copy = pltpu.make_async_copy(held[count + i], targets[i], sems.at[count + i])
            gone.append(Target(held[count + i], copy))
        body_fn(info_ref, *ins, *gone, *rest)
        for target in gone:
            target.send()
        for source in ins:
            source.ready()
        for target in gone:
            target.copy.wait()

    anywhere = pl.BlockSpec(memory_space=pl.ANY)
    vmem = pl.BlockSpec(memory_space=pltpu.VMEM)
    return pl.pallas_call(
        kernel,
        out_shape=[jax.ShapeDtypeStruct(shape, dtype) for shape, dtype in shapes],
        in_specs=[pl.BlockSpec(memory_space=pltpu.SMEM)] + [vmem if p else anywhere for p in plain],
        out_specs=[anywhere] * outs,
        scratch_shapes=[
            pltpu.VMEM((8, lanes) if p else (array.shape[0], last - first), array.dtype)
            for p, (array, first, last) in zip(plain, entries)
        ]
        + [pltpu.VMEM(shape, dtype) for shape, dtype in shapes]
        + [pltpu.SemaphoreType.DMA((count + outs,))]
        + list(scratch),
        compiler_params=kernel_params(),
        cost_estimate=cost(0, 0),
    )(info, *[array for array, _, _ in entries])


def dot(left_side, right_side):
    return jnp.dot(left_side, right_side, preferred_element_type=f32)


def norm_rows(state, gain_row):
    return (state * rms_scale(state) * gain_row).astype(bf16)


def self_kernel(
    width,
    modes,
    info,
    small,
    tokens,
    weight_own,
    weight_other,
    window,
    start,
    normed,
    qkv_own,
    qkv_other,
    attended_own,
    attended_other,
    rows,
):
    length = start.shape[0]
    rows[...] = small[...].astype(f32).T[:8]
    mode_row = jnp.zeros_like(rows[0:1, :])
    for m in range(modes):
        mode_row = mode_row + jnp.where(info[1] == m, rows[3 + m : 4 + m, :], 0.0)
    at = pl.ds(pl.multiple_of(info[0] * length, 16), length)
    start[...] = tokens[at, :].astype(f32) + mode_row
    normed[...] = norm_rows(start[...], rows[0:1, :])
    for target in (rows, start, normed):
        target.send()
    sides = ((weight_own, qkv_own, attended_own), (weight_other, qkv_other, attended_other))
    for side, (weight, qkv, attended) in enumerate(sides):
        for first in range(0, 3 * width, width):
            qkv[:, first : first + width] = dot(
                normed[...], weight[:, first : first + width]
            ).astype(bf16)
        qkv.send()
        attend(
            True,
            (0, width, 2 * width),
            info[2],
            window.ready(),
            side,
            (qkv.held,) * 3,
            attended.held,
        )
        attended.send()


def cross_kernel(
    width,
    info,
    attended_own,
    out_own,
    attended_other,
    out_other,
    start,
    rows,
    memory,
    kv_weight_own,
    q_weight_own,
    kv_weight_other,
    q_weight_other,
    after_self,
    normed,
    q_own,
    q_other,
    kv_own,
    kv_other,
    crossed_own,
    crossed_other,
):
    length = start.shape[0]
    part = dot_rows(attended_own[...], out_own[...])
    part = part + dot_rows(attended_other[...], out_other[...])
    after_self[...] = start[...] + part
    normed[...] = norm_rows(after_self[...], rows[1:2, :])
    after_self.send()
    normed.send()
    at = pl.ds(pl.multiple_of(info[0] * length, 16), length)
    sides = (
        (kv_weight_own, q_weight_own, q_own, kv_own, crossed_own),
        (kv_weight_other, q_weight_other, q_other, kv_other, crossed_other),
    )
    for side, (kv_weight, q_weight, q, kv, crossed) in enumerate(sides):
        kv[:, :width] = dot(memory[at, :], kv_weight[:, :width]).astype(bf16)
        kv[:, width:] = dot(memory[at, :], kv_weight[:, width:]).astype(bf16)
        q[...] = dot(normed[...], q_weight[...]).astype(bf16)
        q.send()
        kv.send()
        attend(
            False,
            (0, 0, width),
            info[3],
            None,
            side,
            (q.held, kv.held, kv.held),
            crossed.held,
        )
        crossed.send()


def ffn_kernel(
    info,
    crossed_own,
    out_own,
    crossed_other,
    out_other,
    after_self,
    rows,
    cot,
    gate_own,
    up_own,
    down_own,
    gate_other,
    up_other,
    down_other,
    after_cross,
    normed,
    hidden_own,
    hidden_other,
    grad_pre_own,
    grad_pre_other,
    output,
    total,
):
    hidden_width = hidden_own.shape[1]
    part = dot_rows(crossed_own[...], out_own[...])
    part = part + dot_rows(crossed_other[...], out_other[...])
    after_cross[...] = after_self[...] + part
    normed[...] = norm_rows(after_cross[...], rows[2:3, :])
    total[...] = after_cross[...]
    after_cross.send()
    normed.send()
    sides = (
        (gate_own, up_own, down_own, hidden_own, grad_pre_own),
        (gate_other, up_other, down_other, hidden_other, grad_pre_other),
    )
    for gate, up, down, hidden, grad_pre in sides:
        for first in range(0, hidden_width, 256):
            here = slice(first, first + 256)
            there = slice(hidden_width + first, hidden_width + first + 256)
            gate_pre = dot(normed[...], gate[:, here])
            up_pre = dot(normed[...], up[:, here])
            grad_hidden = dot(cot[...], down[:, here]).astype(bf16).astype(f32)
            square = gate_pre * gate_pre * 0.044715
            bend = jnp.tanh(0.7978845608028654 * (gate_pre + square * gate_pre))
            half_more = 0.5 * (1.0 + bend)
            gelu = gate_pre * half_more
            slope = half_more + 0.5 * gate_pre * (1.0 - bend * bend) * 0.7978845608028654 * (
                1.0 + 3.0 * square
            )
            low = (gelu * up_pre).astype(bf16)
            hidden[:, here] = low
            grad_pre[:, here] = (grad_hidden * up_pre * slope).astype(bf16)
            grad_pre[:, there] = (grad_hidden * gelu).astype(bf16)
            total[...] = total[...] + dot_rows(low, down[:, here])
        hidden.send()
        grad_pre.send()
    output[...] = total[...].astype(bf16)


def norm_back_rows(state, gain_row, grad_normed):
    scale = rms_scale(state)
    scaled = state * scale
    weighted = grad_normed * gain_row
    inner = jnp.mean(weighted * scaled, axis=-1, keepdims=True)
    return scale * (weighted - scaled * inner), jnp.sum(grad_normed * scaled, axis=0, keepdims=True)


def ffn_back_kernel(
    info,
    grad_pre_own,
    gate_up_own,
    grad_pre_other,
    gate_up_other,
    after_cross,
    rows,
    cot,
    out_own,
    out_other,
    grad_state,
    branch,
    grad_own,
    grad_other,
    gains,
):
    grad_normed = dot_rows(grad_pre_own[...], gate_up_own[...])
    grad_normed = grad_normed + dot_rows(grad_pre_other[...], gate_up_other[...])
    part, gain = norm_back_rows(after_cross[...], rows[2:3, :], grad_normed)
    gains[...] = jnp.zeros_like(gains[...])
    gains[2:3, :] = gain
    grad_state[...] = cot[...].astype(f32) + part
    branch[...] = grad_state[...].astype(bf16)
    for target in (gains, grad_state, branch):
        target.send()
    grad_own[...] = dot(branch[...], out_own[...]).astype(bf16)
    grad_other[...] = dot(branch[...], out_other[...]).astype(bf16)


def cross_back_kernel(
    width,
    info,
    q_own,
    kv_own,
    grad_own,
    q_other,
    kv_other,
    grad_other,
    grad_q_own,
    grad_q_other,
    grad_kv_own,
    grad_kv_other,
    key_sum,
    value_sum,
):
    sides = (
        (q_own, kv_own, grad_own, grad_q_own, grad_kv_own),
        (q_other, kv_other, grad_other, grad_q_other, grad_kv_other),
    )
    for side, (q, kv, grad, grad_q, grad_kv) in enumerate(sides):
        attend_back(
            False,
            (0, 0, width),
            info[3],
            None,
            side,
            (q.ready(), kv.ready(), kv.ready(), grad.ready()),
            grad_q.held,
            grad_kv.held,
            None,
            key_sum,
            value_sum,
        )


def between_kernel(
    info,
    grad_q_own,
    q_weight_own,
    grad_q_other,
    q_weight_other,
    after_self,
    rows,
    grad_in,
    out_own,
    out_other,
    grad_kv_own,
    kv_weight_own,
    grad_kv_other,
    kv_weight_other,
    grad_state,
    branch,
    grad_own,
    grad_other,
    grad_memory,
    gains,
):
    grad_normed = dot_rows(grad_q_own[...], q_weight_own[...])
    grad_normed = grad_normed + dot_rows(grad_q_other[...], q_weight_other[...])
    part, gain = norm_back_rows(after_self[...], rows[1:2, :], grad_normed)
    gains[...] = jnp.zeros_like(gains[...])
    gains[1:2, :] = gain
    grad_state[...] = grad_in[...] + part
    branch[...] = grad_state[...].astype(bf16)
    for target in (gains, grad_state, branch):
        target.send()
    grad_own[...] = dot(branch[...], out_own[...]).astype(bf16)
    grad_own.send()
    grad_other[...] = dot(branch[...], out_other[...]).astype(bf16)
    grad_other.send()
    memory_part = dot_rows(grad_kv_own[...], kv_weight_own[...])
    grad_memory[...] = memory_part + dot_rows(grad_kv_other[...], kv_weight_other[...])


def self_back_kernel(
    width,
    info,
    window,
    qkv_own,
    grad_own,
    qkv_other,
    grad_other,
    grad_qkv_own,
    grad_qkv_other,
    sums,
    key_sum,
    value_sum,
):
    sides = ((qkv_own, grad_own, grad_qkv_own), (qkv_other, grad_other, grad_qkv_other))
    for side, (qkv, grad, grad_qkv) in enumerate(sides):
        attend_back(
            True,
            (0, width, 2 * width),
            info[2],
            window.ready(),
            side,
            (qkv.ready(),) * 3 + (grad.ready(),),
            grad_qkv.held,
            grad_qkv.held,
            sums.held,
            key_sum,
            value_sum,
        )
        grad_qkv.send()


def start_kernel(
    width,
    modes,
    info,
    grad_qkv_own,
    weight_own,
    grad_qkv_other,
    weight_other,
    start,
    rows,
    grad_in,
    sums,
    hot,
    gains_two,
    gains_three,
    grad_start,
    small,
):
    heads_here = width // 64
    grad_normed = dot_rows(grad_qkv_own[...], weight_own[...])
    grad_normed = grad_normed + dot_rows(grad_qkv_other[...], weight_other[...])
    part, gain = norm_back_rows(start[...], rows[0:1, :], grad_normed)
    grad_start[...] = grad_in[...] + part
    grad_start.send()
    small[...] = jnp.zeros_like(small[...])
    small[0:8, :] = gains_two[...] + gains_three[...]
    small[0:1, :] = gain
    total = jnp.sum(grad_start[...], axis=0, keepdims=True)
    for m in range(modes):
        small[3 + m : 4 + m, :] = jnp.where(info[1] == m, total, 0.0)
    table = lax.dot_general(
        sums[...], hot[...], (((1,), (1,)), ((), ())), precision=highest, preferred_element_type=f32
    )
    first, second = table[:heads_here], table[heads_here : 2 * heads_here]
    is_first = info[0] == 0
    small[8 : 8 + heads_here, : hot.shape[0]] = jnp.where(is_first, first, second)
    small[8 + heads_here : 8 + 2 * heads_here, : hot.shape[0]] = jnp.where(is_first, second, first)


def small_block(small, rows):
    depth = small.shape[1]
    turned = jnp.concatenate([small[:8], jnp.zeros((lanes - 8, depth), f32)], axis=0).T
    table = jnp.concatenate([small[8:24, :lanes], jnp.zeros((lanes - 16, lanes), f32)], axis=0).T
    lane = lax.broadcasted_iota(jnp.int32, (rows, lanes), 1)
    table = pltpu.roll(table[:rows], 8, 1)
    parts = [
        jnp.where(lane < 8, turned[at : at + rows], table) for at in range(0, depth, rows)
    ]
    return parts


def grad_tiles(counts, with_small, half):
    tiles, start = [], 0
    for i, count in enumerate(counts):
        for first in range(0, count, 512):
            stop = min(count, first + 512)
            cuts = [start + first, start + stop]
            if cuts[0] < half < cuts[1]:
                cuts.insert(1, half)
            for a, b in zip(cuts[:-1], cuts[1:]):
                tiles.append((i, a - start, b - start, a))
        start += count
    if with_small:
        tiles.append((len(counts), 0, lanes, start))
    return tiles


def grad_kernel(counts, with_small, info, *refs):
    total = 4 * len(counts) + (2 if with_small else 0)
    given, (left_ref, right_ref, mid_ref) = refs[:total], refs[total : total + 3]
    held, (quad, in_sems, out_sems) = refs[total + 3 : -3], refs[-3:]
    inputs = [
        Source(held[i], pltpu.make_async_copy(given[i], held[i], in_sems.at[i]))
        for i in range(total)
    ]
    high, rows = quad.shape[1], quad.shape[2]
    half = left_ref.shape[2]
    low = info[4]
    copies = []
    for n, (i, first, stop, at) in enumerate(grad_tiles(counts, with_small, half)):
        width = stop - first
        here = slice(at, at + width)
        if i < len(counts):
            left_own, left_other, right_own, right_other = inputs[4 * i : 4 * i + 4]
            part = matmul_left_t(left_own[...], right_own[:, first:stop])
            part = part + matmul_left_t(left_other[...], right_other[:, first:stop])
            part = part.astype(bf16)
            blocks = [part[k * rows : (k + 1) * rows] for k in range(4 * high)]
        else:
            small = inputs[-2][...] + inputs[-1][...]
            blocks = [block.astype(bf16) for block in small_block(small, rows)]
        for z in range(high):
            for l in range(4):
                quad[low ^ l, z, :, here] = blocks[4 * z + l]
        far_ref, far_at = (left_ref, at) if at < half else (right_ref, at - half)
        moves = (
            (quad.at[3, :, :, here], far_ref.at[:, :, far_at : far_at + width]),
            (quad.at[0:3, :, :, here], mid_ref.at[:, :, :, here]),
        )
        for j, (source, target) in enumerate(moves):
            copy = pltpu.make_async_copy(source, target, out_sems.at[2 * n + j])
            copy.start()
            copies.append(copy)
    for copy in copies:
        copy.wait()


def weight_grads(entries, info, groups, small=()):
    counts = [entry[2].shape[1] for entry in entries]
    width = sum(counts) + (lanes if small else 0)
    depth = entries[0][0].shape[1]
    length = entries[0][0].shape[0]
    if not stepwise(groups):
        parts = [
            matmul_left_t(
                jnp.concatenate([a, b], axis=0), jnp.concatenate([c, d], axis=0)
            ).astype(bf16)
            for a, b, c, d in entries
        ]
        if small:
            both = small[0] + small[1]
            table = jnp.pad(both[8:24, : depth // groups].T, ((0, 0), (0, lanes - 24)))
            block = jnp.concatenate([both[:8].T, jnp.tile(table, (groups, 1))], axis=1)
            parts.append(block.astype(bf16))
        return (jnp.concatenate(parts, axis=1),)
    high, rows = groups // 4, depth // groups
    arrays = [value for entry in entries for value in entry] + list(small)
    anywhere = pl.BlockSpec(memory_space=pl.ANY)
    half = width // 2 // lanes * lanes
    shapes = [(high, rows, half), (high, rows, width - half), (3, high, rows, width)]
    tiles = len(grad_tiles(counts, bool(small), half))
    return pl.pallas_call(
        functools.partial(grad_kernel, counts, bool(small)),
        out_shape=[jax.ShapeDtypeStruct(shape, bf16) for shape in shapes],
        in_specs=[pl.BlockSpec(memory_space=pltpu.SMEM)] + [anywhere] * len(arrays),
        out_specs=[anywhere] * 3,
        scratch_shapes=[pltpu.VMEM(array.shape, array.dtype) for array in arrays]
        + [
            pltpu.VMEM((4, high, rows, width), bf16),
            pltpu.SemaphoreType.DMA((len(arrays),)),
            pltpu.SemaphoreType.DMA((2 * tiles,)),
        ],
        compiler_params=kernel_params(),
        cost_estimate=cost(0, 0),
    )(info, *arrays)


def body(
    tokens,
    memory,
    cotangent,
    seq_modes,
    dec_lengths,
    enc_lengths,
    slot_plan,
    buckets,
    mode_table,
    gain_self,
    gain_cross,
    gain_ffn,
    bucket_table,
    self_query,
    self_key,
    self_value,
    self_output,
    cross_query,
    cross_key,
    cross_value,
    cross_output,
    ffn_gate,
    ffn_up,
    ffn_down,
):
    groups = lax.axis_size(dp_axes)
    group_id = lax.axis_index(dp_axes)
    half_id = lax.axis_index("heads")
    seq_total = slot_plan.shape[0]
    seq_len = buckets.shape[0]
    model_width = tokens.shape[1]
    shard_width = model_width // groups
    heads_here = bucket_table.shape[1]
    bucket_count = bucket_table.shape[0]
    modes = mode_table.shape[0]
    width = self_query.shape[1]
    hidden_width = ffn_gate.shape[1]
    own_seq = group_id * 2 + half_id

    small = jnp.concatenate([jnp.stack([gain_self, gain_cross, gain_ffn]), mode_table]).T
    small = jnp.pad(small, ((0, 0), (0, lanes - small.shape[1])))
    pack_one = jnp.concatenate([self_query, self_key, self_value, small], axis=1)
    pack_two = jnp.concatenate(
        [self_output.T, cross_query, cross_key, cross_value], axis=1
    )
    pack_three = jnp.concatenate([cross_output.T, ffn_gate, ffn_up, ffn_down.T], axis=1)

    seq_ids = jnp.arange(seq_total, dtype=jnp.int32)
    placed = (slot_plan[:, None] == seq_ids[None, :]).astype(jnp.int32)
    source_of = jnp.sum(placed * seq_ids[:, None], axis=0)
    chosen = (seq_ids == own_seq).astype(jnp.int32)
    facts = jnp.sum(jnp.stack([seq_modes, dec_lengths, enc_lengths]) * chosen[None, :], axis=1)
    info = jnp.concatenate(
        [half_id.reshape(1), facts, (group_id % 4).reshape(1), (group_id // 4).reshape(1)]
    ).astype(jnp.int32)

    table_rows = jnp.concatenate([bucket_table, swap_halves(bucket_table)], axis=1).T
    reach = seq_len - lanes
    hole = window_width - seq_len
    window_bucket = jnp.concatenate(
        [
            jnp.flip(buckets[: reach + 1]),
            jnp.full((hole,), -1, jnp.int32),
            jnp.flip(buckets[reach + 1 :]),
        ]
    )
    window_hot = (jnp.arange(bucket_count)[:, None] == window_bucket[None, :]).astype(bf16)
    window = matmul(table_rows, window_hot)
    window = jnp.where(window_bucket[None, :] < 0, masked_score, window)
    window = jnp.pad(window, ((0, 16 - 2 * heads_here), (0, 0)))

    def stacked(parts):
        return jnp.stack(parts) if stepwise(groups) else parts

    high_one = gather_high(pack_one, groups)
    high_one, pack_two, pack_three = pin(high_one, pack_two, pack_three)
    three_own = lax.all_gather(pack_three, dp_axes, axis=0, tiled=True)
    cot_pieces = sequence_pieces(cotangent, groups, half_id)
    stack_one = stacked(high_one)
    near_one = gather_near(stack_one, groups)
    high_two = gather_high(pack_two, groups)
    near_one, high_two, cot_pieces = pin(near_one, high_two, cot_pieces)
    far_one = gather_far(near_one, groups)
    cot_pieces = exchange(cot_pieces)
    stack_two = stacked(high_two)
    near_two = gather_near(stack_two, groups)
    one_own = gather_place(stack_one, near_one, far_one, groups, group_id)
    one_other = swap_halves(one_own)

    tall = (seq_len, model_width)
    gate_at, up_at, down_at = width, width + hidden_width, width + 2 * hidden_width
    (
        start_state,
        normed_one,
        qkv_own,
        qkv_other,
        attended_own,
        attended_other,
        rows,
    ) = call(
        functools.partial(self_kernel, width, modes),
        info,
        (
            (one_own, 3 * width, 3 * width + lanes),
            tokens,
            (one_own, 0, 3 * width),
            (one_other, 0, 3 * width),
            window,
        ),
        [(tall, f32), (tall, bf16)]
        + [((seq_len, 3 * width), bf16)] * 2
        + [((seq_len, width), bf16)] * 2
        + [((8, model_width), f32)],
    )
    near_two, attended_own, attended_other, cot_pieces = pin(
        near_two, attended_own, attended_other, cot_pieces
    )
    far_two = gather_far(near_two, groups)
    cot_pair = collect_pieces(ordered_pieces(cot_pieces, slot_plan, groups))
    two_own = gather_place(stack_two, near_two, far_two, groups, group_id)
    other_memory = lax.dynamic_slice_in_dim(memory, (1 - half_id) * seq_len, seq_len, 0)
    own_memory = lax.dynamic_slice_in_dim(memory, half_id * seq_len, seq_len, 0)
    wide_hot = jnp.pad(window_hot.astype(f32), ((0, lanes - bucket_count), (0, 0)))
    two_own, cot_pair, other_memory, own_memory, wide_hot, source_of = pin(
        two_own, cot_pair, other_memory, own_memory, wide_hot, source_of
    )
    two_other = swap_halves(two_own)
    cot_pair_other = swap_halves(cot_pair)
    (
        after_self,
        normed_two,
        q_own,
        q_other,
        kv_own,
        kv_other,
        crossed_own,
        crossed_other,
    ) = call(
        functools.partial(cross_kernel, width),
        info,
        (
            attended_own,
            (two_own, 0, width),
            attended_other,
            (two_other, 0, width),
            start_state,
            rows,
            memory,
            (two_own, 2 * width, 4 * width),
            (two_own, width, 2 * width),
            (two_other, 2 * width, 4 * width),
            (two_other, width, 2 * width),
        ),
        [(tall, f32), (tall, bf16)]
        + [((seq_len, width), bf16)] * 2
        + [((seq_len, 2 * width), bf16)] * 2
        + [((seq_len, width), bf16)] * 2,
    )
    crossed_own, crossed_other, three_own = pin(crossed_own, crossed_other, three_own)
    three_other = swap_halves(three_own)
    cot_whole = join_columns(cot_pair, cot_pair_other, half_id)
    cot_own = lax.dynamic_index_in_dim(cot_whole, half_id, 0, keepdims=False)
    cot_other = lax.dynamic_index_in_dim(cot_whole, 1 - half_id, 0, keepdims=False)
    (
        after_cross,
        normed_three,
        hidden_own,
        hidden_other,
        grad_pre_own,
        grad_pre_other,
        seq_output,
    ) = stream(
        ffn_kernel,
        info,
        (
            crossed_own,
            (three_own, 0, width),
            crossed_other,
            (three_other, 0, width),
            after_self,
            rows,
            cot_own,
            (three_own, gate_at, up_at),
            (three_own, up_at, down_at),
            (three_own, down_at, down_at + hidden_width),
            (three_other, gate_at, up_at),
            (three_other, up_at, down_at),
            (three_other, down_at, down_at + hidden_width),
        ),
        [(tall, f32), (tall, bf16)]
        + [((seq_len, hidden_width), bf16)] * 2
        + [((seq_len, 2 * hidden_width), bf16)] * 2
        + [(tall, bf16)],
        (pltpu.VMEM(tall, f32),),
    )

    ffn_grad = weight_grads(
        (
            (normed_three, swap_halves(normed_three), grad_pre_own, swap_halves(grad_pre_other)),
            (cot_own, cot_other, hidden_own, swap_halves(hidden_other)),
        ),
        info,
        groups,
    )
    out_pieces = sequence_pieces(seq_output, groups, half_id)
    ffn_grad, grad_pre_own, grad_pre_other, out_pieces = pin(
        ffn_grad, grad_pre_own, grad_pre_other, out_pieces
    )
    ffn_far = scatter_far(ffn_grad, groups)
    sum_scratch = [pltpu.VMEM((seq_len, lanes), f32)] * 2
    grad_after_cross, cross_branch, grad_crossed_own, grad_crossed_other, gains_three = stream(
        ffn_back_kernel,
        info,
        (
            grad_pre_own,
            (three_own, gate_at, down_at),
            grad_pre_other,
            (three_other, gate_at, down_at),
            after_cross,
            rows,
            cot_own,
            (three_own, 0, width),
            (three_other, 0, width),
        ),
        [(tall, f32), (tall, bf16)]
        + [((seq_len, width), bf16)] * 2
        + [((8, model_width), f32)],
    )
    ffn_far, grad_crossed_own, grad_crossed_other, out_pieces = pin(
        ffn_far, grad_crossed_own, grad_crossed_other, out_pieces
    )
    ffn_sums = near_sums(ffn_grad, ffn_far, groups)
    out_pieces = exchange(out_pieces)
    ffn_sums, grad_crossed_own, grad_crossed_other = pin(
        ffn_sums, grad_crossed_own, grad_crossed_other
    )
    ffn_near = scatter_near(ffn_sums, groups)
    grad_q_own, grad_q_other, grad_kv_own, grad_kv_other = call(
        functools.partial(cross_back_kernel, width),
        info,
        (q_own, kv_own, grad_crossed_own, q_other, kv_other, grad_crossed_other),
        [((seq_len, width), bf16)] * 2 + [((seq_len, 2 * width), bf16)] * 2,
        sum_scratch,
    )
    out_pieces, grad_q_own, grad_q_other = pin(out_pieces, grad_q_own, grad_q_other)
    out_mixed = ordered_pieces(out_pieces, source_of, groups)
    out_pair = collect_pieces(out_mixed)
    (
        grad_after_self,
        self_branch,
        grad_att_own,
        grad_att_other,
        grad_memory,
        gains_two,
    ) = call(
        between_kernel,
        info,
        (
            grad_q_own,
            (two_own, width, 2 * width),
            grad_q_other,
            (two_other, width, 2 * width),
            after_self,
            rows,
            grad_after_cross,
            (two_own, 0, width),
            (two_other, 0, width),
            grad_kv_own,
            (two_own, 2 * width, 4 * width),
            grad_kv_other,
            (two_other, 2 * width, 4 * width),
        ),
        [(tall, f32), (tall, bf16)]
        + [((seq_len, width), bf16)] * 2
        + [(tall, f32), ((8, model_width), f32)],
    )
    cross_grad = weight_grads(
        (
            (normed_two, swap_halves(normed_two), grad_q_own, swap_halves(grad_q_other)),
            (own_memory, other_memory, grad_kv_own, swap_halves(grad_kv_other)),
            (cross_branch, swap_halves(cross_branch), crossed_own, swap_halves(crossed_other)),
            (self_branch, swap_halves(self_branch), attended_own, swap_halves(attended_other)),
        ),
        info,
        groups,
    )
    ffn_near, cross_grad, grad_att_own, grad_att_other, out_pair = pin(
        ffn_near, cross_grad, grad_att_own, grad_att_other, out_pair
    )
    cut = 3 * hidden_width // 2
    ffn_planes = plane_sums(ffn_grad, ffn_near, groups, 0, cut)
    more_planes = plane_sums(ffn_grad, ffn_near, groups, cut, 2 * cut)
    ffn_planes, more_planes, grad_att_own, grad_att_other = pin(
        ffn_planes, more_planes, grad_att_own, grad_att_other
    )
    cross_far = scatter_far(cross_grad, groups)
    ffn_high = scatter_planes(ffn_planes, groups)
    grad_qkv_own, grad_qkv_other, distance_sums = call(
        functools.partial(self_back_kernel, width),
        info,
        (
            window,
            qkv_own,
            grad_att_own,
            qkv_other,
            grad_att_other,
        ),
        [((seq_len, 3 * width), bf16)] * 2 + [(window.shape, f32)],
        sum_scratch,
    )
    cross_far, ffn_high, more_planes, grad_qkv_own, grad_qkv_other, grad_memory = pin(
        cross_far, ffn_high, more_planes, grad_qkv_own, grad_qkv_other, grad_memory
    )
    more_high = scatter_planes(more_planes, groups)
    cross_sums = near_sums(cross_grad, cross_far, groups)
    cross_sums, grad_qkv_own, grad_qkv_other = pin(cross_sums, grad_qkv_own, grad_qkv_other)
    cross_near = scatter_near(cross_sums, groups)
    grad_start, small = call(
        functools.partial(start_kernel, width, modes),
        info,
        (
            grad_qkv_own,
            (one_own, 0, 3 * width),
            grad_qkv_other,
            (one_other, 0, 3 * width),
            start_state,
            rows,
            grad_after_self,
            distance_sums,
            wide_hot,
            gains_two,
            gains_three,
        ),
        [(tall, f32), ((24, model_width), f32)],
    )
    small_other = swap_halves(small)
    qkv_grad = weight_grads(
        ((normed_one, swap_halves(normed_one), grad_qkv_own, swap_halves(grad_qkv_other)),),
        info,
        groups,
        (small, small_other),
    )
    qkv_grad, more_high, cross_near, grad_start, grad_memory = pin(
        qkv_grad, more_high, cross_near, grad_start, grad_memory
    )
    qkv_far = scatter_far(qkv_grad, groups)
    cross_planes = plane_sums(cross_grad, cross_near, groups, 0, 5 * width)
    cross_high = scatter_planes(cross_planes, groups)
    out_mine = lax.dynamic_index_in_dim(out_pair, half_id, 0, keepdims=False)
    out_sent = lax.dynamic_index_in_dim(out_pair, 1 - half_id, 0, keepdims=False)
    out_other, memory_other = swap_halves(out_sent), swap_halves(grad_memory)
    qkv_far, out_other, memory_other, grad_start = pin(qkv_far, out_other, memory_other, grad_start)
    qkv_sums = near_sums(qkv_grad, qkv_far, groups)
    qkv_sums, grad_start = pin(qkv_sums, grad_start)
    qkv_near = scatter_near(qkv_sums, groups)
    start_other = swap_halves(grad_start)
    qkv_near, start_other, memory_other, out_mine, out_other, ffn_high, more_high = pin(
        qkv_near, start_other, memory_other, out_mine, out_other, ffn_high, more_high
    )
    layer_output = join_columns(out_mine, out_other, half_id)
    tokens_grad = both_sequences(grad_start, start_other, half_id)
    memory_grad = both_sequences(grad_memory, memory_other, half_id)
    ffn_mine = jnp.concatenate(
        [jnp.sum(part.astype(f32), axis=0) for part in (ffn_high, more_high)], axis=1
    )
    self_mine = scatter_sum(
        scatter_high(high_sums(qkv_grad, qkv_near, groups, group_id), groups)
    )
    cross_mine = jnp.sum(cross_high.astype(f32), axis=0)
    small_mine = self_mine[:, 3 * width :]
    mine = small_mine[:, :8].T
    if shard_width >= bucket_count:
        table_total = small_mine[:bucket_count, 8:24]
    else:
        table_total = lax.psum(small[8:24, :bucket_count] + small_other[8:24, :bucket_count], dp_axes).T
    table_mine = lax.dynamic_slice_in_dim(table_total, half_id * heads_here, heads_here, 1)
    return (
        layer_output,
        tokens_grad,
        memory_grad,
        mine[3 : 3 + modes],
        mine[0],
        mine[1],
        mine[2],
        table_mine,
        self_mine[:, :width],
        self_mine[:, width : 2 * width],
        self_mine[:, 2 * width : 3 * width],
        cross_mine[:, 4 * width :].T,
        cross_mine[:, :width],
        cross_mine[:, width : 2 * width],
        cross_mine[:, 2 * width : 3 * width],
        cross_mine[:, 3 * width : 4 * width].T,
        ffn_mine[:, :hidden_width],
        ffn_mine[:, hidden_width : 2 * hidden_width],
        ffn_mine[:, 2 * hidden_width :].T,
    )


def solution(mesh):
    groups, halves = mesh.shape["dp"], mesh.shape["heads"]
    low = 4 if groups % 4 == 0 else 1
    mesh = Mesh(mesh.devices.reshape(groups // low, low, halves), dp_axes + ("heads",))
    rows_dp = P(dp_axes, None)
    columns = P(dp_axes, "heads")
    rows_heads = P("heads", dp_axes)
    in_specs = (
        (rows_dp, rows_dp, P(dp_axes + ("heads",), None))
        + (P(),) * 5
        + (P(None, dp_axes), P(dp_axes), P(dp_axes), P(dp_axes), P(None, "heads"))
        + (columns, columns, columns, rows_heads) * 2
        + (columns, columns, rows_heads)
    )
    out_specs = (
        (P(dp_axes + ("heads",), None), rows_dp, rows_dp)
        + (P(None, dp_axes), P(dp_axes), P(dp_axes), P(dp_axes), P(None, "heads"))
        + (columns, columns, columns, rows_heads) * 2
        + (columns, columns, rows_heads)
    )
    return jax.shard_map(body, mesh=mesh, in_specs=in_specs, out_specs=out_specs, check_vma=False)
```
